128 devices in a mesh: photo: 8 (over y, x_lo), tile: 16 (over x_hi, z, core).
Axes of the slice: x: 4 (x_hi: 2, x_lo: 2; x = x_hi * 2 + x_lo), y: 4, z: 4, core: 2. Of those that a mesh axis runs over, the one named last changes fastest.
Arguments:
- photos: bfloat16 [128, 256, 4096], P('photo', 'tile'), may hold values from 0.25 to 64, as said below
- camera_id: int32 [128], P('photo'), may hold values from 0 to 31, never falling along the last dimension, each value on 1 to 8 neighbouring positions
Outputs:
- fingerprints: float32 [32, 256, 4096], P(None, 'tile', 'photo')
- correlation: float32 [32, 32], replicated
The draws below stay inside these ranges and needn't reach their ends.
Inputs may be any that keep to these rules, and one draw needn't show every extreme that they name: `photos`: values are positive intensities. `camera_id`: photos are ordered by camera: ids never fall, every camera has 1 to 8 photos, and one has exactly 8.
All inputs are finite; a program needn't handle non-finite values.
Results may differ from the reference program's by a relative error of at most 0.0026.
Values may be sent and summed in bfloat16 or wider, within the bound.
A program may use at most 192 MiB of HBM per device.

```python
import math
import jax
import jax.numpy as jnp
import numpy as np
from jax import lax

W = 4096
CAMS = 32
H = 256
PHOTOS = 128
MOST_PHOTOS = 8


def draw_photos(key, part):
    keys = jax.random.split(key, 4)
    positions = jnp.arange(H, dtype=jnp.float32) / float(max(H - 1, 1))
    ramp = jnp.exp(jnp.log(1.5) * positions)[None, :, None]
    row_texture = jnp.exp(jax.random.uniform(keys[0], (PHOTOS, H, 1), jnp.float32) * jnp.log(4.0))
    col_texture = jnp.exp(jax.random.uniform(keys[1], (PHOTOS, 1, W), jnp.float32) * jnp.log(4.0))
    shared = jax.random.uniform(keys[2], (1, H, W), jnp.float32, 0.5, 1.5)
    own_part = jax.random.uniform(keys[3], (PHOTOS, H, W), jnp.float32)
    content = shared + own_part
    values = ramp * row_texture * col_texture * content
    return values.astype(jnp.bfloat16)


def split_up(number_of, total, limit, lean):
    loads = [(1 << 20) // math.isqrt(grade ** lean) + 1 for grade in range(2, number_of + 1)]
    surplus, holding = total - limit - (number_of - 1), [1] * (number_of - 1)
    while surplus > 0:
        free = [i for i in range(number_of - 1) if holding[i] < limit]
        mass, left = sum([loads[i] for i in free]), surplus
        for i in free:
            addition = min(limit - holding[i], max(1, left * loads[i] // mass), surplus)
            holding[i] = holding[i] + addition
            surplus = surplus - addition
    return np.array([limit] + holding)


def uneven_parts(own_key, amount, total, most, slope):
    if amount == 2:
        one = jax.random.randint(own_key, (), max(1, total - most), min(most, total - 1) + 1)
        return jnp.stack([one, total - one])
    sizes = jnp.asarray(split_up(amount, total, most, slope), jnp.int32)
    couples = (amount - 1) // 2
    donor, taker = sizes[1:1 + 2 * couples:2], sizes[2:2 + 2 * couples:2]
    room = jnp.minimum(donor - 1, most - taker)
    moved = jax.random.randint(jax.random.fold_in(own_key, 1), (couples,), 0, 1 << 20) % (room + 1)
    sizes = sizes.at[1:1 + 2 * couples:2].set(donor - moved).at[2:2 + 2 * couples:2].set(taker + moved)
    return sizes[jax.random.permutation(jax.random.fold_in(own_key, 2), amount)]


def setup_inputs(seed: int = 0) -> dict:
    streams_of = jax.random.split(jax.random.key(seed), 3)
    return {
        "photos": draw_photos(jax.random.fold_in(streams_of[2], 71), 0),
        "camera_id": jnp.searchsorted(jnp.cumsum(uneven_parts(streams_of[1], CAMS, PHOTOS, MOST_PHOTOS, 2)), jnp.arange(PHOTOS), side="right").astype(jnp.int32),
    }


noise_power = 1.0
var_eps = 1e-06

def forward_haar(field):
    top_left = field[..., 0::2, 0::2]
    top_right = field[..., 0::2, 1::2]
    low_left = field[..., 1::2, 0::2]
    low_right = field[..., 1::2, 1::2]
    horiz = (top_left + top_right - low_left - low_right) * 0.5
    vertic = (top_left - top_right + low_left - low_right) * 0.5
    diagon = (top_left - top_right - low_left + low_right) * 0.5
    return jnp.stack([horiz, vertic, diagon])

def inverse_haar(bands):
    horiz, vertic, diagon = (bands[0], bands[1], bands[2])
    top_left = (horiz + vertic + diagon) * 0.5
    top_right = (horiz - vertic - diagon) * 0.5
    low_left = (vertic - horiz - diagon) * 0.5
    low_right = (diagon - horiz - vertic) * 0.5
    upper = jnp.stack([top_left, top_right], -1).reshape(top_left.shape[:-1] + (-1,))
    lower = jnp.stack([low_left, low_right], -1).reshape(low_left.shape[:-1] + (-1,))
    joined = jnp.stack([upper, lower], -2)
    return joined.reshape(upper.shape[:-2] + (-1, upper.shape[-1]))

def local_variance(padded, rows, cols):
    squares = padded * padded
    column_box = squares[..., :, 4:4 + cols]
    lowest = None
    for radius in range(1, 5):
        column_box = column_box + squares[..., :, 4 - radius:4 - radius + cols] + squares[..., :, 4 + radius:4 + radius + cols]
        row_box = column_box[..., 4:4 + rows, :]
        for offset in range(1, radius + 1):
            row_box = row_box + column_box[..., 4 - offset:4 - offset + rows, :] + column_box[..., 4 + offset:4 + offset + rows, :]
        mean_square = row_box / float((2 * radius + 1) ** 2)
        lowest = mean_square if lowest is None else jnp.minimum(lowest, mean_square)
    return lowest

def residual_of(image):
    field = image.astype(jnp.float32)
    bands = forward_haar(field)
    half_rows, half_cols = (bands.shape[1], bands.shape[2])
    padded = jnp.pad(bands, ((0, 0), (4, 4), (4, 4)))
    variance = local_variance(padded, half_rows, half_cols)
    gain = noise_power / jnp.maximum(variance, noise_power)
    return inverse_haar(bands * gain).astype(jnp.bfloat16)

def correlate(gram, totals, pixel_count):
    average = totals / pixel_count
    covar = gram / pixel_count - average[:, None] * average[None, :]
    spread = jnp.diagonal(covar) + var_eps
    return covar / jnp.sqrt(spread[:, None] * spread[None, :])

def reference(photos, camera_id):
    rows_all, width_all = (photos.shape[1], photos.shape[2])

    def accumulate(carry, item):
        weighted, energy = carry
        image, camera = item
        noise_map = residual_of(image)
        field = image.astype(jnp.float32)
        weighted = weighted.at[camera].add(noise_map.astype(jnp.float32) * field)
        energy = energy.at[camera].add(field * field)
        return ((weighted, energy), None)
    empty = jnp.zeros((CAMS, rows_all, width_all), jnp.float32)
    (weighted, energy), unused = lax.scan(accumulate, (empty, empty), (photos, camera_id))
    fingerprints = weighted / energy
    flat = fingerprints.reshape(CAMS, -1)
    gram = jnp.dot(flat, flat.T, precision=lax.Precision.HIGHEST, preferred_element_type=jnp.float32)
    totals = lax.optimization_barrier(jnp.sum(flat, axis=1))
    correlation = correlate(gram, totals, float(rows_all * width_all))
    return (fingerprints, correlation)
```

```python
import functools

import jax
import jax.numpy as jnp
import numpy as np
from jax import lax
from jax.experimental import pallas as pl
from jax.experimental.pallas import tpu as pltpu
from jax.sharding import PartitionSpec as P

MESH = pl.DeviceIdType.MESH
F32 = jnp.float32
BF16 = jnp.bfloat16

CAMS = 32
NOISE_POWER = 1.0
VAR_EPS = 1e-06

PH = 8
TI = 16
OWN = 16
HR = 8
LANES = 1152
VMEM_LIMIT = 60 * 1024 * 1024


def constants():
    perm = np.zeros((256, 256), np.float32)
    for tb in range(2):
        for i in range(HR):
            for p in range(OWN):
                perm[(tb * HR + i) * OWN + p, p * 16 + 2 * i + tb] = 1.0
    edge = np.zeros((2, 2, 256, 128), np.float32)
    for tb in range(2):
        for k in range(8):
            edge[tb, 0, 248 + k, 16 * tb + k] = 1.0
            edge[tb, 1, k, 16 * tb + 8 + k] = 1.0
    sign = np.array([[1, 1, 1], [1, -1, -1], [-1, 1, -1], [-1, -1, 1]], np.float32) * 0.5
    haar = np.zeros((512, 384), np.float32)
    for j in range(128):
        for b in range(3):
            haar[2 * j, 128 * b + j] = sign[0, b]
            haar[2 * j + 1, 128 * b + j] = sign[1, b]
            haar[256 + 2 * j, 128 * b + j] = sign[2, b]
            haar[256 + 2 * j + 1, 128 * b + j] = sign[3, b]
    haar_edge = np.zeros((128, 128), np.float32)
    for k in range(8):
        for b in range(3):
            haar_edge[2 * k, 8 * b + k] = sign[0, b]
            haar_edge[2 * k + 1, 8 * b + k] = sign[1, b]
            haar_edge[16 + 2 * k, 8 * b + k] = sign[2, b]
            haar_edge[16 + 2 * k + 1, 8 * b + k] = sign[3, b]
    split = np.zeros((256, 256), np.float32)
    for j in range(128):
        split[2 * j, j] = 1.0
        split[2 * j + 1, 128 + j] = 1.0
    out = np.arange(256)
    box = np.zeros((4, 3, 768, 256), np.float32)
    for r in range(1, 5):
        inner = (np.abs(out[:, None] - out[None, :]) <= r).astype(np.float32)
        for b in range(3):
            side = np.zeros((128, 256), np.float32)
            for k in range(8):
                cell = k - 4 if k < 4 else 252 + k
                side[8 * b + k] = np.abs(cell - out) <= r
            box[r - 1, b] = np.concatenate([inner, inner, side, side])
    return [jnp.asarray(c, BF16) for c in (perm, edge, haar, haar_edge, split, box)]


def dot(a, b):
    return jnp.dot(a, b, preferred_element_type=F32)


def hi_lo(x):
    hi = x.astype(BF16)
    lo = (x - hi.astype(F32)).astype(BF16)
    return hi, lo


def pack_kernel(x_ref, perm_ref, edge_ref, out_ref, y_ref):
    perm = perm_ref[...]
    for c in range(16):
        x = x_ref[:, :, 256 * c : 256 * c + 256].reshape(256, 256)
        y = dot(perm, x).astype(BF16)
        y_ref[c] = y
        d, ct = divmod(c, 2)
        for tb in range(2):
            lane = ct * 512 + tb * 256
            out_ref[d, :, :, lane : lane + 256] = y[tb * 128 : tb * 128 + 128].reshape(HR, OWN, 256)
    for d in range(PH):
        side = jnp.zeros((128, 128), F32)
        for tb in range(2):
            if d > 0:
                side += dot(y_ref[2 * d - 1, pl.ds(tb * 128, 128), :], edge_ref[tb, 0])
            if d < PH - 1:
                side += dot(y_ref[2 * d + 2, pl.ds(tb * 128, 128), :], edge_ref[tb, 1])
        out_ref[d, :, :, 1024:1152] = side.astype(BF16).reshape(HR, OWN, 128)


def packed(photos, perm, edge):
    return pl.pallas_call(
        pack_kernel,
        out_shape=jax.ShapeDtypeStruct((PH, HR, OWN, LANES), BF16),
        in_specs=[pl.BlockSpec(memory_space=pltpu.VMEM)] * 3,
        out_specs=pl.BlockSpec(memory_space=pltpu.VMEM),
        scratch_shapes=[pltpu.VMEM((16, 256, 256), BF16)],
        compiler_params=pltpu.CompilerParams(vmem_limit_bytes=VMEM_LIMIT),
        name="pack",
    )(photos, perm, edge)


def exchange_kernel(
    ext_ref, idr_ref, main_ref, top_ref, bot_ref, ids_ref,
    own_sem, send_sem, recv_sem, isend_sem, irecv_sem, up_send, up_recv, dn_send, dn_recv,
):
    me = lax.axis_index("photo")
    t = lax.axis_index("tile")

    barrier = pltpu.get_barrier_semaphore()
    for k in range(1, PH):
        peer = lax.rem(me + k, PH)
        pl.semaphore_signal(barrier, inc=1, device_id={"photo": peer}, device_id_type=MESH)

    for k in (1, TI - 1):
        pl.semaphore_signal(
            barrier, inc=1, device_id={"tile": lax.rem(t + k, TI)}, device_id_type=MESH
        )
    pl.semaphore_wait(barrier, PH + 1)

    def a2a(k):
        peer = lax.rem(me + k, PH)
        return pltpu.make_async_remote_copy(
            src_ref=ext_ref.at[peer], dst_ref=main_ref.at[me],
            send_sem=send_sem.at[k - 1], recv_sem=recv_sem.at[k - 1],
            device_id={"photo": peer}, device_id_type=MESH,
        )

    def idc(k):
        peer = lax.rem(me + k, PH)
        return pltpu.make_async_remote_copy(
            src_ref=idr_ref, dst_ref=ids_ref.at[me],
            send_sem=isend_sem.at[k - 1], recv_sem=irecv_sem.at[k - 1],
            device_id={"photo": peer}, device_id_type=MESH,
        )

    def up(k, src, s):
        return pltpu.make_async_remote_copy(
            src_ref=src.at[s, pl.ds(0, 4)], dst_ref=bot_ref.at[s],
            send_sem=up_send.at[k], recv_sem=up_recv.at[k],
            device_id={"tile": t - 1}, device_id_type=MESH,
        )

    def down(k, src, s):
        return pltpu.make_async_remote_copy(
            src_ref=src.at[s, pl.ds(4, 4)], dst_ref=top_ref.at[s],
            send_sem=dn_send.at[k], recv_sem=dn_recv.at[k],
            device_id={"tile": t + 1}, device_id_type=MESH,
        )

    def pass_on(k, src, s):
        @pl.when(t > 0)
        def _():
            up(k, src, s).start()

        @pl.when(t < TI - 1)
        def _():
            down(k, src, s).start()

    for k in range(1, PH):
        a2a(k).start()
    for k in range(1, PH):
        idc(k).start()
    pass_on(0, ext_ref, me)
    own = pltpu.make_async_copy(ext_ref.at[me], main_ref.at[me], own_sem.at[0])
    own.start()
    own_id = pltpu.make_async_copy(idr_ref, ids_ref.at[me], own_sem.at[1])
    own_id.start()

    @pl.when(t == 0)
    def _():
        top_ref[...] = jnp.zeros(top_ref.shape, BF16)

    @pl.when(t == TI - 1)
    def _():
        bot_ref[...] = jnp.zeros(bot_ref.shape, BF16)

    for k in range(1, PH):
        s = lax.rem(me + PH - k, PH)
        a2a(k).wait_recv()
        pass_on(k, main_ref, s)
    for k in range(1, PH):
        a2a(k).wait_send()
        idc(k).wait()
    own.wait()
    own_id.wait()

    @pl.when(t > 0)
    def _():
        for k in range(PH):
            s = lax.rem(me + PH - k, PH)
            up(k, main_ref, s).wait_send()
            down(k, main_ref, s).wait_recv()

    @pl.when(t < TI - 1)
    def _():
        for k in range(PH):
            s = lax.rem(me + PH - k, PH)
            down(k, main_ref, s).wait_send()
            up(k, main_ref, s).wait_recv()


def exchanged(ext, idr):
    vm = pl.BlockSpec(memory_space=pltpu.VMEM)
    dma = pltpu.SemaphoreType.DMA
    return pl.pallas_call(
        exchange_kernel,
        out_shape=(
            jax.ShapeDtypeStruct((PH, HR, OWN, LANES), BF16),
            jax.ShapeDtypeStruct((PH, 4, OWN, LANES), BF16),
            jax.ShapeDtypeStruct((PH, 4, OWN, LANES), BF16),
            jax.ShapeDtypeStruct((PH, 8, 128), jnp.int32),
        ),
        in_specs=[vm] * 2,
        out_specs=(vm,) * 4,
        scratch_shapes=[
            dma((2,)), dma((PH - 1,)), dma((PH - 1,)), dma((PH - 1,)), dma((PH - 1,)),
            dma((PH,)), dma((PH,)), dma((PH,)), dma((PH,)),
        ],
        compiler_params=pltpu.CompilerParams(
            collective_id=0, has_side_effects=True, vmem_limit_bytes=VMEM_LIMIT
        ),
        name="exchange",
    )(ext, idr)


def bands_of(x, rows, sq_ref, eq_ref, band_ref, s2, first, haar, haar_edge):
    m = rows * OWN
    for ct in range(2):
        got = dot(x[:, :, 512 * ct : 512 * ct + 512].reshape(m, 512), haar)
        for b in range(3):
            one = got[:, 128 * b : 128 * b + 128].reshape(rows, OWN, 128)
            if band_ref is not None:
                band_ref[b, s2, :, :, 128 * ct : 128 * ct + 128] = one
            sq_ref[b, s2, first : first + rows, :, 128 * ct : 128 * ct + 128] = one * one
    edge = dot(x[:, :, 1024:1152].reshape(m, 128), haar_edge).reshape(rows, OWN, 128)
    eq_ref[s2, first : first + rows] = edge * edge


def chunk(k, main_ref, top_ref, bot_ref, ids_ref, consts, scratch):
    haar_ref, haar_edge_ref, split_ref, box_ref = consts
    sq_ref, eq_ref, band_ref, lhs_ref, sum_ref, px_ref, data_ref, acc_ref = scratch
    haar, haar_edge = haar_ref[...], haar_edge_ref[...]
    for s2 in range(2):
        s = 2 * k + s2
        bands_of(top_ref[s], 4, sq_ref, eq_ref, None, s2, 0, haar, haar_edge)
        bands_of(main_ref[s], HR, sq_ref, eq_ref, band_ref, s2, 4, haar, haar_edge)
        bands_of(bot_ref[s], 4, sq_ref, eq_ref, None, s2, 12, haar, haar_edge)
        for ct in range(2):
            for tb in range(2):
                lane = 512 * ct + 256 * tb
                x = main_ref[s, :, :, lane : lane + 256].reshape(HR * OWN, 256)
                got = dot(x, split_ref[...])
                for odd in range(2):
                    px_ref[2 * tb + odd, s2, :, :, 128 * ct : 128 * ct + 128] = got[
                        :, 128 * odd : 128 * odd + 128
                    ].reshape(HR, OWN, 128)

    def sums(n, _):
        s2, i = n // HR, lax.rem(n, HR)
        row = eq_ref[s2, i + 4]
        for r in range(1, 5):
            row = row + eq_ref[s2, i + 4 - r] + eq_ref[s2, i + 4 + r]
            hi, lo = hi_lo(row)
            for b in range(3):
                lhs_ref[r - 1, b, n, :, 512:640] = hi
                lhs_ref[r - 1, b, n, :, 640:768] = lo
        for b in range(3):
            row = sq_ref[b, s2, i + 4]
            for r in range(1, 5):
                row = row + sq_ref[b, s2, i + 4 - r] + sq_ref[b, s2, i + 4 + r]
                hi, lo = hi_lo(row)
                lhs_ref[r - 1, b, n, :, 0:256] = hi
                lhs_ref[r - 1, b, n, :, 256:512] = lo
        return 0

    lax.fori_loop(0, 2 * HR, sums, 0)

    for r in range(4):
        for b in range(3):
            got = dot(lhs_ref[r, b].reshape(256, 768), box_ref[r, b])
            sum_ref[r, b] = got.reshape(2 * HR, OWN, 256)

    def residual(n, _):
        s2, i = n // HR, lax.rem(n, HR)
        res = []
        for b in range(3):
            var = sum_ref[0, b, n] * (1.0 / 9.0)
            for r in range(1, 4):
                var = jnp.minimum(var, sum_ref[r, b, n] * (1.0 / (2 * r + 3) ** 2))
            gain = NOISE_POWER / jnp.maximum(var, NOISE_POWER)
            res.append(band_ref[b, s2, i] * gain * 0.5)
        hz, vt, dg = res
        plus, minus = hz + vt, hz - vt
        noise = (plus + dg, minus - dg, -minus - dg, dg - plus)
        at = pl.multiple_of(n * OWN, OWN)
        for j in range(4):
            x = px_ref[j, s2, i]
            for part, value in enumerate((noise[j].astype(BF16).astype(F32) * x, x * x)):
                hi, lo = hi_lo(value)
                data_ref[2 * j + part, pl.ds(at, OWN), :] = hi
                data_ref[2 * j + part, pl.ds(256 + at, OWN), :] = lo
        return 0

    lax.fori_loop(0, 2 * HR, residual, 0)

    ids = jnp.concatenate([ids_ref[2 * k, 0:1, :], ids_ref[2 * k + 1, 0:1, :]], axis=1)
    row = lax.broadcasted_iota(jnp.int32, (256, 256), 0)
    col = lax.broadcasted_iota(jnp.int32, (256, 256), 1)
    same = (row // HR == ids) & (lax.rem(row, HR) == lax.rem(col // OWN, HR))
    pick = jnp.where(same, 1.0, 0.0).astype(BF16)
    pick = jnp.concatenate([pick, pick], axis=1)
    for j in range(8):
        acc_ref[j] += dot(pick, data_ref[j])


def three(x):
    hi = x.astype(BF16)
    rest = x - hi.astype(F32)
    mid = rest.astype(BF16)
    low = (rest - mid.astype(F32)).astype(BF16)
    return jnp.concatenate([hi, mid, low], axis=1)


def finish(acc_ref, join_ref, rows_ref, fp_ref):
    for tb in range(2):
        for ct in range(2):
            pair = []
            for odd in range(2):
                j = 2 * tb + odd
                lanes = pl.ds(128 * ct, 128)
                pair.append(acc_ref[2 * j, :, lanes] / acc_ref[2 * j + 1, :, lanes])
            got = dot(three(jnp.concatenate(pair, axis=1)), join_ref[...])
            for part in range(2):
                one = got[:, 128 * part : 128 * part + 128].reshape(CAMS, HR, 128)
                rows_ref[2 * ct + part, :, pl.ds(tb, HR, stride=2), :] = one
    for part in range(4):
        fp_ref[:, :, 128 * part : 128 * part + 128] = rows_ref[part]


def compute_kernel(
    main_ref, top_ref, bot_ref, ids_ref, haar_ref, haar_edge_ref, split_ref, join_ref, box_ref,
    fp_ref, *scratch,
):
    *scratch, rows_ref = scratch
    acc_ref = scratch[-1]
    acc_ref[...] = jnp.zeros(acc_ref.shape, F32)
    consts = (haar_ref, haar_edge_ref, split_ref, box_ref)

    def step(k, _):
        chunk(k, main_ref, top_ref, bot_ref, ids_ref, consts, scratch)
        return 0

    lax.fori_loop(0, PH // 2, step, 0)
    finish(acc_ref, join_ref, rows_ref, fp_ref)


SCRATCH = [
    ((3, 2, 16, OWN, 256), F32),
    ((2, 16, OWN, 128), F32),
    ((3, 2, HR, OWN, 256), F32),
    ((4, 3, 2 * HR, OWN, 768), BF16),
    ((4, 3, 2 * HR, OWN, 256), F32),
    ((4, 2, HR, OWN, 256), F32),
    ((8, 512, 256), BF16),
    ((8, 256, 256), F32),
    ((4, CAMS, 16, 128), F32),
]


def computed(main, top, bot, ids, haar, haar_edge, split, join, box):
    vm = pl.BlockSpec(memory_space=pltpu.VMEM)
    return pl.pallas_call(
        compute_kernel,
        out_shape=jax.ShapeDtypeStruct((CAMS, 16, 512), F32),
        in_specs=[vm] * 9,
        out_specs=vm,
        scratch_shapes=[pltpu.VMEM(s, d) for s, d in SCRATCH],
        compiler_params=pltpu.CompilerParams(vmem_limit_bytes=VMEM_LIMIT),
        name="residuals",
    )(main, top, bot, ids, haar, haar_edge, split, join, box)


def allsum_kernel(x_ref, o_ref, a_ref, m_ref, b_ref, own_sem, as_sem, ar_sem, bs_sem, br_sem):
    me = lax.axis_index("photo")
    t = lax.axis_index("tile")
    barrier = pltpu.get_barrier_semaphore()
    for k in range(1, PH):
        pl.semaphore_signal(
            barrier, inc=1, device_id={"photo": lax.rem(me + k, PH)}, device_id_type=MESH
        )
    for k in range(1, TI):
        pl.semaphore_signal(
            barrier, inc=1, device_id={"tile": lax.rem(t + k, TI)}, device_id_type=MESH
        )
    pl.semaphore_wait(barrier, PH + TI - 2)

    def first(k):
        return pltpu.make_async_remote_copy(
            src_ref=x_ref, dst_ref=a_ref.at[k - 1], send_sem=as_sem.at[k - 1],
            recv_sem=ar_sem.at[k - 1],
            device_id={"photo": lax.rem(me + k, PH)}, device_id_type=MESH,
        )

    def second(k):
        return pltpu.make_async_remote_copy(
            src_ref=m_ref, dst_ref=b_ref.at[k - 1], send_sem=bs_sem.at[k - 1],
            recv_sem=br_sem.at[k - 1],
            device_id={"tile": lax.rem(t + k, TI)}, device_id_type=MESH,
        )

    for k in range(1, PH):
        first(k).start()
    for k in range(1, PH):
        first(k).wait_recv()
    total = jnp.zeros(x_ref.shape, F32)
    for s in range(PH):
        k = lax.rem(me + PH - s, PH)
        other = a_ref[jnp.maximum(k - 1, 0)]
        total += jnp.where(k == 0, x_ref[...], other)
    m_ref[...] = total
    for k in range(1, TI):
        second(k).start()
    for k in range(1, TI):
        second(k).wait_recv()
    total = jnp.zeros(x_ref.shape, F32)
    for s in range(TI):
        k = lax.rem(t + TI - s, TI)
        other = b_ref[jnp.maximum(k - 1, 0)]
        total += jnp.where(k == 0, m_ref[...], other)
    o_ref[...] = total
    for k in range(1, PH):
        first(k).wait_send()
    for k in range(1, TI):
        second(k).wait_send()


def allsum(x):
    vm = pl.BlockSpec(memory_space=pltpu.VMEM)
    dma = pltpu.SemaphoreType.DMA
    return pl.pallas_call(
        allsum_kernel,
        out_shape=jax.ShapeDtypeStruct(x.shape, F32),
        in_specs=[vm],
        out_specs=vm,
        scratch_shapes=[
            pltpu.VMEM((PH - 1,) + x.shape, F32),
            pltpu.VMEM(x.shape, F32),
            pltpu.VMEM((TI - 1,) + x.shape, F32),
            dma((1,)), dma((PH - 1,)), dma((PH - 1,)), dma((TI - 1,)), dma((TI - 1,)),
        ],
        compiler_params=pltpu.CompilerParams(collective_id=1, has_side_effects=True),
        name="allsum",
    )(x)


def on_device(photos, camera_id):
    perm, edge, haar, haar_edge, split, box = constants()
    join = jnp.concatenate([split.T] * 3)
    ext = packed(photos, perm, edge)
    idr = jnp.broadcast_to(jnp.tile(camera_id, HR)[None, :], (8, 128))
    main, top, bot, ids = exchanged(ext, idr)
    fingerprints = computed(main, top, bot, ids, haar, haar_edge, split, join, box)
    flat = fingerprints.reshape(CAMS, -1)
    gram_local = jnp.dot(flat, flat.T, precision=lax.Precision.HIGHEST, preferred_element_type=F32)
    totals_local = jnp.sum(flat, axis=1)
    both = jnp.zeros((CAMS, 128), F32)
    both = both.at[:, :CAMS].set(gram_local).at[:, CAMS].set(totals_local)
    both = allsum(both)
    pixels = float(256 * 4096)
    average = both[:, CAMS] / pixels
    covar = both[:, :CAMS] / pixels - average[:, None] * average[None, :]
    spread = jnp.diagonal(covar) + VAR_EPS
    correlation = covar / jnp.sqrt(spread[:, None] * spread[None, :])
    return (fingerprints, correlation)


def solution(mesh):
    return jax.shard_map(
        on_device,
        mesh=mesh,
        in_specs=(P("photo", "tile", None), P("photo")),
        out_specs=(P(None, "tile", "photo"), P()),
        check_vma=False,
    )
```

```python
import functools

import jax
import jax.numpy as jnp
import numpy as np
from jax import lax
from jax.experimental import pallas as pl
from jax.experimental.pallas import tpu as pltpu
from jax.sharding import PartitionSpec as P

MESH = pl.DeviceIdType.MESH
F32 = jnp.float32
BF16 = jnp.bfloat16

CAMS = 32
NOISE_POWER = 1.0
VAR_EPS = 1e-06

PH = 8
TI = 16
OWN = 16
HR = 8
LANES = 1152
VMEM_LIMIT = 60 * 1024 * 1024


def constants():
    perm = np.zeros((256, 256), np.float32)
    for tb in range(2):
        for i in range(HR):
            for p in range(OWN):
                perm[(tb * HR + i) * OWN + p, p * 16 + 2 * i + tb] = 1.0
    edge = np.zeros((2, 2, 256, 128), np.float32)
    for tb in range(2):
        for k in range(8):
            edge[tb, 0, 248 + k, 16 * tb + k] = 1.0
            edge[tb, 1, k, 16 * tb + 8 + k] = 1.0
    sign = np.array([[1, 1, 1], [1, -1, -1], [-1, 1, -1], [-1, -1, 1]], np.float32) * 0.5
    haar = np.zeros((512, 384), np.float32)
    for j in range(128):
        for b in range(3):
            haar[2 * j, 128 * b + j] = sign[0, b]
            haar[2 * j + 1, 128 * b + j] = sign[1, b]
            haar[256 + 2 * j, 128 * b + j] = sign[2, b]
            haar[256 + 2 * j + 1, 128 * b + j] = sign[3, b]
    haar_edge = np.zeros((128, 128), np.float32)
    for k in range(8):
        for b in range(3):
            haar_edge[2 * k, 8 * b + k] = sign[0, b]
            haar_edge[2 * k + 1, 8 * b + k] = sign[1, b]
            haar_edge[16 + 2 * k, 8 * b + k] = sign[2, b]
            haar_edge[16 + 2 * k + 1, 8 * b + k] = sign[3, b]
    split = np.zeros((256, 256), np.float32)
    for j in range(128):
        split[2 * j, j] = 1.0
        split[2 * j + 1, 128 + j] = 1.0
    out = np.arange(256)
    box = np.zeros((4, 512, 256), np.float32)
    box_edge = np.zeros((4, 3, 256, 256), np.float32)
    for r in range(1, 5):
        inner = (np.abs(out[:, None] - out[None, :]) <= r).astype(np.float32)
        box[r - 1] = np.concatenate([inner, inner])
        for b in range(3):
            side = np.zeros((128, 256), np.float32)
            for k in range(8):
                cell = k - 4 if k < 4 else 252 + k
                side[8 * b + k] = np.abs(cell - out) <= r
            box_edge[r - 1, b] = np.concatenate([side, side])
    join = np.concatenate([split.T] * 3)
    fold = np.zeros((256, 128), np.float32)
    fold[np.arange(256), np.arange(256) // HR] = 1.0
    fold = np.concatenate([fold] * 3)
    every = (perm, edge, haar, haar_edge, split, join, fold, box, box_edge)
    return [jnp.asarray(c, BF16) for c in every]


def dot(a, b):
    return jnp.dot(a, b, preferred_element_type=F32)


def hi_lo(x):
    hi = x.astype(BF16)
    lo = (x - hi.astype(F32)).astype(BF16)
    return hi, lo


def pack_kernel(x_ref, perm_ref, edge_ref, out_ref, y_ref):
    perm = perm_ref[...]
    for c in range(16):
        x = x_ref[:, :, 256 * c : 256 * c + 256].reshape(256, 256)
        y = dot(perm, x).astype(BF16)
        y_ref[c] = y
        d, ct = divmod(c, 2)
        for tb in range(2):
            lane = ct * 512 + tb * 256
            out_ref[d, :, :, lane : lane + 256] = y[tb * 128 : tb * 128 + 128].reshape(HR, OWN, 256)
    for d in range(PH):
        side = jnp.zeros((128, 128), F32)
        for tb in range(2):
            if d > 0:
                side += dot(y_ref[2 * d - 1, pl.ds(tb * 128, 128), :], edge_ref[tb, 0])
            if d < PH - 1:
                side += dot(y_ref[2 * d + 2, pl.ds(tb * 128, 128), :], edge_ref[tb, 1])
        out_ref[d, :, :, 1024:1152] = side.astype(BF16).reshape(HR, OWN, 128)


def packed(photos, perm, edge):
    return pl.pallas_call(
        pack_kernel,
        out_shape=jax.ShapeDtypeStruct((PH, HR, OWN, LANES), BF16),
        in_specs=[pl.BlockSpec(memory_space=pltpu.VMEM)] * 3,
        out_specs=pl.BlockSpec(memory_space=pltpu.VMEM),
        scratch_shapes=[pltpu.VMEM((16, 256, 256), BF16)],
        compiler_params=pltpu.CompilerParams(vmem_limit_bytes=VMEM_LIMIT),
        name="pack",
    )(photos, perm, edge)


def chunk(s, x_ref, ids_ref, consts, scratch):
    haar_ref, haar_edge_ref, split_ref, _, _, box_ref, box_edge_ref = consts
    sq_ref, eq_ref, band_ref, lhs_ref, edge_ref, sum_ref, side_ref, px_ref, data_ref, acc_ref = scratch

    rows = 2 * HR
    for ct in range(2):
        x = x_ref[s, :, :, 512 * ct : 512 * ct + 512].reshape(rows * OWN, 512)
        got = dot(x, haar_ref[...])
        for b in range(3):
            one = got[:, 128 * b : 128 * b + 128].reshape(rows, OWN, 128)
            band_ref[b, :, :, 128 * ct : 128 * ct + 128] = one[4 : 4 + HR]
            sq_ref[b, :, :, 128 * ct : 128 * ct + 128] = one * one
        for tb in range(2):
            lane = 512 * ct + 256 * tb
            x = x_ref[s, pl.ds(4, HR), :, lane : lane + 256].reshape(HR * OWN, 256)
            got = dot(x, split_ref[...])
            for odd in range(2):
                px_ref[2 * tb + odd, :, :, 128 * ct : 128 * ct + 128] = got[
                    :, 128 * odd : 128 * odd + 128
                ].reshape(HR, OWN, 128)
    x = x_ref[s, :, :, 1024:1152].reshape(rows * OWN, 128)
    one = dot(x, haar_edge_ref[...]).reshape(rows, OWN, 128)
    eq_ref[...] = one * one

    def sums(i, _):
        row = eq_ref[i + 4]
        for r in range(1, 5):
            row = row + eq_ref[i + 4 - r] + eq_ref[i + 4 + r]
            hi, lo = hi_lo(row)
            edge_ref[r - 1, i, :, 0:128] = hi
            edge_ref[r - 1, i, :, 128:256] = lo
        for b in range(3):
            row = sq_ref[b, i + 4]
            for r in range(1, 5):
                row = row + sq_ref[b, i + 4 - r] + sq_ref[b, i + 4 + r]
                hi, lo = hi_lo(row)
                lhs_ref[r - 1, b, i, :, 0:256] = hi
                lhs_ref[r - 1, b, i, :, 256:512] = lo
        return 0

    lax.fori_loop(0, HR, sums, 0)

    for r in range(4):
        got = dot(lhs_ref[r].reshape(3 * HR * OWN, 512), box_ref[r])
        sum_ref[r] = got.reshape(3, HR, OWN, 256)
        for b in range(3):
            got = dot(edge_ref[r].reshape(HR * OWN, 256), box_edge_ref[r, b])
            side_ref[r, b] = got.reshape(HR, OWN, 256)

    def residual(i, _):
        res = []
        for b in range(3):
            var = None
            for r in range(4):
                mean = (sum_ref[r, b, i] + side_ref[r, b, i]) * (1.0 / (2 * r + 3) ** 2)
                var = mean if var is None else jnp.minimum(var, mean)
            gain = NOISE_POWER / jnp.maximum(var, NOISE_POWER)
            res.append(band_ref[b, i] * gain * 0.5)
        hz, vt, dg = res
        plus, minus = hz + vt, hz - vt
        noise = (plus + dg, minus - dg, -minus - dg, dg - plus)
        at = pl.multiple_of(i * OWN, OWN)
        for j in range(4):
            x = px_ref[j, i]
            for part, value in enumerate((noise[j].astype(BF16).astype(F32) * x, x * x)):
                hi, lo = hi_lo(value)
                data_ref[2 * j + part, pl.ds(at, OWN), :] = hi
                data_ref[2 * j + part, pl.ds(HR * OWN + at, OWN), :] = lo
        return 0

    lax.fori_loop(0, HR, residual, 0)

    ids = ids_ref[s, 0:1, :]
    row = lax.broadcasted_iota(jnp.int32, (256, 128), 0)
    col = lax.broadcasted_iota(jnp.int32, (256, 128), 1)
    same = (row // HR == ids) & (lax.rem(row, HR) == col // OWN)
    pick = jnp.where(same, 1.0, 0.0).astype(BF16)
    pick = jnp.concatenate([pick, pick], axis=1)
    for j in range(8):
        acc_ref[j] += dot(pick, data_ref[j])


def three(x):
    hi = x.astype(BF16)
    rest = x - hi.astype(F32)
    mid = rest.astype(BF16)
    low = (rest - mid.astype(F32)).astype(BF16)
    return jnp.concatenate([hi, mid, low], axis=1)


def finish(acc_ref, consts, rows_ref, fp_ref, sums_ref):
    _, _, _, join_ref, fold_ref, _, _ = consts
    planes = [acc_ref[2 * j] / acc_ref[2 * j + 1] for j in range(4)]
    for tb in range(2):
        for ct in range(2):
            pair = [planes[2 * tb + odd][:, 128 * ct : 128 * ct + 128] for odd in range(2)]
            got = dot(three(jnp.concatenate(pair, axis=1)), join_ref[...])
            for part in range(2):
                one = got[:, 128 * part : 128 * part + 128].reshape(CAMS, HR, 128)
                rows_ref[2 * ct + part, :, pl.ds(tb, HR, stride=2), :] = one
    for part in range(4):
        fp_ref[:, :, 128 * part : 128 * part + 128] = rows_ref[part]

    gram = jnp.zeros((256, 256), F32)
    for plane in planes:
        hi, lo = hi_lo(plane)
        left = jnp.concatenate([hi, hi, lo], axis=1)
        right = jnp.concatenate([hi, lo, hi], axis=1)
        gram += lax.dot_general(left, right, (((1,), (1,)), ((), ())), preferred_element_type=F32)
    row = lax.broadcasted_iota(jnp.int32, (256, 256), 0)
    col = lax.broadcasted_iota(jnp.int32, (256, 256), 1)
    gram = jnp.where(lax.rem(row, HR) == lax.rem(col, HR), gram, 0.0)
    gram = gram.reshape(CAMS, HR, 256).sum(axis=1)
    gram = dot(three(gram), fold_ref[...])
    total = planes[0] + planes[1] + planes[2] + planes[3]
    total = total.reshape(CAMS, HR, 256).sum(axis=1).sum(axis=1, keepdims=True)
    lane = lax.broadcasted_iota(jnp.int32, (CAMS, 128), 1)
    sums_ref[...] = jnp.where(lane == CAMS, total, gram)


N_CONST = 7


def fused_kernel(ext_ref, idr_ref, *rest):
    const_hbm, rest = rest[:N_CONST], rest[N_CONST:]
    fp_ref, sums_ref, x_ref, ids_ref, rows_ref = rest[:5]
    consts, rest = rest[5 : 5 + N_CONST], rest[5 + N_CONST :]
    scratch, rest = rest[:10], rest[10:]
    acc_ref = scratch[-1]
    (const_sem, own_sem, send_sem, recv_sem, isend_sem, irecv_sem,
     up_send, up_recv, dn_send, dn_recv) = rest
    me = lax.axis_index("photo")
    t = lax.axis_index("tile")

    def loads():
        return [
            pltpu.make_async_copy(a, b, const_sem.at[n])
            for n, (a, b) in enumerate(zip(const_hbm, consts))
        ]

    for copy in loads():
        copy.start()

    barrier = pltpu.get_barrier_semaphore()
    for k in range(1, PH):
        peer = lax.rem(me + k, PH)
        pl.semaphore_signal(barrier, inc=1, device_id={"photo": peer}, device_id_type=MESH)
    for k in (1, TI - 1):
        pl.semaphore_signal(
            barrier, inc=1, device_id={"tile": lax.rem(t + k, TI)}, device_id_type=MESH
        )
    pl.semaphore_wait(barrier, PH + 1)

    def a2a(k):
        peer = lax.rem(me + k, PH)
        return pltpu.make_async_remote_copy(
            src_ref=ext_ref.at[peer], dst_ref=x_ref.at[me, pl.ds(4, HR)],
            send_sem=send_sem.at[k], recv_sem=recv_sem.at[k],
            device_id={"photo": peer}, device_id_type=MESH,
        )

    def idc(k):
        peer = lax.rem(me + k, PH)
        return pltpu.make_async_remote_copy(
            src_ref=idr_ref, dst_ref=ids_ref.at[me],
            send_sem=isend_sem.at[k], recv_sem=irecv_sem.at[k],
            device_id={"photo": peer}, device_id_type=MESH,
        )

    def up(k, src, s):
        return pltpu.make_async_remote_copy(
            src_ref=src, dst_ref=x_ref.at[s, pl.ds(12, 4)],
            send_sem=up_send.at[k], recv_sem=up_recv.at[k],
            device_id={"tile": t - 1}, device_id_type=MESH,
        )

    def down(k, src, s):
        return pltpu.make_async_remote_copy(
            src_ref=src, dst_ref=x_ref.at[s, pl.ds(0, 4)],
            send_sem=dn_send.at[k], recv_sem=dn_recv.at[k],
            device_id={"tile": t + 1}, device_id_type=MESH,
        )

    def pass_on(k, first, last, s):
        @pl.when(t > 0)
        def _():
            up(k, first, s).start()

        @pl.when(t < TI - 1)
        def _():
            down(k, last, s).start()

    for k in range(1, PH):
        a2a(k).start()
    pass_on(0, ext_ref.at[me, pl.ds(0, 4)], ext_ref.at[me, pl.ds(4, 4)], me)
    for k in range(1, PH):
        idc(k).start()
    own = pltpu.make_async_copy(ext_ref.at[me], x_ref.at[me, pl.ds(4, HR)], own_sem.at[0])
    own.start()
    own_id = pltpu.make_async_copy(idr_ref, ids_ref.at[me], own_sem.at[1])
    own_id.start()

    @pl.when(t == 0)
    def _():
        x_ref[:, pl.ds(0, 4)] = jnp.zeros((PH, 4, OWN, LANES), BF16)

    @pl.when(t == TI - 1)
    def _():
        x_ref[:, pl.ds(12, 4)] = jnp.zeros((PH, 4, OWN, LANES), BF16)

    acc_ref[...] = jnp.zeros(acc_ref.shape, F32)
    own.wait()
    own_id.wait()
    for copy in loads():
        copy.wait()

    def step(k, _):
        s = lax.rem(me + PH - k, PH)

        @pl.when(k < PH - 1)
        def _():
            after = lax.rem(me + PH - 1 - k, PH)
            a2a(k + 1).wait_recv()
            idc(k + 1).wait_recv()
            pass_on(k + 1, x_ref.at[after, pl.ds(4, 4)], x_ref.at[after, pl.ds(8, 4)], after)

        @pl.when(t > 0)
        def _():
            down(k, x_ref.at[s, pl.ds(8, 4)], s).wait_recv()

        @pl.when(t < TI - 1)
        def _():
            up(k, x_ref.at[s, pl.ds(4, 4)], s).wait_recv()

        chunk(s, x_ref, ids_ref, consts, scratch)
        return 0

    lax.fori_loop(0, PH, step, 0)
    finish(acc_ref, consts, rows_ref, fp_ref, sums_ref)

    for k in range(1, PH):
        a2a(k).wait_send()
        idc(k).wait_send()
    for k in range(PH):
        s = lax.rem(me + PH - k, PH)

        @pl.when(t > 0)
        def _():
            up(k, x_ref.at[s, pl.ds(4, 4)], s).wait_send()

        @pl.when(t < TI - 1)
        def _():
            down(k, x_ref.at[s, pl.ds(8, 4)], s).wait_send()


SCRATCH = [
    ((3, 2 * HR, OWN, 256), F32),
    ((2 * HR, OWN, 128), F32),
    ((3, HR, OWN, 256), F32),
    ((4, 3, HR, OWN, 512), BF16),
    ((4, HR, OWN, 256), BF16),
    ((4, 3, HR, OWN, 256), F32),
    ((4, 3, HR, OWN, 256), F32),
    ((4, HR, OWN, 256), F32),
    ((8, 256, 256), BF16),
    ((8, 256, 256), F32),
]


def fused(ext, idr, consts):
    vm = pl.BlockSpec(memory_space=pltpu.VMEM)
    anywhere = pl.BlockSpec(memory_space=pl.ANY)
    dma = pltpu.SemaphoreType.DMA
    return pl.pallas_call(
        fused_kernel,
        out_shape=(
            jax.ShapeDtypeStruct((CAMS, 16, 512), F32),
            jax.ShapeDtypeStruct((CAMS, 128), F32),
        ),
        in_specs=[anywhere] * (2 + N_CONST),
        out_specs=(vm, vm),
        scratch_shapes=[
            pltpu.VMEM((PH, 2 * HR, OWN, LANES), BF16),
            pltpu.VMEM((PH, 8, 128), jnp.int32),
            pltpu.VMEM((4, CAMS, 16, 128), F32),
        ]
        + [pltpu.VMEM(c.shape, c.dtype) for c in consts]
        + [pltpu.VMEM(s, d) for s, d in SCRATCH]
        + [dma((N_CONST,)), dma((2,))]
        + [dma((PH,))] * 8,
        compiler_params=pltpu.CompilerParams(
            collective_id=0, has_side_effects=True, vmem_limit_bytes=VMEM_LIMIT
        ),
        name="fused",
    )(ext, idr, *consts)


def correlated(total):
    pixels = float(256 * 4096)
    row = lax.broadcasted_iota(jnp.int32, total.shape, 0)
    lane = lax.broadcasted_iota(jnp.int32, total.shape, 1)
    average = total[:, CAMS : CAMS + 1] / pixels
    across = jnp.sum(jnp.where(row == lane, average, 0.0), axis=0, keepdims=True)
    covar = total / pixels - average * across
    own = jnp.where(row == lane, covar, 0.0)
    down = jnp.sum(own, axis=1, keepdims=True) + VAR_EPS
    along = jnp.sum(own, axis=0, keepdims=True) + VAR_EPS
    return covar / jnp.sqrt(down * along)


def allsum_kernel(x_ref, o_ref, a_ref, m_ref, b_ref, as_sem, ar_sem, bs_sem, br_sem):
    me = lax.axis_index("photo")
    t = lax.axis_index("tile")
    barrier = pltpu.get_barrier_semaphore()
    for k in range(1, PH):
        pl.semaphore_signal(
            barrier, inc=1, device_id={"photo": lax.rem(me + k, PH)}, device_id_type=MESH
        )
    for k in range(1, TI):
        pl.semaphore_signal(
            barrier, inc=1, device_id={"tile": lax.rem(t + k, TI)}, device_id_type=MESH
        )
    pl.semaphore_wait(barrier, PH + TI - 2)

    def first(k):
        return pltpu.make_async_remote_copy(
            src_ref=x_ref, dst_ref=a_ref.at[k - 1], send_sem=as_sem.at[k - 1],
            recv_sem=ar_sem.at[k - 1],
            device_id={"photo": lax.rem(me + k, PH)}, device_id_type=MESH,
        )

    def second(k):
        return pltpu.make_async_remote_copy(
            src_ref=m_ref, dst_ref=b_ref.at[k - 1], send_sem=bs_sem.at[k - 1],
            recv_sem=br_sem.at[k - 1],
            device_id={"tile": lax.rem(t + k, TI)}, device_id_type=MESH,
        )

    for k in range(1, PH):
        first(k).start()
    for k in range(1, PH):
        first(k).wait_recv()
    total = jnp.zeros(x_ref.shape, F32)
    for s in range(PH):
        k = lax.rem(me + PH - s, PH)
        other = a_ref[jnp.maximum(k - 1, 0)]
        total += jnp.where(k == 0, x_ref[...], other)
    m_ref[...] = total
    for k in range(1, TI):
        second(k).start()
    for k in range(1, TI):
        second(k).wait_recv()
    total = jnp.zeros(x_ref.shape, F32)
    for s in range(TI):
        k = lax.rem(t + TI - s, TI)
        other = b_ref[jnp.maximum(k - 1, 0)]
        total += jnp.where(k == 0, m_ref[...], other)
    o_ref[...] = correlated(total)[:, :CAMS]
    for k in range(1, PH):
        first(k).wait_send()
    for k in range(1, TI):
        second(k).wait_send()


def allsum(x):
    vm = pl.BlockSpec(memory_space=pltpu.VMEM)
    dma = pltpu.SemaphoreType.DMA
    return pl.pallas_call(
        allsum_kernel,
        out_shape=jax.ShapeDtypeStruct((CAMS, CAMS), F32),
        in_specs=[vm],
        out_specs=vm,
        scratch_shapes=[
            pltpu.VMEM((PH - 1,) + x.shape, F32),
            pltpu.VMEM(x.shape, F32),
            pltpu.VMEM((TI - 1,) + x.shape, F32),
            dma((PH - 1,)), dma((PH - 1,)), dma((TI - 1,)), dma((TI - 1,)),
        ],
        compiler_params=pltpu.CompilerParams(collective_id=1, has_side_effects=True),
        name="allsum",
    )(x)


def on_device(photos, camera_id):
    perm, edge, *consts = constants()
    ext = packed(photos, perm, edge)
    idr = jnp.broadcast_to(camera_id[None, None, :], (8, HR, OWN))
    fingerprints, sums = fused(ext, idr.reshape(8, 128), consts)
    return (fingerprints, allsum(sums))


def solution(mesh):
    return jax.shard_map(
        on_device,
        mesh=mesh,
        in_specs=(P("photo", "tile", None), P("photo")),
        out_specs=(P(None, "tile", "photo"), P()),
        check_vma=False,
    )
```

```python
import functools

import jax
import jax.numpy as jnp
import numpy as np
from jax import lax
from jax.experimental import pallas as pl
from jax.experimental.pallas import tpu as pltpu
from jax.sharding import PartitionSpec as P

MESH = pl.DeviceIdType.MESH
F32 = jnp.float32
BF16 = jnp.bfloat16

CAMS = 32
NOISE_POWER = 1.0
VAR_EPS = 1e-06

PH = 8
TI = 16
OWN = 16
HR = 8
LANES = 1024
VMEM_LIMIT = 60 * 1024 * 1024


def constants():
    perm = np.zeros((256, 256), np.float32)
    for tb in range(2):
        for i in range(HR):
            for p in range(OWN):
                perm[(tb * HR + i) * OWN + p, p * 16 + 2 * i + tb] = 1.0
    edge = np.zeros((8, 256, 128), np.float32)
    for jt in range(8):
        for k in range(8):
            edge[jt, 120 + k, 16 * jt + k] = 1.0
            edge[jt, 128 + k, 16 * jt + 8 + k] = 1.0
    sign = np.array([[1, 1, 1], [1, -1, -1], [-1, 1, -1], [-1, -1, 1]], np.float32) * 0.5
    haar = np.zeros((512, 384), np.float32)
    for j in range(128):
        for b in range(3):
            haar[2 * j, 128 * b + j] = sign[0, b]
            haar[2 * j + 1, 128 * b + j] = sign[1, b]
            haar[256 + 2 * j, 128 * b + j] = sign[2, b]
            haar[256 + 2 * j + 1, 128 * b + j] = sign[3, b]
    haar_edge = np.zeros((128, 512), np.float32)
    for j in range(4):
        for k in range(8):
            for b in range(3):
                for n in range(4):
                    at = 32 * j + 16 * (n // 2) + 2 * k + n % 2
                    haar_edge[at, 128 * j + 8 * b + k] = sign[n, b]
    split = np.zeros((256, 256), np.float32)
    for j in range(128):
        split[2 * j, j] = 1.0
        split[2 * j + 1, 128 + j] = 1.0
    out = np.arange(256)
    box = np.zeros((4, 512, 256), np.float32)
    box_edge = np.zeros((4, 3, 256, 256), np.float32)
    for r in range(1, 5):
        inner = (np.abs(out[:, None] - out[None, :]) <= r).astype(np.float32)
        box[r - 1] = np.concatenate([inner, inner])
        for b in range(3):
            side = np.zeros((128, 256), np.float32)
            for k in range(8):
                cell = k - 4 if k < 4 else 252 + k
                side[8 * b + k] = np.abs(cell - out) <= r
            box_edge[r - 1, b] = np.concatenate([side, side])
    join = np.concatenate([split.T] * 3)
    fold = np.zeros((256, 128), np.float32)
    fold[np.arange(256), np.arange(256) // HR] = 1.0
    fold = np.concatenate([fold] * 3)
    every = (perm, edge, haar, haar_edge, split, join, fold, box, box_edge)
    return [jnp.asarray(c, BF16) for c in every]


def dot(a, b):
    return jnp.dot(a, b, preferred_element_type=F32)


def hi_lo(x):
    hi = x.astype(BF16)
    lo = (x - hi.astype(F32)).astype(BF16)
    return hi, lo


def chunk(s, x_ref, e_ref, consts, scratch):
    haar_ref, haar_edge_ref, split_ref, _, _, box_ref, box_edge_ref = consts[2:]
    sq_ref, eq_ref, band_ref, lhs_ref, edge_ref, sum_ref, side_ref, px_ref, data_ref, acc_ref = scratch

    rows = 2 * HR
    for ct in range(2):
        x = x_ref[s, :, :, 512 * ct : 512 * ct + 512].reshape(rows * OWN, 512)
        got = dot(x, haar_ref[...])
        for b in range(3):
            one = got[:, 128 * b : 128 * b + 128].reshape(rows, OWN, 128)
            band_ref[b, :, :, 128 * ct : 128 * ct + 128] = one[4 : 4 + HR]
            sq_ref[b, :, :, 128 * ct : 128 * ct + 128] = one * one
        for tb in range(2):
            lane = 512 * ct + 256 * tb
            x = x_ref[s, pl.ds(4, HR), :, lane : lane + 256].reshape(HR * OWN, 256)
            got = dot(x, split_ref[...])
            for odd in range(2):
                px_ref[2 * tb + odd, :, :, 128 * ct : 128 * ct + 128] = got[
                    :, 128 * odd : 128 * odd + 128
                ].reshape(HR, OWN, 128)
    x = jnp.concatenate([e_ref[s, n] for n in (0, 1, 2, 4)])
    one = dot(x, haar_edge_ref[...])
    for n in range(rows):
        g, j = divmod(n, 4)
        part = one[OWN * g : OWN * g + OWN, 128 * j : 128 * j + 128]
        eq_ref[n] = part * part

    def sums(i, _):
        row = eq_ref[i + 4]
        for r in range(1, 5):
            row = row + eq_ref[i + 4 - r] + eq_ref[i + 4 + r]
            hi, lo = hi_lo(row)
            edge_ref[r - 1, i, :, 0:128] = hi
            edge_ref[r - 1, i, :, 128:256] = lo
        for b in range(3):
            row = sq_ref[b, i + 4]
            for r in range(1, 5):
                row = row + sq_ref[b, i + 4 - r] + sq_ref[b, i + 4 + r]
                hi, lo = hi_lo(row)
                lhs_ref[r - 1, b, i, :, 0:256] = hi
                lhs_ref[r - 1, b, i, :, 256:512] = lo
        return 0

    lax.fori_loop(0, HR, sums, 0)

    for r in range(4):
        got = dot(lhs_ref[r].reshape(3 * HR * OWN, 512), box_ref[r])
        sum_ref[r] = got.reshape(3, HR, OWN, 256)
        for b in range(3):
            got = dot(edge_ref[r].reshape(HR * OWN, 256), box_edge_ref[r, b])
            side_ref[r, b] = got.reshape(HR, OWN, 256)

    def residual(i, _):
        res = []
        for b in range(3):
            var = None
            for r in range(4):
                mean = (sum_ref[r, b, i] + side_ref[r, b, i]) * (1.0 / (2 * r + 3) ** 2)
                var = mean if var is None else jnp.minimum(var, mean)
            gain = NOISE_POWER / jnp.maximum(var, NOISE_POWER)
            res.append(band_ref[b, i] * gain * 0.5)
        hz, vt, dg = res
        plus, minus = hz + vt, hz - vt
        noise = (plus + dg, minus - dg, -minus - dg, dg - plus)
        at = pl.multiple_of(i * OWN, OWN)
        for j in range(4):
            x = px_ref[j, i]
            for part, value in enumerate((noise[j].astype(BF16).astype(F32) * x, x * x)):
                hi, lo = hi_lo(value)
                data_ref[2 * j + part, pl.ds(at, OWN), :] = hi
                data_ref[2 * j + part, pl.ds(HR * OWN + at, OWN), :] = lo
        return 0

    lax.fori_loop(0, HR, residual, 0)

    ids = e_ref[s, 3].astype(F32)[0:1, :]
    row = lax.broadcasted_iota(jnp.int32, (256, 128), 0)
    col = lax.broadcasted_iota(jnp.int32, (256, 128), 1)
    same = ((row // HR).astype(F32) == ids) & (lax.rem(row, HR) == col // OWN)
    pick = jnp.where(same, 1.0, 0.0).astype(BF16)
    pick = jnp.concatenate([pick, pick], axis=1)
    for j in range(8):
        acc_ref[j] += dot(pick, data_ref[j])


def three(x):
    hi = x.astype(BF16)
    rest = x - hi.astype(F32)
    mid = rest.astype(BF16)
    low = (rest - mid.astype(F32)).astype(BF16)
    return jnp.concatenate([hi, mid, low], axis=1)


def total_gram(acc_ref, fold_ref):
    planes = [acc_ref[2 * j] / acc_ref[2 * j + 1] for j in range(4)]
    gram = jnp.zeros((256, 256), F32)
    for plane in planes:
        hi, lo = hi_lo(plane)
        left = jnp.concatenate([hi, hi, lo], axis=1)
        right = jnp.concatenate([hi, lo, hi], axis=1)
        gram += lax.dot_general(left, right, (((1,), (1,)), ((), ())), preferred_element_type=F32)
    row = lax.broadcasted_iota(jnp.int32, (256, 256), 0)
    col = lax.broadcasted_iota(jnp.int32, (256, 256), 1)
    gram = jnp.where(lax.rem(row, HR) == lax.rem(col, HR), gram, 0.0)
    gram = gram.reshape(CAMS, HR, 256).sum(axis=1)
    gram = dot(three(gram), fold_ref[...])
    total = planes[0] + planes[1] + planes[2] + planes[3]
    total = total.reshape(CAMS, HR, 256).sum(axis=1).sum(axis=1, keepdims=True)
    lane = lax.broadcasted_iota(jnp.int32, (8, 128), 1)
    upper, lower = jnp.zeros((8, 128), F32), jnp.zeros((8, 128), F32)
    for q in range(4):
        part = gram[8 * q : 8 * q + 8]
        if q:
            part = pltpu.roll(part, 32 * q, 1)
        upper = jnp.where(lane // 32 == q, part, upper)
        lower = jnp.where(lane == q, total[8 * q : 8 * q + 8], lower)
    return planes, jnp.concatenate([upper, lower])


def correlated(sums):
    upper, lower = sums[0:8], sums[8:16]
    gram = jnp.concatenate([upper] + [pltpu.roll(upper, 128 - 32 * q, 1) for q in range(1, 4)])
    total = jnp.concatenate([lower[:, q : q + 1] for q in range(4)])
    pixels = float(256 * 4096)
    row = lax.broadcasted_iota(jnp.int32, gram.shape, 0)
    lane = lax.broadcasted_iota(jnp.int32, gram.shape, 1)
    average = total / pixels
    across = jnp.sum(jnp.where(row == lane, average, 0.0), axis=0, keepdims=True)
    covar = gram / pixels - average * across
    own = jnp.where(row == lane, covar, 0.0)
    down = jnp.sum(own, axis=1, keepdims=True) + VAR_EPS
    along = jnp.sum(own, axis=0, keepdims=True) + VAR_EPS
    return (covar / jnp.sqrt(down * along))[:, :CAMS]


def join(planes, join_ref, rows_ref):
    for tb in range(2):
        for ct in range(2):
            pair = [planes[2 * tb + odd][:, 128 * ct : 128 * ct + 128] for odd in range(2)]
            got = dot(three(jnp.concatenate(pair, axis=1)), join_ref[...])
            for part in range(2):
                one = got[:, 128 * part : 128 * part + 128].reshape(CAMS, HR, 128)
                rows_ref[2 * ct + part, :, pl.ds(tb, HR, stride=2), :] = one


def pack(photo_ref, cid_ref, perm_ref, edge_ref, block_ref, side_ref, beside_ref):
    beside_ref[:, 1, :, :, 0:128] = jnp.zeros((8, 2, OWN, 128), BF16)
    beside_ref[:, PH, :, :, 128:256] = jnp.zeros((8, 2, OWN, 128), BF16)

    def block(d, _):
        for ct in range(2):
            lane = pl.multiple_of(512 * d + 256 * ct, 256)
            x = photo_ref[:, :, pl.ds(lane, 256)].reshape(256, 256)
            y = dot(perm_ref[...], x).astype(BF16).reshape(2, HR, OWN, 256)
            for tb in range(2):
                lane = ct * 512 + tb * 256
                block_ref[d, :, :, lane : lane + 256] = y[tb]
                for i in range(HR):
                    g, j = divmod(i, 4)
                    if ct == 0:
                        beside_ref[2 * j + tb, d, g, :, 128:256] = y[tb, i, :, 0:128]
                    else:
                        beside_ref[2 * j + tb, d + 2, g, :, 0:128] = y[tb, i, :, 128:256]
        return 0

    lax.fori_loop(0, PH, block, 0)
    side = jnp.zeros((256, 128), F32)
    for jt in range(8):
        side += dot(beside_ref[jt, pl.ds(1, PH)].reshape(256, 256), edge_ref[jt])
    side_ref[:, pl.ds(0, 2)] = side.astype(BF16).reshape(PH, 2, OWN, 128)
    lane = lax.broadcasted_iota(jnp.int32, (OWN, 128), 1)
    ids = jnp.zeros((OWN, 128), jnp.int32)
    for n in range(OWN):
        ids = jnp.where(lax.rem(lane, OWN) == n, cid_ref[n], ids)
    ids = ids.astype(F32).astype(BF16)
    for d in range(PH):
        side_ref[d, 2] = ids


N_CONST = 9


def fused_kernel(photo_ref, cid_ref, *rest):
    const_hbm, rest = rest[:N_CONST], rest[N_CONST:]
    fp_ref, corr_ref, block_ref, side_ref, beside_ref, x_ref, e_ref, rows_ref, a_ref, b_ref = rest[:10]
    consts, rest = rest[10 : 10 + N_CONST], rest[10 + N_CONST :]
    scratch, rest = rest[:10], rest[10:]
    acc_ref = scratch[-1]
    (const_sem, own_sem, send_sem, recv_sem, up_send, up_recv, dn_send, dn_recv,
     as_sem, ar_sem, bs_sem, br_sem) = rest
    me = lax.axis_index("photo")
    t = lax.axis_index("tile")

    def load(n):
        return pltpu.make_async_copy(const_hbm[n], consts[n], const_sem.at[n])

    for n in range(N_CONST):
        load(n).start()

    barrier = pltpu.get_barrier_semaphore()
    middle = t * (TI - 1 - t) // 56
    for k in range(1, PH):
        peer = lax.rem(me + k, PH)
        pl.semaphore_signal(barrier, inc=1, device_id={"photo": peer}, device_id_type=MESH)
    for k in range(1, TI):
        pl.semaphore_signal(
            barrier, inc=1, device_id={"tile": lax.rem(t + k, TI)}, device_id_type=MESH
        )

    @pl.when(middle == 1)
    def _():
        for k in range(1, PH):
            where = {"photo": lax.rem(me + k, PH), "tile": TI - 1 - t}
            pl.semaphore_signal(barrier, inc=1, device_id=where, device_id_type=MESH)

    load(0).wait()
    load(1).wait()
    pack(photo_ref, cid_ref, consts[0], consts[1], block_ref, side_ref, beside_ref)
    pl.semaphore_wait(barrier, PH + TI - 2 + (PH - 1) * middle)

    def remote(srcs, dsts, send, recv, k, where):
        return [
            pltpu.make_async_remote_copy(
                src_ref=a, dst_ref=b, send_sem=send.at[n, k], recv_sem=recv.at[n, k],
                device_id=where, device_id_type=MESH,
            )
            for n, (a, b) in enumerate(zip(srcs, dsts))
        ]

    def a2a(k):
        peer = lax.rem(me + k, PH)
        return remote(
            (block_ref.at[peer], side_ref.at[peer]),
            (x_ref.at[me, pl.ds(4, HR)], e_ref.at[me, pl.ds(1, 3)]),
            send_sem, recv_sem, k, {"photo": peer},
        )

    def up(k, srcs, s, where):
        dsts = (x_ref.at[s, pl.ds(12, 4)], e_ref.at[s, 4])
        return remote(srcs, dsts, up_send, up_recv, k, where)

    def down(k, srcs, s, where):
        dsts = (x_ref.at[s, pl.ds(0, 4)], e_ref.at[s, 0])
        return remote(srcs, dsts, dn_send, dn_recv, k, where)

    def held(s, first):
        return (x_ref.at[s, pl.ds(4 if first else 8, 4)], e_ref.at[s, 1 if first else 2])

    def mine(d, first):
        return (block_ref.at[d, pl.ds(0 if first else 4, 4)], side_ref.at[d, 0 if first else 1])

    def each(copies, act):
        for copy in copies:
            getattr(copy, act)()

    for k in range(1, PH):
        each(a2a(k), "start")

    @pl.when(t == TI // 2 - 1)
    def _():
        for k in range(PH):
            peer = lax.rem(me + k, PH)
            each(down(k, mine(peer, False), me, {"photo": peer, "tile": t + 1}), "start")

    @pl.when(t == TI // 2)
    def _():
        for k in range(PH):
            peer = lax.rem(me + k, PH)
            each(up(k, mine(peer, True), me, {"photo": peer, "tile": t - 1}), "start")

    def pass_on(k, source, s):
        @pl.when((t > 0) & (t != TI // 2))
        def _():
            each(up(k, source(s, True), s, {"tile": t - 1}), "start")

        @pl.when((t < TI - 1) & (t != TI // 2 - 1))
        def _():
            each(down(k, source(s, False), s, {"tile": t + 1}), "start")

    pass_on(0, mine, me)
    own = [
        pltpu.make_async_copy(block_ref.at[me], x_ref.at[me, pl.ds(4, HR)], own_sem.at[0]),
        pltpu.make_async_copy(side_ref.at[me], e_ref.at[me, pl.ds(1, 3)], own_sem.at[1]),
    ]
    each(own, "start")

    @pl.when(t == 0)
    def _():
        x_ref[:, pl.ds(0, 4)] = jnp.zeros((PH, 4, OWN, LANES), BF16)
        e_ref[:, 0] = jnp.zeros((PH, OWN, 128), BF16)

    @pl.when(t == TI - 1)
    def _():
        x_ref[:, pl.ds(12, 4)] = jnp.zeros((PH, 4, OWN, LANES), BF16)
        e_ref[:, 4] = jnp.zeros((PH, OWN, 128), BF16)

    acc_ref[...] = jnp.zeros(acc_ref.shape, F32)
    each(own, "wait")
    for n in range(2, N_CONST):
        load(n).wait()

    def step(k, _):
        s = lax.rem(me + PH - k, PH)

        @pl.when(k < PH - 1)
        def _():
            after = lax.rem(me + PH - 1 - k, PH)
            each(a2a(k + 1), "wait_recv")
            pass_on(k + 1, held, after)

        @pl.when(t > 0)
        def _():
            each(down(k, held(s, False), s, {"tile": t - 1}), "wait_recv")

        @pl.when(t < TI - 1)
        def _():
            each(up(k, held(s, True), s, {"tile": t + 1}), "wait_recv")

        chunk(s, x_ref, e_ref, consts, scratch)
        return 0

    lax.fori_loop(0, PH, step, 0)

    def first(k):
        return pltpu.make_async_remote_copy(
            src_ref=a_ref.at[me], dst_ref=a_ref.at[me], send_sem=as_sem.at[k],
            recv_sem=ar_sem.at[k],
            device_id={"photo": lax.rem(me + k, PH)}, device_id_type=MESH,
        )

    def second(k):
        return pltpu.make_async_remote_copy(
            src_ref=b_ref.at[t], dst_ref=b_ref.at[t], send_sem=bs_sem.at[k],
            recv_sem=br_sem.at[k],
            device_id={"tile": lax.rem(t + k, TI)}, device_id_type=MESH,
        )

    planes, sums = total_gram(acc_ref, consts[6])
    a_ref[me] = sums
    for k in range(1, PH):
        first(k).start()
    join(planes, consts[5], rows_ref)
    out = [
        pltpu.make_async_copy(
            rows_ref.at[n], fp_ref.at[:, :, pl.ds(128 * n, 128)], own_sem.at[2 + n]
        )
        for n in range(4)
    ]
    each(out, "start")
    for k in range(1, PH):
        first(k).wait_recv()
    sums = a_ref[0]
    for n in range(1, PH):
        sums += a_ref[n]
    b_ref[t] = sums
    for k in range(1, TI):
        second(k).start()
    for k in range(1, TI):
        second(k).wait_recv()
    sums = b_ref[0]
    for n in range(1, TI):
        sums += b_ref[n]
    corr_ref[...] = correlated(sums)

    each(out, "wait")
    for k in range(1, PH):
        each(a2a(k), "wait_send")
        first(k).wait_send()
    for k in range(1, TI):
        second(k).wait_send()
    for k in range(PH):
        s = lax.rem(me + PH - k, PH)

        @pl.when(t > 0)
        def _():
            each(up(k, held(s, True), s, {"tile": t - 1}), "wait_send")

        @pl.when(t < TI - 1)
        def _():
            each(down(k, held(s, False), s, {"tile": t + 1}), "wait_send")


SCRATCH = [
    ((3, 2 * HR, OWN, 256), F32),
    ((2 * HR, OWN, 128), F32),
    ((3, HR, OWN, 256), F32),
    ((4, 3, HR, OWN, 512), BF16),
    ((4, HR, OWN, 256), BF16),
    ((4, 3, HR, OWN, 256), F32),
    ((4, 3, HR, OWN, 256), F32),
    ((4, HR, OWN, 256), F32),
    ((8, 256, 256), BF16),
    ((8, 256, 256), F32),
]


def fused(photos, camera_id, consts):
    vm = pl.BlockSpec(memory_space=pltpu.VMEM)
    anywhere = pl.BlockSpec(memory_space=pl.ANY)
    dma = pltpu.SemaphoreType.DMA
    return pl.pallas_call(
        fused_kernel,
        out_shape=(
            jax.ShapeDtypeStruct((CAMS, 16, 512), F32),
            jax.ShapeDtypeStruct((CAMS, CAMS), F32),
        ),
        in_specs=[vm, pl.BlockSpec(memory_space=pltpu.SMEM)] + [anywhere] * N_CONST,
        out_specs=(anywhere, vm),
        scratch_shapes=[
            pltpu.VMEM((PH, HR, OWN, LANES), BF16),
            pltpu.VMEM((PH, 3, OWN, 128), BF16),
            pltpu.VMEM((8, PH + 2, 2, OWN, 256), BF16),
            pltpu.VMEM((PH, 2 * HR, OWN, LANES), BF16),
            pltpu.VMEM((PH, 5, OWN, 128), BF16),
            pltpu.VMEM((4, CAMS, 16, 128), F32),
            pltpu.VMEM((PH, 16, 128), F32),
            pltpu.VMEM((TI, 16, 128), F32),
        ]
        + [pltpu.VMEM(c.shape, c.dtype) for c in consts]
        + [pltpu.VMEM(s, d) for s, d in SCRATCH]
        + [dma((N_CONST,)), dma((6,))]
        + [dma((2, PH))] * 6
        + [dma((PH,))] * 2
        + [dma((TI,))] * 2,
        compiler_params=pltpu.CompilerParams(
            collective_id=0, has_side_effects=True, vmem_limit_bytes=VMEM_LIMIT
        ),
        name="fused",
    )(photos, camera_id, *consts)


def on_device(photos, camera_id):
    return fused(photos, camera_id, constants())


def solution(mesh):
    return jax.shard_map(
        on_device,
        mesh=mesh,
        in_specs=(P("photo", "tile", None), P("photo")),
        out_specs=(P(None, "tile", "photo"), P()),
        check_vma=False,
    )
```

```python
import functools

import jax
import jax.numpy as jnp
import numpy as np
from jax import lax
from jax.experimental import pallas as pl
from jax.experimental.pallas import tpu as pltpu
from jax.sharding import PartitionSpec as P

MESH = pl.DeviceIdType.MESH
F32 = jnp.float32
BF16 = jnp.bfloat16

CAMS = 32
NOISE_POWER = 1.0
VAR_EPS = 1e-06

PH = 8
TI = 16
OWN = 16
HR = 8
LANES = 1024
VMEM_LIMIT = 60 * 1024 * 1024

MOVES = ((0, 0), (0, 1), (3, 0), (1, 0), (1, 1), (3, 1), (2, 0), (2, 1))
ISSUE = (1, 3, 2, 6, 4, 5, 7)


def constants():
    perm = np.zeros((256, 256), np.float32)
    for tb in range(2):
        for i in range(HR):
            for p in range(OWN):
                perm[(tb * HR + i) * OWN + p, p * 16 + 2 * i + tb] = 1.0
    edge = np.zeros((8, 256, 128), np.float32)
    for jt in range(8):
        for k in range(8):
            edge[jt, 120 + k, 16 * jt + k] = 1.0
            edge[jt, 128 + k, 16 * jt + 8 + k] = 1.0
    sign = np.array([[1, 1, 1], [1, -1, -1], [-1, 1, -1], [-1, -1, 1]], np.float32) * 0.5
    haar_edge = np.zeros((128, 512), np.float32)
    for j in range(4):
        for k in range(8):
            for b in range(3):
                for n in range(4):
                    at = 32 * j + 16 * (n // 2) + 2 * k + n % 2
                    haar_edge[at, 128 * j + 8 * b + k] = sign[n, b]
    split = np.zeros((256, 256), np.float32)
    for j in range(128):
        split[2 * j, j] = 0.5
        split[2 * j + 1, 128 + j] = 0.5
    out = np.arange(256)
    box = np.zeros((4, 512, 256), np.float32)
    box_edge = np.zeros((4, 3, 256, 256), np.float32)
    for r in range(1, 5):
        inner = (np.abs(out[:, None] - out[None, :]) <= r).astype(np.float32)
        box[r - 1] = np.concatenate([inner, inner])
        for b in range(3):
            side = np.zeros((128, 256), np.float32)
            for k in range(8):
                cell = k - 4 if k < 4 else 252 + k
                side[8 * b + k] = np.abs(cell - out) <= r
            box_edge[r - 1, b] = np.concatenate([side, side])
    join = np.concatenate([split.T] * 3)
    fold = np.zeros((256, 128), np.float32)
    fold[np.arange(256), np.arange(256) // HR] = 1.0
    fold = np.concatenate([fold] * 3)
    every = (perm, edge, haar_edge, split, join, fold, box, box_edge)
    return [jnp.asarray(c, BF16) for c in every]


def dot(a, b):
    return jnp.dot(a, b, preferred_element_type=F32)


def hi_lo(x):
    hi = x.astype(BF16)
    lo = (x - hi.astype(F32)).astype(BF16)
    return hi, lo


def bands_of(px_ref, n):
    a, b, c, d = (px_ref[j, n] for j in range(4))
    plus, minus, low_plus, low_minus = a + b, a - b, c + d, c - d
    return plus - low_plus, minus + low_minus, minus - low_minus


def chunk(s, x_ref, e_ref, consts, scratch):
    haar_edge_ref, split_ref, _, _, box_ref, box_edge_ref = consts[2:]
    sq_ref, eq_ref, lhs_ref, edge_ref, sum_ref, side_ref, px_ref, data_ref, acc_ref = scratch

    rows = 2 * HR
    for ct in range(2):
        for tb in range(2):
            lane = 512 * ct + 256 * tb
            x = x_ref[s, :, :, lane : lane + 256].reshape(rows * OWN, 256)
            got = dot(x, split_ref[...])
            for odd in range(2):
                px_ref[2 * tb + odd, :, :, 128 * ct : 128 * ct + 128] = got[
                    :, 128 * odd : 128 * odd + 128
                ].reshape(rows, OWN, 128)

    def squares(n, _):
        for b, band in enumerate(bands_of(px_ref, n)):
            sq_ref[b, n] = band * band
        return 0

    lax.fori_loop(0, rows, squares, 0, unroll=2)
    x = jnp.concatenate([e_ref[s, n] for n in (0, 1, 2, 4)])
    one = dot(x, haar_edge_ref[...])
    for n in range(rows):
        g, j = divmod(n, 4)
        part = one[OWN * g : OWN * g + OWN, 128 * j : 128 * j + 128]
        eq_ref[n] = part * part

    def sums(i, _):
        row = eq_ref[i + 4]
        for r in range(1, 5):
            row = row + eq_ref[i + 4 - r] + eq_ref[i + 4 + r]
            hi, lo = hi_lo(row)
            edge_ref[r - 1, i, :, 0:128] = hi
            edge_ref[r - 1, i, :, 128:256] = lo
        for b in range(3):
            row = sq_ref[b, i + 4]
            for r in range(1, 5):
                row = row + sq_ref[b, i + 4 - r] + sq_ref[b, i + 4 + r]
                hi, lo = hi_lo(row)
                lhs_ref[r - 1, b, i, :, 0:256] = hi
                lhs_ref[r - 1, b, i, :, 256:512] = lo
        return 0

    lax.fori_loop(0, HR, sums, 0)

    for r in range(4):
        got = dot(lhs_ref[r].reshape(3 * HR * OWN, 512), box_ref[r])
        sum_ref[r] = got.reshape(3, HR, OWN, 256)
        for b in range(3):
            got = dot(edge_ref[r].reshape(HR * OWN, 256), box_edge_ref[r, b])
            side_ref[r, b] = got.reshape(HR, OWN, 256)

    def residual(i, _):
        res = []
        for b, band in enumerate(bands_of(px_ref, i + 4)):
            var = None
            for r in range(4):
                mean = (sum_ref[r, b, i] + side_ref[r, b, i]) * (1.0 / (2 * r + 3) ** 2)
                var = mean if var is None else jnp.minimum(var, mean)
            gain = NOISE_POWER / jnp.maximum(var, NOISE_POWER)
            res.append(band * gain * 0.5)
        hz, vt, dg = res
        plus, minus = hz + vt, hz - vt
        noise = (plus + dg, minus - dg, -minus - dg, dg - plus)
        at = pl.multiple_of(i * OWN, OWN)
        for j in range(4):
            x = px_ref[j, i + 4]
            for part, value in enumerate((noise[j].astype(BF16).astype(F32) * x, x * x)):
                hi, lo = hi_lo(value)
                data_ref[2 * j + part, pl.ds(at, OWN), :] = hi
                data_ref[2 * j + part, pl.ds(HR * OWN + at, OWN), :] = lo
        return 0

    lax.fori_loop(0, HR, residual, 0)

    ids = e_ref[s, 3].astype(F32)[0:1, :]
    row = lax.broadcasted_iota(jnp.int32, (256, 128), 0)
    col = lax.broadcasted_iota(jnp.int32, (256, 128), 1)
    same = ((row // HR).astype(F32) == ids) & (lax.rem(row, HR) == col // OWN)
    pick = jnp.where(same, 1.0, 0.0).astype(BF16)
    pick = jnp.concatenate([pick, pick], axis=1)
    for j in range(8):
        acc_ref[j] += dot(pick, data_ref[j])


def three(x):
    hi = x.astype(BF16)
    rest = x - hi.astype(F32)
    mid = rest.astype(BF16)
    low = (rest - mid.astype(F32)).astype(BF16)
    return jnp.concatenate([hi, mid, low], axis=1)


def total_gram(acc_ref, fold_ref):
    planes = [acc_ref[2 * j] / acc_ref[2 * j + 1] for j in range(4)]
    gram = jnp.zeros((256, 256), F32)
    for plane in planes:
        hi, lo = hi_lo(plane)
        left = jnp.concatenate([hi, hi, lo], axis=1)
        right = jnp.concatenate([hi, lo, hi], axis=1)
        gram += lax.dot_general(left, right, (((1,), (1,)), ((), ())), preferred_element_type=F32)
    row = lax.broadcasted_iota(jnp.int32, (256, 256), 0)
    col = lax.broadcasted_iota(jnp.int32, (256, 256), 1)
    gram = jnp.where(lax.rem(row, HR) == lax.rem(col, HR), gram, 0.0)
    gram = gram.reshape(CAMS, HR, 256).sum(axis=1)
    gram = dot(three(gram), fold_ref[...]) * 0.25
    total = planes[0] + planes[1] + planes[2] + planes[3]
    total = total.reshape(CAMS, HR, 256).sum(axis=1).sum(axis=1, keepdims=True) * 0.5
    row = lax.broadcasted_iota(jnp.int32, (CAMS, 128), 0)
    lane = lax.broadcasted_iota(jnp.int32, (CAMS, 128), 1)
    gram = jnp.where(lane == lax.rem(row + CAMS - 1, CAMS), total, gram)
    lane = lax.broadcasted_iota(jnp.int32, (8, 128), 1)
    sums = gram[0:8]
    for q in range(1, 4):
        part = pltpu.roll(gram[8 * q : 8 * q + 8], 32 * q, 1)
        sums = jnp.where(lane // 32 == q, part, sums)
    return planes, sums


def correlated(sums):
    gram = jnp.concatenate([sums] + [pltpu.roll(sums, 128 - 32 * q, 1) for q in range(1, 4)])
    row = lax.broadcasted_iota(jnp.int32, gram.shape, 0)
    lane = lax.broadcasted_iota(jnp.int32, gram.shape, 1)
    before = lane == lax.rem(row + CAMS - 1, CAMS)
    total = jnp.sum(jnp.where(before, gram, 0.0), axis=1, keepdims=True)
    after = (row == lax.rem(lane + CAMS - 1, CAMS)) & (lane < CAMS)
    along = jnp.sum(jnp.where(after, gram, 0.0), axis=0, keepdims=True)
    down = jnp.sum(jnp.where(row == lane, along, 0.0), axis=1, keepdims=True)
    gram = jnp.where(before, down, gram)
    pixels = float(256 * 4096)
    average = total / pixels
    across = jnp.sum(jnp.where(row == lane, average, 0.0), axis=0, keepdims=True)
    covar = gram / pixels - average * across
    own = jnp.where(row == lane, covar, 0.0)
    down = jnp.sum(own, axis=1, keepdims=True) + VAR_EPS
    along = jnp.sum(own, axis=0, keepdims=True) + VAR_EPS
    return (covar / jnp.sqrt(down * along))[:, :CAMS]


def join(planes, join_ref, rows_ref):
    for tb in range(2):
        for ct in range(2):
            pair = [planes[2 * tb + odd][:, 128 * ct : 128 * ct + 128] for odd in range(2)]
            got = dot(three(jnp.concatenate(pair, axis=1)), join_ref[...])
            for part in range(2):
                one = got[:, 128 * part : 128 * part + 128].reshape(CAMS, HR, 128)
                rows_ref[2 * ct + part, :, pl.ds(tb, HR, stride=2), :] = one


def pack(photo_ref, cid_ref, perm_ref, edge_ref, block_ref, side_ref, beside_ref):
    beside_ref[:, 1, :, :, 0:128] = jnp.zeros((8, 2, OWN, 128), BF16)
    beside_ref[:, PH, :, :, 128:256] = jnp.zeros((8, 2, OWN, 128), BF16)

    def block(d, _):
        for ct in range(2):
            lane = pl.multiple_of(512 * d + 256 * ct, 256)
            x = photo_ref[:, :, pl.ds(lane, 256)].reshape(256, 256)
            y = dot(perm_ref[...], x).astype(BF16).reshape(2, HR, OWN, 256)
            for tb in range(2):
                lane = ct * 512 + tb * 256
                block_ref[d, :, :, lane : lane + 256] = y[tb]
                for i in range(HR):
                    g, j = divmod(i, 4)
                    if ct == 0:
                        beside_ref[2 * j + tb, d, g, :, 128:256] = y[tb, i, :, 0:128]
                    else:
                        beside_ref[2 * j + tb, d + 2, g, :, 0:128] = y[tb, i, :, 128:256]
        return 0

    lax.fori_loop(0, PH, block, 0)
    side = jnp.zeros((256, 128), F32)
    for jt in range(8):
        side += dot(beside_ref[jt, pl.ds(1, PH)].reshape(256, 256), edge_ref[jt])
    side_ref[:, pl.ds(0, 2)] = side.astype(BF16).reshape(PH, 2, OWN, 128)
    lane = lax.broadcasted_iota(jnp.int32, (OWN, 128), 1)
    ids = jnp.zeros((OWN, 128), jnp.int32)
    for n in range(OWN):
        ids = jnp.where(lax.rem(lane, OWN) == n, cid_ref[n], ids)
    ids = ids.astype(F32).astype(BF16)
    for d in range(PH):
        side_ref[d, 2] = ids


N_CONST = 8


def moved(me, k, sign):
    if isinstance(k, int):
        dy, dx = MOVES[k]
    else:
        dy, dx = 0, 0
        for n in range(1, PH):
            dy = jnp.where(k == n, MOVES[n][0], dy)
            dx = jnp.where(k == n, MOVES[n][1], dx)
    y, x = me // 2, lax.rem(me, 2)
    return lax.rem(y + 4 + sign * dy, 4) * 2 + lax.rem(x + dx, 2)


def fused_kernel(photo_ref, cid_ref, *rest):
    const_hbm, rest = rest[:N_CONST], rest[N_CONST:]
    fp_ref, sums_ref, block_ref, side_ref, beside_ref, x_ref, e_ref, rows_ref, a_ref, b_ref = rest[:10]
    consts, rest = rest[10 : 10 + N_CONST], rest[10 + N_CONST :]
    scratch, rest = rest[:9], rest[9:]
    acc_ref = scratch[-1]
    (const_sem, own_sem, send_sem, recv_sem, up_send, up_recv, dn_send, dn_recv,
     as_sem, ar_sem, bs_sem, br_sem) = rest
    me = lax.axis_index("photo")
    t = lax.axis_index("tile")

    def load(n):
        return pltpu.make_async_copy(const_hbm[n], consts[n], const_sem.at[n])

    for n in range(N_CONST):
        load(n).start()

    barrier = pltpu.get_barrier_semaphore()
    middle = t * (TI - 1 - t) // 56
    for k in range(1, PH):
        peer = lax.rem(me + k, PH)
        pl.semaphore_signal(barrier, inc=1, device_id={"photo": peer}, device_id_type=MESH)
    for k in range(1, TI):
        pl.semaphore_signal(
            barrier, inc=1, device_id={"tile": lax.rem(t + k, TI)}, device_id_type=MESH
        )

    for k in range(1, PH):
        where = {"photo": lax.rem(me + k, PH), "tile": lax.rem(t + TI // 2, TI)}
        pl.semaphore_signal(barrier, inc=1, device_id=where, device_id_type=MESH)

    @pl.when(middle == 1)
    def _():
        for k in range(1, PH):
            where = {"photo": lax.rem(me + k, PH), "tile": TI - 1 - t}
            pl.semaphore_signal(barrier, inc=1, device_id=where, device_id_type=MESH)

    load(0).wait()
    load(1).wait()
    pack(photo_ref, cid_ref, consts[0], consts[1], block_ref, side_ref, beside_ref)
    pl.semaphore_wait(barrier, 2 * PH + TI - 3 + (PH - 1) * middle)

    def remote(srcs, dsts, send, recv, k, where):
        return [
            pltpu.make_async_remote_copy(
                src_ref=a, dst_ref=b, send_sem=send.at[n, k], recv_sem=recv.at[n, k],
                device_id=where, device_id_type=MESH,
            )
            for n, (a, b) in enumerate(zip(srcs, dsts))
        ]

    def a2a(k):
        peer = moved(me, k, 1)
        return remote(
            (block_ref.at[peer], side_ref.at[peer]),
            (x_ref.at[me, pl.ds(4, HR)], e_ref.at[me, pl.ds(1, 3)]),
            send_sem, recv_sem, k, {"photo": peer},
        )

    def up(k, srcs, s, where):
        dsts = (x_ref.at[s, pl.ds(12, 4)], e_ref.at[s, 4])
        return remote(srcs, dsts, up_send, up_recv, k, where)

    def down(k, srcs, s, where):
        dsts = (x_ref.at[s, pl.ds(0, 4)], e_ref.at[s, 0])
        return remote(srcs, dsts, dn_send, dn_recv, k, where)

    def held(s, first):
        return (x_ref.at[s, pl.ds(4 if first else 8, 4)], e_ref.at[s, 1 if first else 2])

    def mine(d, first):
        return (block_ref.at[d, pl.ds(0 if first else 4, 4)], side_ref.at[d, 0 if first else 1])

    def each(copies, act):
        for copy in copies:
            getattr(copy, act)()

    def over_middle(k):
        peer = moved(me, k, 1)

        @pl.when(t == TI // 2 - 1)
        def _():
            each(down(k, mine(peer, False), me, {"photo": peer, "tile": t + 1}), "start")

        @pl.when(t == TI // 2)
        def _():
            each(up(k, mine(peer, True), me, {"photo": peer, "tile": t - 1}), "start")

    for k in ISSUE:
        each(a2a(k), "start")
    for k in range(PH):
        over_middle(k)

    def pass_on(k, source, s):
        @pl.when((t > 0) & (t != TI // 2))
        def _():
            each(up(k, source(s, True), s, {"tile": t - 1}), "start")

        @pl.when((t < TI - 1) & (t != TI // 2 - 1))
        def _():
            each(down(k, source(s, False), s, {"tile": t + 1}), "start")

    pass_on(0, mine, me)
    own = [
        pltpu.make_async_copy(block_ref.at[me], x_ref.at[me, pl.ds(4, HR)], own_sem.at[0]),
        pltpu.make_async_copy(side_ref.at[me], e_ref.at[me, pl.ds(1, 3)], own_sem.at[1]),
    ]
    each(own, "start")

    @pl.when(t == 0)
    def _():
        x_ref[:, pl.ds(0, 4)] = jnp.zeros((PH, 4, OWN, LANES), BF16)
        e_ref[:, 0] = jnp.zeros((PH, OWN, 128), BF16)

    @pl.when(t == TI - 1)
    def _():
        x_ref[:, pl.ds(12, 4)] = jnp.zeros((PH, 4, OWN, LANES), BF16)
        e_ref[:, 4] = jnp.zeros((PH, OWN, 128), BF16)

    acc_ref[...] = jnp.zeros(acc_ref.shape, F32)
    each(own, "wait")
    for n in range(2, N_CONST):
        load(n).wait()

    def step(k, _):
        s = moved(me, k, -1)

        @pl.when(k < PH - 1)
        def _():
            after = moved(me, k + 1, -1)
            each(a2a(k + 1), "wait_recv")
            pass_on(k + 1, held, after)

        @pl.when(t > 0)
        def _():
            each(down(k, held(s, False), s, {"tile": t - 1}), "wait_recv")

        @pl.when(t < TI - 1)
        def _():
            each(up(k, held(s, True), s, {"tile": t + 1}), "wait_recv")

        chunk(s, x_ref, e_ref, consts, scratch)
        return 0

    lax.fori_loop(0, PH, step, 0)

    place = lax.rem(t, 8)
    plane = me * 2 + t // 8

    def first(k):
        to = lax.rem(plane + k, 16)
        return pltpu.make_async_remote_copy(
            src_ref=a_ref.at[plane], dst_ref=a_ref.at[plane], send_sem=as_sem.at[k],
            recv_sem=ar_sem.at[k],
            device_id={"photo": to // 2, "tile": lax.rem(to, 2) * 8 + place},
            device_id_type=MESH,
        )

    def second(k):
        to = lax.rem(place + k, 8)
        return pltpu.make_async_remote_copy(
            src_ref=b_ref.at[place], dst_ref=b_ref.at[place], send_sem=bs_sem.at[k],
            recv_sem=br_sem.at[k],
            device_id={"tile": t // 8 * 8 + to}, device_id_type=MESH,
        )

    planes, sums = total_gram(acc_ref, consts[5])
    a_ref[plane] = sums
    for k in range(1, 16):
        first(k).start()
    join(planes, consts[4], rows_ref)
    out = [
        pltpu.make_async_copy(
            rows_ref.at[n], fp_ref.at[:, :, pl.ds(128 * n, 128)], own_sem.at[2 + n]
        )
        for n in range(4)
    ]
    each(out, "start")
    for k in range(1, 16):
        first(k).wait_recv()
    sums = a_ref[0]
    for n in range(1, 16):
        sums += a_ref[n]
    b_ref[place] = sums
    for k in range(1, 8):
        second(k).start()
    for k in range(1, 8):
        second(k).wait_recv()
    sums = b_ref[0]
    for n in range(1, 8):
        sums += b_ref[n]
    sums_ref[...] = sums

    each(out, "wait")
    for k in range(1, PH):
        each(a2a(k), "wait_send")
        second(k).wait_send()
    for k in range(1, 16):
        first(k).wait_send()
    for k in range(PH):
        s = moved(me, k, -1)

        @pl.when(t > 0)
        def _():
            each(up(k, held(s, True), s, {"tile": t - 1}), "wait_send")

        @pl.when(t < TI - 1)
        def _():
            each(down(k, held(s, False), s, {"tile": t + 1}), "wait_send")


SCRATCH = [
    ((3, 2 * HR, OWN, 256), F32),
    ((2 * HR, OWN, 128), F32),
    ((4, 3, HR, OWN, 512), BF16),
    ((4, HR, OWN, 256), BF16),
    ((4, 3, HR, OWN, 256), F32),
    ((4, 3, HR, OWN, 256), F32),
    ((4, 2 * HR, OWN, 256), F32),
    ((8, 256, 256), BF16),
    ((8, 256, 256), F32),
]


def fused(photos, camera_id, consts):
    vm = pl.BlockSpec(memory_space=pltpu.VMEM)
    anywhere = pl.BlockSpec(memory_space=pl.ANY)
    dma = pltpu.SemaphoreType.DMA
    return pl.pallas_call(
        fused_kernel,
        out_shape=(
            jax.ShapeDtypeStruct((CAMS, 16, 512), F32),
            jax.ShapeDtypeStruct((8, 128), F32),
        ),
        in_specs=[vm, pl.BlockSpec(memory_space=pltpu.SMEM)] + [anywhere] * N_CONST,
        out_specs=(anywhere, vm),
        scratch_shapes=[
            pltpu.VMEM((PH, HR, OWN, LANES), BF16),
            pltpu.VMEM((PH, 3, OWN, 128), BF16),
            pltpu.VMEM((8, PH + 2, 2, OWN, 256), BF16),
            pltpu.VMEM((PH, 2 * HR, OWN, LANES), BF16),
            pltpu.VMEM((PH, 5, OWN, 128), BF16),
            pltpu.VMEM((4, CAMS, 16, 128), F32),
            pltpu.VMEM((16, 8, 128), F32),
            pltpu.VMEM((8, 8, 128), F32),
        ]
        + [pltpu.VMEM(c.shape, c.dtype) for c in consts]
        + [pltpu.VMEM(s, d) for s, d in SCRATCH]
        + [dma((N_CONST,)), dma((6,))]
        + [dma((2, PH))] * 6
        + [dma((16,))] * 2
        + [dma((8,))] * 2,
        compiler_params=pltpu.CompilerParams(
            collective_id=0, has_side_effects=True, vmem_limit_bytes=VMEM_LIMIT
        ),
        name="fused",
    )(photos, camera_id, *consts)


def last_kernel(raw_ref, sums_ref, fp_ref, corr_ref):
    fp_ref[...] = raw_ref[...]

    @pl.when(pl.program_id(0) == 0)
    def _():
        corr_ref[...] = correlated(sums_ref[...])


def last(raw, sums):
    part = pl.BlockSpec((8, 16, 512), lambda n: (n, 0, 0))
    return pl.pallas_call(
        last_kernel,
        grid=(CAMS // 8,),
        out_shape=(
            jax.ShapeDtypeStruct((CAMS, 16, 512), F32),
            jax.ShapeDtypeStruct((CAMS, CAMS), F32),
        ),
        in_specs=[part, pl.BlockSpec((8, 128), lambda n: (0, 0))],
        out_specs=(part, pl.BlockSpec((CAMS, CAMS), lambda n: (0, 0))),
        name="last",
    )(raw, sums)


def on_device(photos, camera_id):
    return last(*fused(photos, camera_id, constants()))


def solution(mesh):
    return jax.shard_map(
        on_device,
        mesh=mesh,
        in_specs=(P("photo", "tile", None), P("photo")),
        out_specs=(P(None, "tile", "photo"), P()),
        check_vma=False,
    )
```

```python
import functools

import jax
import jax.numpy as jnp
import numpy as np
from jax import lax
from jax.experimental import pallas as pl
from jax.experimental.pallas import tpu as pltpu
from jax.sharding import PartitionSpec as P

MESH = pl.DeviceIdType.MESH
F32 = jnp.float32
BF16 = jnp.bfloat16

CAMS = 32
NOISE_POWER = 1.0
VAR_EPS = 1e-06

PH = 8
TI = 16
OWN = 16
HR = 8
LANES = 1024
VMEM_LIMIT = 60 * 1024 * 1024

MOVES = ((0, 0), (0, 1), (3, 0), (1, 0), (1, 1), (3, 1), (2, 0), (2, 1))
WAVES = ((1, 3, 2), (4, 6), (5,), (7,))
ROUTES = ((0, 1), (2, 4), (3, 5), (6, 7))


def constants():
    perm = np.zeros((256, 256), np.float32)
    for tb in range(2):
        for i in range(HR):
            for p in range(OWN):
                perm[(tb * HR + i) * OWN + p, p * 16 + 2 * i + tb] = 1.0
    edge = np.zeros((8, 256, 128), np.float32)
    for jt in range(8):
        for k in range(8):
            edge[jt, 120 + k, 16 * jt + k] = 1.0
            edge[jt, 128 + k, 16 * jt + 8 + k] = 1.0
    sign = np.array([[1, 1, 1], [1, -1, -1], [-1, 1, -1], [-1, -1, 1]], np.float32) * 0.5
    haar_edge = np.zeros((128, 512), np.float32)
    for j in range(4):
        for k in range(8):
            for b in range(3):
                for n in range(4):
                    at = 32 * j + 16 * (n // 2) + 2 * k + n % 2
                    haar_edge[at, 128 * j + 8 * b + k] = sign[n, b]
    split = np.zeros((256, 256), np.float32)
    for j in range(128):
        split[2 * j, j] = 0.5
        split[2 * j + 1, 128 + j] = 0.5
    out = np.arange(256)
    box = np.zeros((4, 512, 256), np.float32)
    box_edge = np.zeros((4, 3, 256, 256), np.float32)
    for r in range(1, 5):
        inner = (np.abs(out[:, None] - out[None, :]) <= r).astype(np.float32)
        box[r - 1] = np.concatenate([inner, inner])
        for b in range(3):
            side = np.zeros((128, 256), np.float32)
            for k in range(8):
                cell = k - 4 if k < 4 else 252 + k
                side[8 * b + k] = np.abs(cell - out) <= r
            box_edge[r - 1, b] = np.concatenate([side, side])
    join = np.concatenate([split.T] * 3)
    fold = np.zeros((256, 128), np.float32)
    fold[np.arange(256), np.arange(256) // HR] = 1.0
    fold = np.concatenate([fold] * 3)
    every = (perm, edge, haar_edge, split, join, fold, box, box_edge)
    return [jnp.asarray(c, BF16) for c in every]


def dot(a, b):
    return jnp.dot(a, b, preferred_element_type=F32)


def hi_lo(x):
    hi = x.astype(BF16)
    lo = (x - hi.astype(F32)).astype(BF16)
    return hi, lo


def bands_of(px_ref, n):
    a, b, c, d = (px_ref[j, n] for j in range(4))
    plus, minus, low_plus, low_minus = a + b, a - b, c + d, c - d
    return plus - low_plus, minus + low_minus, minus - low_minus


def chunk(s, x_ref, e_ref, consts, scratch):
    haar_edge_ref, split_ref, _, _, box_ref, box_edge_ref = consts[2:]
    sq_ref, eq_ref, lhs_ref, edge_ref, sum_ref, side_ref, px_ref, data_ref, acc_ref = scratch

    rows = 2 * HR
    for ct in range(2):
        for tb in range(2):
            lane = 512 * ct + 256 * tb
            x = x_ref[s, :, :, lane : lane + 256].reshape(rows * OWN, 256)
            got = dot(x, split_ref[...])
            for odd in range(2):
                px_ref[2 * tb + odd, :, :, 128 * ct : 128 * ct + 128] = got[
                    :, 128 * odd : 128 * odd + 128
                ].reshape(rows, OWN, 128)

    def squares(n, _):
        for b, band in enumerate(bands_of(px_ref, n)):
            sq_ref[b, n] = band * band
        return 0

    lax.fori_loop(0, rows, squares, 0, unroll=2)
    x = jnp.concatenate([e_ref[s, n] for n in (0, 1, 2, 4)])
    one = dot(x, haar_edge_ref[...])
    for n in range(rows):
        g, j = divmod(n, 4)
        part = one[OWN * g : OWN * g + OWN, 128 * j : 128 * j + 128]
        eq_ref[n] = part * part

    def sums(i, _):
        row = eq_ref[i + 4]
        for r in range(1, 5):
            row = row + eq_ref[i + 4 - r] + eq_ref[i + 4 + r]
            hi, lo = hi_lo(row)
            edge_ref[r - 1, i, :, 0:128] = hi
            edge_ref[r - 1, i, :, 128:256] = lo
        for b in range(3):
            row = sq_ref[b, i + 4]
            for r in range(1, 5):
                row = row + sq_ref[b, i + 4 - r] + sq_ref[b, i + 4 + r]
                hi, lo = hi_lo(row)
                lhs_ref[r - 1, b, i, :, 0:256] = hi
                lhs_ref[r - 1, b, i, :, 256:512] = lo
        return 0

    lax.fori_loop(0, HR, sums, 0)

    for r in range(4):
        got = dot(lhs_ref[r].reshape(3 * HR * OWN, 512), box_ref[r])
        sum_ref[r] = got.reshape(3, HR, OWN, 256)
        for b in range(3):
            got = dot(edge_ref[r].reshape(HR * OWN, 256), box_edge_ref[r, b])
            side_ref[r, b] = got.reshape(HR, OWN, 256)

    def residual(i, _):
        res = []
        for b, band in enumerate(bands_of(px_ref, i + 4)):
            var = None
            for r in range(4):
                mean = (sum_ref[r, b, i] + side_ref[r, b, i]) * (1.0 / (2 * r + 3) ** 2)
                var = mean if var is None else jnp.minimum(var, mean)
            gain = NOISE_POWER / jnp.maximum(var, NOISE_POWER)
            res.append(band * gain * 0.5)
        hz, vt, dg = res
        plus, minus = hz + vt, hz - vt
        noise = (plus + dg, minus - dg, -minus - dg, dg - plus)
        at = pl.multiple_of(i * OWN, OWN)
        for j in range(4):
            x = px_ref[j, i + 4]
            for part, value in enumerate((noise[j].astype(BF16).astype(F32) * x, x * x)):
                hi, lo = hi_lo(value)
                data_ref[2 * j + part, pl.ds(at, OWN), :] = hi
                data_ref[2 * j + part, pl.ds(HR * OWN + at, OWN), :] = lo
        return 0

    lax.fori_loop(0, HR, residual, 0)

    ids = e_ref[s, 3].astype(F32)[0:1, :]
    row = lax.broadcasted_iota(jnp.int32, (256, 128), 0)
    col = lax.broadcasted_iota(jnp.int32, (256, 128), 1)
    same = ((row // HR).astype(F32) == ids) & (lax.rem(row, HR) == col // OWN)
    pick = jnp.where(same, 1.0, 0.0).astype(BF16)
    pick = jnp.concatenate([pick, pick], axis=1)
    for j in range(8):
        acc_ref[j] += dot(pick, data_ref[j])


def three(x):
    hi = x.astype(BF16)
    rest = x - hi.astype(F32)
    mid = rest.astype(BF16)
    low = (rest - mid.astype(F32)).astype(BF16)
    return jnp.concatenate([hi, mid, low], axis=1)


def total_gram(acc_ref, fold_ref):
    planes = [acc_ref[2 * j] / acc_ref[2 * j + 1] for j in range(4)]
    gram = jnp.zeros((256, 256), F32)
    for plane in planes:
        hi, lo = hi_lo(plane)
        left = jnp.concatenate([hi, hi, lo], axis=1)
        right = jnp.concatenate([hi, lo, hi], axis=1)
        gram += lax.dot_general(left, right, (((1,), (1,)), ((), ())), preferred_element_type=F32)
    row = lax.broadcasted_iota(jnp.int32, (256, 256), 0)
    col = lax.broadcasted_iota(jnp.int32, (256, 256), 1)
    gram = jnp.where(lax.rem(row, HR) == lax.rem(col, HR), gram, 0.0)
    gram = gram.reshape(CAMS, HR, 256).sum(axis=1)
    gram = dot(three(gram), fold_ref[...]) * 0.25
    total = planes[0] + planes[1] + planes[2] + planes[3]
    total = total.reshape(CAMS, HR, 256).sum(axis=1).sum(axis=1, keepdims=True) * 0.5
    row = lax.broadcasted_iota(jnp.int32, (CAMS, 128), 0)
    lane = lax.broadcasted_iota(jnp.int32, (CAMS, 128), 1)
    gram = jnp.where(lane == lax.rem(row + CAMS - 1, CAMS), total, gram)
    lane = lax.broadcasted_iota(jnp.int32, (8, 128), 1)
    sums = gram[0:8]
    for q in range(1, 4):
        part = pltpu.roll(gram[8 * q : 8 * q + 8], 32 * q, 1)
        sums = jnp.where(lane // 32 == q, part, sums)
    return planes, sums


def correlated(sums):
    gram = jnp.concatenate([sums] + [pltpu.roll(sums, 128 - 32 * q, 1) for q in range(1, 4)])
    row = lax.broadcasted_iota(jnp.int32, gram.shape, 0)
    lane = lax.broadcasted_iota(jnp.int32, gram.shape, 1)
    before = lane == lax.rem(row + CAMS - 1, CAMS)
    total = jnp.sum(jnp.where(before, gram, 0.0), axis=1, keepdims=True)
    after = (row == lax.rem(lane + CAMS - 1, CAMS)) & (lane < CAMS)
    along = jnp.sum(jnp.where(after, gram, 0.0), axis=0, keepdims=True)
    down = jnp.sum(jnp.where(row == lane, along, 0.0), axis=1, keepdims=True)
    gram = jnp.where(before, down, gram)
    pixels = float(256 * 4096)
    average = total / pixels
    across = jnp.sum(jnp.where(row == lane, average, 0.0), axis=0, keepdims=True)
    covar = gram / pixels - average * across
    own = jnp.where(row == lane, covar, 0.0)
    down = jnp.sum(own, axis=1, keepdims=True) + VAR_EPS
    along = jnp.sum(own, axis=0, keepdims=True) + VAR_EPS
    return (covar / jnp.sqrt(down * along))[:, :CAMS]


def join(planes, join_ref, rows_ref):
    for tb in range(2):
        for ct in range(2):
            pair = [planes[2 * tb + odd][:, 128 * ct : 128 * ct + 128] for odd in range(2)]
            got = dot(three(jnp.concatenate(pair, axis=1)), join_ref[...])
            for part in range(2):
                one = got[:, 128 * part : 128 * part + 128].reshape(CAMS, HR, 128)
                rows_ref[2 * ct + part, :, pl.ds(tb, HR, stride=2), :] = one


def pack(photo_ref, cid_ref, perm_ref, edge_ref, block_ref, side_ref, beside_ref):
    beside_ref[:, 1, :, :, 0:128] = jnp.zeros((8, 2, OWN, 128), BF16)
    beside_ref[:, PH, :, :, 128:256] = jnp.zeros((8, 2, OWN, 128), BF16)

    def block(d, _):
        for ct in range(2):
            lane = pl.multiple_of(512 * d + 256 * ct, 256)
            x = photo_ref[:, :, pl.ds(lane, 256)].reshape(256, 256)
            y = dot(perm_ref[...], x).astype(BF16).reshape(2, HR, OWN, 256)
            for tb in range(2):
                lane = ct * 512 + tb * 256
                block_ref[d, :, :, lane : lane + 256] = y[tb]
                for i in range(HR):
                    g, j = divmod(i, 4)
                    if ct == 0:
                        beside_ref[2 * j + tb, d, g, :, 128:256] = y[tb, i, :, 0:128]
                    else:
                        beside_ref[2 * j + tb, d + 2, g, :, 0:128] = y[tb, i, :, 128:256]
        return 0

    lax.fori_loop(0, PH, block, 0)
    side = jnp.zeros((256, 128), F32)
    for jt in range(8):
        side += dot(beside_ref[jt, pl.ds(1, PH)].reshape(256, 256), edge_ref[jt])
    side_ref[:, pl.ds(0, 2)] = side.astype(BF16).reshape(PH, 2, OWN, 128)
    lane = lax.broadcasted_iota(jnp.int32, (OWN, 128), 1)
    ids = jnp.zeros((OWN, 128), jnp.int32)
    for n in range(OWN):
        ids = jnp.where(lax.rem(lane, OWN) == n, cid_ref[n], ids)
    ids = ids.astype(F32).astype(BF16)
    for d in range(PH):
        side_ref[d, 2] = ids


N_CONST = 8


def moved(me, k, sign):
    if isinstance(k, int):
        dy, dx = MOVES[k]
    else:
        dy, dx = 0, 0
        for n in range(1, PH):
            dy = jnp.where(k == n, MOVES[n][0], dy)
            dx = jnp.where(k == n, MOVES[n][1], dx)
    y, x = me // 2, lax.rem(me, 2)
    return lax.rem(y + 4 + sign * dy, 4) * 2 + lax.rem(x + dx, 2)


def fused_kernel(photo_ref, cid_ref, *rest):
    const_hbm, rest = rest[:N_CONST], rest[N_CONST:]
    fp_ref, sums_ref, block_ref, side_ref, beside_ref, x_ref, e_ref, rows_ref, a_ref, b_ref, by_ref, by_side_ref = rest[:12]
    consts, rest = rest[12 : 12 + N_CONST], rest[12 + N_CONST :]
    scratch, rest = rest[:9], rest[9:]
    acc_ref = scratch[-1]
    (const_sem, own_sem, send_sem, recv_sem, up_send, up_recv, dn_send, dn_recv,
     by_send, by_recv, as_sem, ar_sem, bs_sem, br_sem) = rest
    me = lax.axis_index("photo")
    t = lax.axis_index("tile")

    def load(n):
        return pltpu.make_async_copy(const_hbm[n], consts[n], const_sem.at[n])

    for n in range(N_CONST):
        load(n).start()

    barrier = pltpu.get_barrier_semaphore()
    middle = t * (TI - 1 - t) // 56
    half = t // (TI // 2)
    inward = t + half * (TI - 1 - 2 * t)
    relay = (1 - lax.rem(inward, 2)) * (1 - inward // 6)
    for k in range(1, PH):
        peer = lax.rem(me + k, PH)
        pl.semaphore_signal(barrier, inc=1, device_id={"photo": peer}, device_id_type=MESH)
    for k in range(1, TI):
        pl.semaphore_signal(
            barrier, inc=1, device_id={"tile": lax.rem(t + k, TI)}, device_id_type=MESH
        )

    for k in range(1, PH):
        where = {"photo": lax.rem(me + k, PH), "tile": lax.rem(t + TI // 2, TI)}
        pl.semaphore_signal(barrier, inc=1, device_id=where, device_id_type=MESH)

    @pl.when(middle == 1)
    def _():
        for k in range(1, PH):
            where = {"photo": lax.rem(me + k, PH), "tile": TI - 1 - t}
            pl.semaphore_signal(barrier, inc=1, device_id=where, device_id_type=MESH)
            for q in range(1, 4):
                where = {"photo": lax.rem(me + k, PH), "tile": (1 - half) * (9 + 2 * q) + half * (6 - 2 * q)}
                pl.semaphore_signal(barrier, inc=1, device_id=where, device_id_type=MESH)

    @pl.when(relay == 1)
    def _():
        for k in range(1, PH):
            where = {"photo": lax.rem(me + k, PH), "tile": TI // 2 - half}
            pl.semaphore_signal(barrier, inc=1, device_id=where, device_id_type=MESH)

    load(0).wait()
    load(1).wait()
    pack(photo_ref, cid_ref, consts[0], consts[1], block_ref, side_ref, beside_ref)
    pl.semaphore_wait(barrier, 2 * PH + TI - 3 + (PH - 1) * (4 * middle + relay))

    def remote(srcs, dsts, send, k, recv, j, where):
        return [
            pltpu.make_async_remote_copy(
                src_ref=a, dst_ref=b, send_sem=send.at[n, k], recv_sem=recv.at[n, j],
                device_id=where, device_id_type=MESH,
            )
            for n, (a, b) in enumerate(zip(srcs, dsts))
        ]

    def a2a(k):
        peer = moved(me, k, 1)
        return remote(
            (block_ref.at[peer], side_ref.at[peer]),
            (x_ref.at[me, pl.ds(4, HR)], e_ref.at[me, pl.ds(1, 3)]),
            send_sem, k, recv_sem, k, {"photo": peer},
        )

    def up(k, srcs, s, where):
        dsts = (x_ref.at[s, pl.ds(12, 4)], e_ref.at[s, 4])
        return remote(srcs, dsts, up_send, k, up_recv, k, where)

    def down(k, srcs, s, where):
        dsts = (x_ref.at[s, pl.ds(0, 4)], e_ref.at[s, 0])
        return remote(srcs, dsts, dn_send, k, dn_recv, k, where)

    def held(s, first):
        return (x_ref.at[s, pl.ds(4 if first else 8, 4)], e_ref.at[s, 1 if first else 2])

    def mine(d, first):
        return (block_ref.at[d, pl.ds(0 if first else 4, 4)], side_ref.at[d, 0 if first else 1])

    def each(copies, act):
        for copy in copies:
            getattr(copy, act)()

    def over_middle(first):
        act = up if first else down
        for q in range(4):
            for j, k in enumerate(ROUTES[q]):
                peer = moved(me, k, 1)
                if q == 0:
                    where = {"photo": peer, "tile": TI // 2 - 1 if first else TI // 2}
                    copies = act(k, mine(peer, first), me, where)
                else:
                    copies = remote(
                        mine(peer, first), (by_ref.at[j], by_side_ref.at[j]),
                        up_send if first else dn_send, k, by_recv, j,
                        {"tile": 9 + 2 * q if first else 6 - 2 * q},
                    )
                each(copies, "start")

    def relayed(q, j, first):
        k = ROUTES[q][j]
        if first:
            dsts, recv = (x_ref.at[me, pl.ds(12, 4)], e_ref.at[me, 4]), up_recv
        else:
            dsts, recv = (x_ref.at[me, pl.ds(0, 4)], e_ref.at[me, 0]), dn_recv
        where = {"photo": moved(me, k, 1), "tile": TI // 2 - 1 if first else TI // 2}
        return remote((by_ref.at[j], by_side_ref.at[j]), dsts, by_send, j, recv, k, where)

    def relays(act):
        for q in range(1, 4):
            for first in (False, True):

                @pl.when(t == (9 + 2 * q if first else 6 - 2 * q))
                def _():
                    for j in range(2):
                        act(q, j, first)

    def forward(q, j, first):
        landed = remote(
            mine(me, first), (by_ref.at[j], by_side_ref.at[j]), by_send, j, by_recv, j,
            {"tile": TI // 2 if first else TI // 2 - 1},
        )
        each(landed, "wait_recv")
        each(relayed(q, j, first), "start")

    @pl.when(t == TI // 2 - 1)
    def _():
        over_middle(False)

    @pl.when(t == TI // 2)
    def _():
        over_middle(True)

    for k in WAVES[0]:
        each(a2a(k), "start")

    def pass_on(k, source, s):
        @pl.when((t > 0) & (t != TI // 2))
        def _():
            each(up(k, source(s, True), s, {"tile": t - 1}), "start")

        @pl.when((t < TI - 1) & (t != TI // 2 - 1))
        def _():
            each(down(k, source(s, False), s, {"tile": t + 1}), "start")

    pass_on(0, mine, me)
    own = [
        pltpu.make_async_copy(block_ref.at[me], x_ref.at[me, pl.ds(4, HR)], own_sem.at[0]),
        pltpu.make_async_copy(side_ref.at[me], e_ref.at[me, pl.ds(1, 3)], own_sem.at[1]),
    ]
    each(own, "start")

    @pl.when(t == 0)
    def _():
        x_ref[:, pl.ds(0, 4)] = jnp.zeros((PH, 4, OWN, LANES), BF16)
        e_ref[:, 0] = jnp.zeros((PH, OWN, 128), BF16)

    @pl.when(t == TI - 1)
    def _():
        x_ref[:, pl.ds(12, 4)] = jnp.zeros((PH, 4, OWN, LANES), BF16)
        e_ref[:, 4] = jnp.zeros((PH, OWN, 128), BF16)

    acc_ref[...] = jnp.zeros(acc_ref.shape, F32)
    each(own, "wait")
    for n in range(2, N_CONST):
        load(n).wait()

    def step(k, _):
        s = moved(me, k, -1)

        def ahead():
            each(a2a(k + 1), "wait_recv")
            pass_on(k + 1, held, moved(me, k + 1, -1))

        @pl.when((k > 0) & (k < PH - 1))
        def _():
            ahead()

        @pl.when(t > 0)
        def _():
            each(down(k, held(s, False), s, {"tile": t - 1}), "wait_recv")

        @pl.when(t < TI - 1)
        def _():
            each(up(k, held(s, True), s, {"tile": t + 1}), "wait_recv")

        chunk(s, x_ref, e_ref, consts, scratch)

        @pl.when(k == 0)
        def _():
            relays(forward)

        for n in range(1, 4):

            @pl.when(k == n - 1)
            def _():
                for j in WAVES[n]:
                    each(a2a(j), "start")

        @pl.when(k == 0)
        def _():
            ahead()

        return 0

    lax.fori_loop(0, PH, step, 0)

    place = lax.rem(t, 8)
    plane = me * 2 + t // 8

    def first(k):
        to = lax.rem(plane + k, 16)
        return pltpu.make_async_remote_copy(
            src_ref=a_ref.at[plane], dst_ref=a_ref.at[plane], send_sem=as_sem.at[k],
            recv_sem=ar_sem.at[k],
            device_id={"photo": to // 2, "tile": lax.rem(to, 2) * 8 + place},
            device_id_type=MESH,
        )

    def second(k):
        to = lax.rem(place + k, 8)
        return pltpu.make_async_remote_copy(
            src_ref=b_ref.at[place], dst_ref=b_ref.at[place], send_sem=bs_sem.at[k],
            recv_sem=br_sem.at[k],
            device_id={"tile": t // 8 * 8 + to}, device_id_type=MESH,
        )

    planes, sums = total_gram(acc_ref, consts[5])
    a_ref[plane] = sums
    for k in range(1, 16):
        first(k).start()
    join(planes, consts[4], rows_ref)
    out = [
        pltpu.make_async_copy(
            rows_ref.at[n], fp_ref.at[:, :, pl.ds(128 * n, 128)], own_sem.at[2 + n]
        )
        for n in range(4)
    ]
    each(out, "start")
    for k in range(1, 16):
        first(k).wait_recv()
    sums = a_ref[0]
    for n in range(1, 16):
        sums += a_ref[n]
    b_ref[place] = sums
    for k in range(1, 8):
        second(k).start()
    for k in range(1, 8):
        second(k).wait_recv()
    sums = b_ref[0]
    for n in range(1, 8):
        sums += b_ref[n]
    sums_ref[...] = sums

    each(out, "wait")
    relays(lambda q, j, first: each(relayed(q, j, first), "wait_send"))
    for k in range(1, PH):
        each(a2a(k), "wait_send")
        second(k).wait_send()
    for k in range(1, 16):
        first(k).wait_send()
    for k in range(PH):
        s = moved(me, k, -1)

        @pl.when(t > 0)
        def _():
            each(up(k, held(s, True), s, {"tile": t - 1}), "wait_send")

        @pl.when(t < TI - 1)
        def _():
            each(down(k, held(s, False), s, {"tile": t + 1}), "wait_send")


SCRATCH = [
    ((3, 2 * HR, OWN, 256), F32),
    ((2 * HR, OWN, 128), F32),
    ((4, 3, HR, OWN, 512), BF16),
    ((4, HR, OWN, 256), BF16),
    ((4, 3, HR, OWN, 256), F32),
    ((4, 3, HR, OWN, 256), F32),
    ((4, 2 * HR, OWN, 256), F32),
    ((8, 256, 256), BF16),
    ((8, 256, 256), F32),
]


def fused(photos, camera_id, consts):
    vm = pl.BlockSpec(memory_space=pltpu.VMEM)
    anywhere = pl.BlockSpec(memory_space=pl.ANY)
    dma = pltpu.SemaphoreType.DMA
    return pl.pallas_call(
        fused_kernel,
        out_shape=(
            jax.ShapeDtypeStruct((CAMS, 16, 512), F32),
            jax.ShapeDtypeStruct((8, 128), F32),
        ),
        in_specs=[vm, pl.BlockSpec(memory_space=pltpu.SMEM)] + [anywhere] * N_CONST,
        out_specs=(anywhere, vm),
        scratch_shapes=[
            pltpu.VMEM((PH, HR, OWN, LANES), BF16),
            pltpu.VMEM((PH, 3, OWN, 128), BF16),
            pltpu.VMEM((8, PH + 2, 2, OWN, 256), BF16),
            pltpu.VMEM((PH, 2 * HR, OWN, LANES), BF16),
            pltpu.VMEM((PH, 5, OWN, 128), BF16),
            pltpu.VMEM((4, CAMS, 16, 128), F32),
            pltpu.VMEM((16, 8, 128), F32),
            pltpu.VMEM((8, 8, 128), F32),
            pltpu.VMEM((2, 4, OWN, LANES), BF16),
            pltpu.VMEM((2, OWN, 128), BF16),
        ]
        + [pltpu.VMEM(c.shape, c.dtype) for c in consts]
        + [pltpu.VMEM(s, d) for s, d in SCRATCH]
        + [dma((N_CONST,)), dma((6,))]
        + [dma((2, PH))] * 6
        + [dma((2, 2))] * 2
        + [dma((16,))] * 2
        + [dma((8,))] * 2,
        compiler_params=pltpu.CompilerParams(
            collective_id=0, has_side_effects=True, vmem_limit_bytes=VMEM_LIMIT
        ),
        name="fused",
    )(photos, camera_id, *consts)


def last_kernel(raw_ref, sums_ref, fp_ref, corr_ref, held_ref, in_sem, out_sem):
    parts = 4
    rows = CAMS // parts
    into = [
        pltpu.make_async_copy(raw_ref.at[pl.ds(rows * n, rows)], held_ref.at[n], in_sem.at[n])
        for n in range(parts)
    ]
    back = [
        pltpu.make_async_copy(held_ref.at[n], fp_ref.at[pl.ds(rows * n, rows)], out_sem.at[n])
        for n in range(parts)
    ]
    for copy in into:
        copy.start()
    corr_ref[...] = correlated(sums_ref[...])
    for n in range(parts):
        into[n].wait()
        back[n].start()
    for copy in back:
        copy.wait()


def last(raw, sums):
    vm = pl.BlockSpec(memory_space=pltpu.VMEM)
    anywhere = pl.BlockSpec(memory_space=pl.ANY)
    return pl.pallas_call(
        last_kernel,
        out_shape=(
            jax.ShapeDtypeStruct((CAMS, 16, 512), F32),
            jax.ShapeDtypeStruct((CAMS, CAMS), F32),
        ),
        in_specs=[anywhere, vm],
        out_specs=(anywhere, vm),
        scratch_shapes=[
            pltpu.VMEM((4, CAMS // 4, 16, 512), F32),
            pltpu.SemaphoreType.DMA((4,)),
            pltpu.SemaphoreType.DMA((4,)),
        ],
        name="last",
    )(raw, sums)


def on_device(photos, camera_id):
    return last(*fused(photos, camera_id, constants()))


def solution(mesh):
    return jax.shard_map(
        on_device,
        mesh=mesh,
        in_specs=(P("photo", "tile", None), P("photo")),
        out_specs=(P(None, "tile", "photo"), P()),
        check_vma=False,
    )
```

```python
import functools

import jax
import jax.numpy as jnp
import numpy as np
from jax import lax
from jax.experimental import pallas as pl
from jax.experimental.pallas import tpu as pltpu
from jax.sharding import PartitionSpec as P

MESH = pl.DeviceIdType.MESH
F32 = jnp.float32
BF16 = jnp.bfloat16

CAMS = 32
NOISE_POWER = 1.0
VAR_EPS = 1e-06

PH = 8
TI = 16
OWN = 16
HR = 8
LANES = 1024
VMEM_LIMIT = 60 * 1024 * 1024

MOVES = ((0, 0), (0, 1), (3, 0), (1, 0), (1, 1), (3, 1), (2, 0), (2, 1))
WAVES = ((1, 3, 2), (4, 6), (5,), (7,))
ROUTES = ((0, 1), (2, 4), (3, 5), (6, 7))


def constants():
    perm = np.zeros((256, 256), np.float32)
    for tb in range(2):
        for i in range(HR):
            for p in range(OWN):
                perm[(tb * HR + i) * OWN + p, p * 16 + 2 * i + tb] = 1.0
    edge = np.zeros((8, 256, 128), np.float32)
    for jt in range(8):
        for k in range(8):
            edge[jt, 120 + k, 16 * jt + k] = 1.0
            edge[jt, 128 + k, 16 * jt + 8 + k] = 1.0
    sign = np.array([[1, 1, 1], [1, -1, -1], [-1, 1, -1], [-1, -1, 1]], np.float32) * 0.5
    haar_edge = np.zeros((128, 512), np.float32)
    for j in range(4):
        for k in range(8):
            for b in range(3):
                for n in range(4):
                    at = 32 * j + 16 * (n // 2) + 2 * k + n % 2
                    haar_edge[at, 128 * j + 8 * b + k] = sign[n, b]
    split = np.zeros((256, 256), np.float32)
    for j in range(128):
        split[2 * j, j] = 0.5
        split[2 * j + 1, 128 + j] = 0.5
    out = np.arange(256)
    box = np.zeros((4, 256, 256), np.float32)
    box_edge = np.zeros((4, 3, 128, 256), np.float32)
    for r in range(1, 5):
        inner = (np.abs(out[:, None] - out[None, :]) <= r).astype(np.float32)
        box[r - 1] = inner
        for b in range(3):
            side = np.zeros((128, 256), np.float32)
            for k in range(8):
                cell = k - 4 if k < 4 else 252 + k
                side[8 * b + k] = np.abs(cell - out) <= r
            box_edge[r - 1, b] = side
    join = np.concatenate([split.T] * 3)
    fold = np.zeros((256, 128), np.float32)
    fold[np.arange(256), np.arange(256) // HR] = 1.0
    fold = np.concatenate([fold] * 3)
    every = (perm, edge, haar_edge, split, join, fold, box, box_edge)
    return [jnp.asarray(c, BF16) for c in every]


def dot(a, b):
    return jnp.dot(a, b, preferred_element_type=F32)


def hi_lo(x):
    hi = x.astype(BF16)
    lo = (x - hi.astype(F32)).astype(BF16)
    return hi, lo


def bands_of(px_ref, n):
    a, b, c, d = (px_ref[j, n] for j in range(4))
    plus, minus, low_plus, low_minus = a + b, a - b, c + d, c - d
    return plus - low_plus, minus + low_minus, minus - low_minus


def chunk(s, x_ref, e_ref, consts, scratch):
    haar_edge_ref, split_ref, _, _, box_ref, box_edge_ref = consts[2:]
    sq_ref, eq_ref, lhs_ref, edge_ref, sum_ref, side_ref, px_ref, data_ref, acc_ref = scratch

    rows = 2 * HR
    for ct in range(2):
        for tb in range(2):
            lane = 512 * ct + 256 * tb
            x = x_ref[s, :, :, lane : lane + 256].reshape(rows * OWN, 256)
            got = dot(x, split_ref[...])
            for odd in range(2):
                px_ref[2 * tb + odd, :, :, 128 * ct : 128 * ct + 128] = got[
                    :, 128 * odd : 128 * odd + 128
                ].reshape(rows, OWN, 128)

    def squares(n, _):
        for b, band in enumerate(bands_of(px_ref, n)):
            sq_ref[b, n] = band * band
        return 0

    lax.fori_loop(0, rows, squares, 0, unroll=2)
    x = jnp.concatenate([e_ref[s, n] for n in (0, 1, 2, 4)])
    one = dot(x, haar_edge_ref[...])
    for n in range(rows):
        g, j = divmod(n, 4)
        part = one[OWN * g : OWN * g + OWN, 128 * j : 128 * j + 128]
        eq_ref[n] = part * part

    def sums(i, _):
        row = eq_ref[i + 4]
        for r in range(1, 5):
            row = row + eq_ref[i + 4 - r] + eq_ref[i + 4 + r]
            hi, lo = hi_lo(row)
            edge_ref[r - 1, i, :, 0:128] = hi
            edge_ref[r - 1, i, :, 128:256] = lo
        for b in range(3):
            row = sq_ref[b, i + 4]
            for r in range(1, 5):
                row = row + sq_ref[b, i + 4 - r] + sq_ref[b, i + 4 + r]
                hi, lo = hi_lo(row)
                lhs_ref[r - 1, b, i, :, 0:256] = hi
                lhs_ref[r - 1, b, i, :, 256:512] = lo
        return 0

    lax.fori_loop(0, HR, sums, 0)

    for r in range(4):
        got = dot(lhs_ref[r].reshape(3 * HR * OWN, 512), box_ref[r])
        sum_ref[r] = got.reshape(3, HR, OWN, 256)
        for b in range(3):
            got = dot(edge_ref[r].reshape(HR * OWN, 256), box_edge_ref[r, b])
            side_ref[r, b] = got.reshape(HR, OWN, 256)

    def residual(i, _):
        res = []
        for b, band in enumerate(bands_of(px_ref, i + 4)):
            var = None
            for r in range(4):
                mean = (sum_ref[r, b, i] + side_ref[r, b, i]) * (1.0 / (2 * r + 3) ** 2)
                var = mean if var is None else jnp.minimum(var, mean)
            gain = NOISE_POWER / jnp.maximum(var, NOISE_POWER)
            res.append(band * gain * 0.5)
        hz, vt, dg = res
        plus, minus = hz + vt, hz - vt
        noise = (plus + dg, minus - dg, -minus - dg, dg - plus)
        at = pl.multiple_of(i * OWN, OWN)
        for j in range(4):
            x = px_ref[j, i + 4]
            for part, value in enumerate((noise[j].astype(BF16).astype(F32) * x, x * x)):
                hi, lo = hi_lo(value)
                data_ref[2 * j + part, pl.ds(at, OWN), :] = hi
                data_ref[2 * j + part, pl.ds(HR * OWN + at, OWN), :] = lo
        return 0

    lax.fori_loop(0, HR, residual, 0)

    ids = e_ref[s, 3].astype(F32)[0:1, :]
    row = lax.broadcasted_iota(jnp.int32, (256, 128), 0)
    col = lax.broadcasted_iota(jnp.int32, (256, 128), 1)
    same = ((row // HR).astype(F32) == ids) & (lax.rem(row, HR) == col // OWN)
    pick = jnp.where(same, 1.0, 0.0).astype(BF16)
    pick = jnp.concatenate([pick, pick], axis=1)
    for j in range(8):
        acc_ref[j] += dot(pick, data_ref[j])


def three(x):
    hi = x.astype(BF16)
    rest = x - hi.astype(F32)
    mid = rest.astype(BF16)
    low = (rest - mid.astype(F32)).astype(BF16)
    return jnp.concatenate([hi, mid, low], axis=1)


def total_gram(acc_ref, fold_ref):
    planes = [acc_ref[2 * j] / acc_ref[2 * j + 1] for j in range(4)]
    gram = jnp.zeros((256, 256), F32)
    for plane in planes:
        hi, lo = hi_lo(plane)
        left = jnp.concatenate([hi, hi, lo], axis=1)
        right = jnp.concatenate([hi, lo, hi], axis=1)
        gram += lax.dot_general(left, right, (((1,), (1,)), ((), ())), preferred_element_type=F32)
    row = lax.broadcasted_iota(jnp.int32, (256, 256), 0)
    col = lax.broadcasted_iota(jnp.int32, (256, 256), 1)
    gram = jnp.where(lax.rem(row, HR) == lax.rem(col, HR), gram, 0.0)
    gram = gram.reshape(CAMS, HR, 256).sum(axis=1)
    gram = dot(three(gram), fold_ref[...]) * 0.25
    total = planes[0] + planes[1] + planes[2] + planes[3]
    total = total.reshape(CAMS, HR, 256).sum(axis=1).sum(axis=1, keepdims=True) * 0.5
    row = lax.broadcasted_iota(jnp.int32, (CAMS, 128), 0)
    lane = lax.broadcasted_iota(jnp.int32, (CAMS, 128), 1)
    gram = jnp.where(lane == lax.rem(row + CAMS - 1, CAMS), total, gram)
    lane = lax.broadcasted_iota(jnp.int32, (8, 128), 1)
    sums = gram[0:8]
    for q in range(1, 4):
        part = pltpu.roll(gram[8 * q : 8 * q + 8], 32 * q, 1)
        sums = jnp.where(lane // 32 == q, part, sums)
    return planes, sums


def correlated(sums):
    gram = jnp.concatenate([sums] + [pltpu.roll(sums, 128 - 32 * q, 1) for q in range(1, 4)])
    row = lax.broadcasted_iota(jnp.int32, gram.shape, 0)
    lane = lax.broadcasted_iota(jnp.int32, gram.shape, 1)
    before = lane == lax.rem(row + CAMS - 1, CAMS)
    total = jnp.sum(jnp.where(before, gram, 0.0), axis=1, keepdims=True)
    after = (row == lax.rem(lane + CAMS - 1, CAMS)) & (lane < CAMS)
    along = jnp.sum(jnp.where(after, gram, 0.0), axis=0, keepdims=True)
    down = jnp.sum(jnp.where(row == lane, along, 0.0), axis=1, keepdims=True)
    gram = jnp.where(before, down, gram)
    pixels = float(256 * 4096)
    average = total / pixels
    across = jnp.sum(jnp.where(row == lane, average, 0.0), axis=0, keepdims=True)
    covar = gram / pixels - average * across
    own = jnp.where(row == lane, covar, 0.0)
    down = jnp.sum(own, axis=1, keepdims=True) + VAR_EPS
    along = jnp.sum(own, axis=0, keepdims=True) + VAR_EPS
    return (covar / jnp.sqrt(down * along))[:, :CAMS]


def join(planes, join_ref, rows_ref):
    for tb in range(2):
        for ct in range(2):
            pair = [planes[2 * tb + odd][:, 128 * ct : 128 * ct + 128] for odd in range(2)]
            got = dot(three(jnp.concatenate(pair, axis=1)), join_ref[...])
            for part in range(2):
                one = got[:, 128 * part : 128 * part + 128].reshape(CAMS, HR, 128)
                rows_ref[2 * ct + part, :, pl.ds(tb, HR, stride=2), :] = one


def pack(fetch, photo_ref, cid_ref, perm_ref, edge_ref, block_ref, side_ref, beside_ref):
    beside_ref[:, 1, :, :, 0:128] = jnp.zeros((8, 2, OWN, 128), BF16)
    beside_ref[:, PH, :, :, 128:256] = jnp.zeros((8, 2, OWN, 128), BF16)

    def block(d, _):
        fetch(d).wait()
        for ct in range(2):
            lane = pl.multiple_of(512 * d + 256 * ct, 256)
            x = photo_ref[:, :, pl.ds(lane, 256)].reshape(256, 256)
            y = dot(perm_ref[...], x).astype(BF16).reshape(2, HR, OWN, 256)
            for tb in range(2):
                lane = ct * 512 + tb * 256
                block_ref[d, :, :, lane : lane + 256] = y[tb]
                for i in range(HR):
                    g, j = divmod(i, 4)
                    if ct == 0:
                        beside_ref[2 * j + tb, d, g, :, 128:256] = y[tb, i, :, 0:128]
                    else:
                        beside_ref[2 * j + tb, d + 2, g, :, 0:128] = y[tb, i, :, 128:256]
        return 0

    lax.fori_loop(0, PH, block, 0)
    side = jnp.zeros((256, 128), F32)
    for jt in range(8):
        side += dot(beside_ref[jt, pl.ds(1, PH)].reshape(256, 256), edge_ref[jt])
    side_ref[:, pl.ds(0, 2)] = side.astype(BF16).reshape(PH, 2, OWN, 128)
    lane = lax.broadcasted_iota(jnp.int32, (OWN, 128), 1)
    ids = jnp.zeros((OWN, 128), jnp.int32)
    for n in range(OWN):
        ids = jnp.where(lax.rem(lane, OWN) == n, cid_ref[n], ids)
    ids = ids.astype(F32).astype(BF16)
    for d in range(PH):
        side_ref[d, 2] = ids


N_CONST = 8


def moved(me, k, sign):
    if isinstance(k, int):
        dy, dx = MOVES[k]
    else:
        dy, dx = 0, 0
        for n in range(1, PH):
            dy = jnp.where(k == n, MOVES[n][0], dy)
            dx = jnp.where(k == n, MOVES[n][1], dx)
    y, x = me // 2, lax.rem(me, 2)
    return lax.rem(y + 4 + sign * dy, 4) * 2 + lax.rem(x + dx, 2)


def fused_kernel(photo_hbm, cid_ref, *rest):
    const_hbm, rest = rest[:N_CONST], rest[N_CONST:]
    fp_ref, sums_ref, block_ref, side_ref, beside_ref, x_ref, e_ref, rows_ref, a_ref, b_ref, by_ref, by_side_ref, photo_ref = rest[:13]
    consts, rest = rest[13 : 13 + N_CONST], rest[13 + N_CONST :]
    scratch, rest = rest[:9], rest[9:]
    acc_ref = scratch[-1]
    (photo_sem, const_sem, own_sem, send_sem, recv_sem, up_send, up_recv, dn_send, dn_recv,
     by_send, by_recv, as_sem, ar_sem, bs_sem, br_sem) = rest
    me = lax.axis_index("photo")
    t = lax.axis_index("tile")

    def load(n):
        if n < N_CONST - 2:
            return [pltpu.make_async_copy(const_hbm[n], consts[n], const_sem.at[n, 0])]
        depth = consts[n].shape[-2] // 2
        lead = (slice(None),) * (len(consts[n].shape) - 2)
        return [
            pltpu.make_async_copy(
                const_hbm[n], consts[n].at[(*lead, pl.ds(depth * part, depth))], const_sem.at[n, part]
            )
            for part in range(2)
        ]

    def fetch(d):
        lanes = pl.ds(pl.multiple_of(512 * d, 512), 512)
        return pltpu.make_async_copy(
            photo_hbm.at[:, :, lanes], photo_ref.at[:, :, lanes], photo_sem.at[d]
        )

    def each(copies, act):
        for copy in copies:
            getattr(copy, act)()

    for d in range(PH):
        fetch(d).start()
    for n in range(N_CONST):
        each(load(n), "start")

    barrier = pltpu.get_barrier_semaphore()
    middle = t * (TI - 1 - t) // 56
    half = t // (TI // 2)
    inward = t + half * (TI - 1 - 2 * t)
    relay = (1 - lax.rem(inward, 2)) * (1 - inward // 6)
    for k in range(1, PH):
        peer = lax.rem(me + k, PH)
        pl.semaphore_signal(barrier, inc=1, device_id={"photo": peer}, device_id_type=MESH)
    for k in range(1, TI):
        pl.semaphore_signal(
            barrier, inc=1, device_id={"tile": lax.rem(t + k, TI)}, device_id_type=MESH
        )

    for k in range(1, PH):
        where = {"photo": lax.rem(me + k, PH), "tile": lax.rem(t + TI // 2, TI)}
        pl.semaphore_signal(barrier, inc=1, device_id=where, device_id_type=MESH)

    @pl.when(middle == 1)
    def _():
        for k in range(1, PH):
            where = {"photo": lax.rem(me + k, PH), "tile": TI - 1 - t}
            pl.semaphore_signal(barrier, inc=1, device_id=where, device_id_type=MESH)
            for q in range(1, 4):
                where = {"photo": lax.rem(me + k, PH), "tile": (1 - half) * (9 + 2 * q) + half * (6 - 2 * q)}
                pl.semaphore_signal(barrier, inc=1, device_id=where, device_id_type=MESH)

    @pl.when(relay == 1)
    def _():
        for k in range(1, PH):
            where = {"photo": lax.rem(me + k, PH), "tile": TI // 2 - half}
            pl.semaphore_signal(barrier, inc=1, device_id=where, device_id_type=MESH)

    each(load(0), "wait")
    each(load(1), "wait")
    pack(fetch, photo_ref, cid_ref, consts[0], consts[1], block_ref, side_ref, beside_ref)
    pl.semaphore_wait(barrier, 2 * PH + TI - 3 + (PH - 1) * (4 * middle + relay))

    def remote(srcs, dsts, send, k, recv, j, where):
        return [
            pltpu.make_async_remote_copy(
                src_ref=a, dst_ref=b, send_sem=send.at[n, k], recv_sem=recv.at[n, j],
                device_id=where, device_id_type=MESH,
            )
            for n, (a, b) in enumerate(zip(srcs, dsts))
        ]

    def a2a(k):
        peer = moved(me, k, 1)
        return remote(
            (block_ref.at[peer], side_ref.at[peer]),
            (x_ref.at[me, pl.ds(4, HR)], e_ref.at[me, pl.ds(1, 3)]),
            send_sem, k, recv_sem, k, {"photo": peer},
        )

    def up(k, srcs, s, where):
        dsts = (x_ref.at[s, pl.ds(12, 4)], e_ref.at[s, 4])
        return remote(srcs, dsts, up_send, k, up_recv, k, where)

    def down(k, srcs, s, where):
        dsts = (x_ref.at[s, pl.ds(0, 4)], e_ref.at[s, 0])
        return remote(srcs, dsts, dn_send, k, dn_recv, k, where)

    def held(s, first):
        return (x_ref.at[s, pl.ds(4 if first else 8, 4)], e_ref.at[s, 1 if first else 2])

    def mine(d, first):
        return (block_ref.at[d, pl.ds(0 if first else 4, 4)], side_ref.at[d, 0 if first else 1])

    def over_middle(first):
        act = up if first else down
        for q in range(4):
            for j, k in enumerate(ROUTES[q]):
                peer = moved(me, k, 1)
                if q == 0:
                    where = {"photo": peer, "tile": TI // 2 - 1 if first else TI // 2}
                    copies = act(k, mine(peer, first), me, where)
                else:
                    copies = remote(
                        mine(peer, first), (by_ref.at[j], by_side_ref.at[j]),
                        up_send if first else dn_send, k, by_recv, j,
                        {"tile": 9 + 2 * q if first else 6 - 2 * q},
                    )
                each(copies, "start")

    def relayed(q, j, first):
        k = ROUTES[q][j]
        if first:
            dsts, recv = (x_ref.at[me, pl.ds(12, 4)], e_ref.at[me, 4]), up_recv
        else:
            dsts, recv = (x_ref.at[me, pl.ds(0, 4)], e_ref.at[me, 0]), dn_recv
        where = {"photo": moved(me, k, 1), "tile": TI // 2 - 1 if first else TI // 2}
        return remote((by_ref.at[j], by_side_ref.at[j]), dsts, by_send, j, recv, k, where)

    def relays(act):
        for q in range(1, 4):
            for first in (False, True):

                @pl.when(t == (9 + 2 * q if first else 6 - 2 * q))
                def _():
                    for j in range(2):
                        act(q, j, first)

    def forward(q, j, first):
        landed = remote(
            mine(me, first), (by_ref.at[j], by_side_ref.at[j]), by_send, j, by_recv, j,
            {"tile": TI // 2 if first else TI // 2 - 1},
        )
        each(landed, "wait_recv")
        each(relayed(q, j, first), "start")

    @pl.when(t == TI // 2 - 1)
    def _():
        over_middle(False)

    @pl.when(t == TI // 2)
    def _():
        over_middle(True)

    for k in WAVES[0]:
        each(a2a(k), "start")

    def pass_on(k, source, s):
        @pl.when((t > 0) & (t != TI // 2))
        def _():
            each(up(k, source(s, True), s, {"tile": t - 1}), "start")

        @pl.when((t < TI - 1) & (t != TI // 2 - 1))
        def _():
            each(down(k, source(s, False), s, {"tile": t + 1}), "start")

    pass_on(0, mine, me)
    own = [
        pltpu.make_async_copy(block_ref.at[me], x_ref.at[me, pl.ds(4, HR)], own_sem.at[0]),
        pltpu.make_async_copy(side_ref.at[me], e_ref.at[me, pl.ds(1, 3)], own_sem.at[1]),
    ]
    each(own, "start")

    @pl.when(t == 0)
    def _():
        x_ref[:, pl.ds(0, 4)] = jnp.zeros((PH, 4, OWN, LANES), BF16)
        e_ref[:, 0] = jnp.zeros((PH, OWN, 128), BF16)

    @pl.when(t == TI - 1)
    def _():
        x_ref[:, pl.ds(12, 4)] = jnp.zeros((PH, 4, OWN, LANES), BF16)
        e_ref[:, 4] = jnp.zeros((PH, OWN, 128), BF16)

    acc_ref[...] = jnp.zeros(acc_ref.shape, F32)
    each(own, "wait")
    for n in range(2, N_CONST):
        each(load(n), "wait")

    def step(k, _):
        s = moved(me, k, -1)

        def ahead():
            each(a2a(k + 1), "wait_recv")
            pass_on(k + 1, held, moved(me, k + 1, -1))

        @pl.when((k > 0) & (k < PH - 1))
        def _():
            ahead()

        @pl.when(t > 0)
        def _():
            each(down(k, held(s, False), s, {"tile": t - 1}), "wait_recv")

        @pl.when(t < TI - 1)
        def _():
            each(up(k, held(s, True), s, {"tile": t + 1}), "wait_recv")

        chunk(s, x_ref, e_ref, consts, scratch)

        @pl.when(k == 0)
        def _():
            relays(forward)

        for n in range(1, 4):

            @pl.when(k == n - 1)
            def _():
                for j in WAVES[n]:
                    each(a2a(j), "start")

        @pl.when(k == 0)
        def _():
            ahead()

        return 0

    lax.fori_loop(0, PH, step, 0)

    place = lax.rem(t, 8)
    plane = me * 2 + t // 8

    def first(k):
        to = lax.rem(plane + k, 16)
        return pltpu.make_async_remote_copy(
            src_ref=a_ref.at[plane], dst_ref=a_ref.at[plane], send_sem=as_sem.at[k],
            recv_sem=ar_sem.at[k],
            device_id={"photo": to // 2, "tile": lax.rem(to, 2) * 8 + place},
            device_id_type=MESH,
        )

    def second(k):
        to = lax.rem(place + k, 8)
        return pltpu.make_async_remote_copy(
            src_ref=b_ref.at[place], dst_ref=b_ref.at[place], send_sem=bs_sem.at[k],
            recv_sem=br_sem.at[k],
            device_id={"tile": t // 8 * 8 + to}, device_id_type=MESH,
        )

    planes, sums = total_gram(acc_ref, consts[5])
    a_ref[plane] = sums
    for k in range(1, 16):
        first(k).start()
    join(planes, consts[4], rows_ref)
    out = [
        pltpu.make_async_copy(
            rows_ref.at[n], fp_ref.at[:, :, pl.ds(128 * n, 128)], own_sem.at[2 + n]
        )
        for n in range(4)
    ]
    each(out, "start")
    for k in range(1, 16):
        first(k).wait_recv()
    sums = a_ref[0]
    for n in range(1, 16):
        sums += a_ref[n]
    b_ref[place] = sums
    for k in range(1, 8):
        second(k).start()
    for k in range(1, 8):
        second(k).wait_recv()
    sums = b_ref[0]
    for n in range(1, 8):
        sums += b_ref[n]
    sums_ref[...] = sums

    each(out, "wait")
    relays(lambda q, j, first: each(relayed(q, j, first), "wait_send"))
    for k in range(1, PH):
        each(a2a(k), "wait_send")
        second(k).wait_send()
    for k in range(1, 16):
        first(k).wait_send()
    for k in range(PH):
        s = moved(me, k, -1)

        @pl.when(t > 0)
        def _():
            each(up(k, held(s, True), s, {"tile": t - 1}), "wait_send")

        @pl.when(t < TI - 1)
        def _():
            each(down(k, held(s, False), s, {"tile": t + 1}), "wait_send")


SCRATCH = [
    ((3, 2 * HR, OWN, 256), F32),
    ((2 * HR, OWN, 128), F32),
    ((4, 3, HR, OWN, 512), BF16),
    ((4, HR, OWN, 256), BF16),
    ((4, 3, HR, OWN, 256), F32),
    ((4, 3, HR, OWN, 256), F32),
    ((4, 2 * HR, OWN, 256), F32),
    ((8, 256, 256), BF16),
    ((8, 256, 256), F32),
]


def fused(photos, camera_id, consts):
    vm = pl.BlockSpec(memory_space=pltpu.VMEM)
    anywhere = pl.BlockSpec(memory_space=pl.ANY)
    dma = pltpu.SemaphoreType.DMA
    return pl.pallas_call(
        fused_kernel,
        out_shape=(
            jax.ShapeDtypeStruct((CAMS, 16, 512), F32),
            jax.ShapeDtypeStruct((8, 128), F32),
        ),
        in_specs=[anywhere, pl.BlockSpec(memory_space=pltpu.SMEM)] + [anywhere] * N_CONST,
        out_specs=(anywhere, vm),
        scratch_shapes=[
            pltpu.VMEM((PH, HR, OWN, LANES), BF16),
            pltpu.VMEM((PH, 3, OWN, 128), BF16),
            pltpu.VMEM((8, PH + 2, 2, OWN, 256), BF16),
            pltpu.VMEM((PH, 2 * HR, OWN, LANES), BF16),
            pltpu.VMEM((PH, 5, OWN, 128), BF16),
            pltpu.VMEM((4, CAMS, 16, 128), F32),
            pltpu.VMEM((16, 8, 128), F32),
            pltpu.VMEM((8, 8, 128), F32),
            pltpu.VMEM((2, 4, OWN, LANES), BF16),
            pltpu.VMEM((2, OWN, 128), BF16),
            pltpu.VMEM((OWN, 16, 4096), BF16),
        ]
        + [pltpu.VMEM(c.shape, c.dtype) for c in consts[:-2]]
        + [pltpu.VMEM((*c.shape[:-2], 2 * c.shape[-2], 256), c.dtype) for c in consts[-2:]]
        + [pltpu.VMEM(s, d) for s, d in SCRATCH]
        + [dma((PH,)), dma((N_CONST, 2)), dma((6,))]
        + [dma((2, PH))] * 6
        + [dma((2, 2))] * 2
        + [dma((16,))] * 2
        + [dma((8,))] * 2,
        compiler_params=pltpu.CompilerParams(
            collective_id=0, has_side_effects=True, vmem_limit_bytes=VMEM_LIMIT
        ),
        name="fused",
    )(photos, camera_id, *consts)


def last_kernel(raw_ref, sums_hbm, fp_ref, corr_hbm, held_ref, sums_ref, corr_ref, in_sem, out_sem):
    parts = 4
    rows = CAMS // parts
    into = [pltpu.make_async_copy(sums_hbm, sums_ref, in_sem.at[parts])] + [
        pltpu.make_async_copy(raw_ref.at[pl.ds(rows * n, rows)], held_ref.at[n], in_sem.at[n])
        for n in range(parts)
    ]
    back = [pltpu.make_async_copy(corr_ref, corr_hbm, out_sem.at[parts])] + [
        pltpu.make_async_copy(held_ref.at[n], fp_ref.at[pl.ds(rows * n, rows)], out_sem.at[n])
        for n in range(parts)
    ]
    for copy in into:
        copy.start()
    for n in range(1, parts + 1):
        into[n].wait()
        back[n].start()
    into[0].wait()
    corr_ref[...] = correlated(sums_ref[...])
    back[0].start()
    for copy in back:
        copy.wait()


def last(raw, sums):
    anywhere = pl.BlockSpec(memory_space=pl.ANY)
    return pl.pallas_call(
        last_kernel,
        out_shape=(
            jax.ShapeDtypeStruct((CAMS, 16, 512), F32),
            jax.ShapeDtypeStruct((CAMS, CAMS), F32),
        ),
        in_specs=[anywhere, anywhere],
        out_specs=(anywhere, anywhere),
        scratch_shapes=[
            pltpu.VMEM((4, CAMS // 4, 16, 512), F32),
            pltpu.VMEM((8, 128), F32),
            pltpu.VMEM((CAMS, CAMS), F32),
            pltpu.SemaphoreType.DMA((5,)),
            pltpu.SemaphoreType.DMA((5,)),
        ],
        name="last",
    )(raw, sums)


def on_device(photos, camera_id):
    return last(*fused(photos, camera_id, constants()))


def solution(mesh):
    return jax.shard_map(
        on_device,
        mesh=mesh,
        in_specs=(P("photo", "tile", None), P("photo")),
        out_specs=(P(None, "tile", "photo"), P()),
        check_vma=False,
    )
```

```python
import functools

import jax
import jax.numpy as jnp
import numpy as np
from jax import lax
from jax.experimental import pallas as pl
from jax.experimental.pallas import tpu as pltpu
from jax.sharding import PartitionSpec as P

MESH = pl.DeviceIdType.MESH
F32 = jnp.float32
BF16 = jnp.bfloat16

CAMS = 32
NOISE_POWER = 1.0
VAR_EPS = 1e-06

PH = 8
TI = 16
OWN = 16
HR = 8
LANES = 1024
VMEM_LIMIT = 60 * 1024 * 1024

MOVES = ((0, 0), (0, 1), (3, 0), (1, 0), (1, 1), (3, 1), (2, 0), (2, 1))
WAVES = ((1, 3, 2), (4, 6, 5), (7,), ())
ROUTES = ((0, 1), (2, 4), (3, 5), (6, 7))


def constants():
    perm = np.zeros((256, 256), np.float32)
    for tb in range(2):
        for i in range(HR):
            for p in range(OWN):
                perm[(tb * HR + i) * OWN + p, p * 16 + 2 * i + tb] = 1.0
    edge = np.zeros((8, 256, 128), np.float32)
    for jt in range(8):
        for k in range(8):
            edge[jt, 120 + k, 16 * jt + k] = 1.0
            edge[jt, 128 + k, 16 * jt + 8 + k] = 1.0
    sign = np.array([[1, 1, 1], [1, -1, -1], [-1, 1, -1], [-1, -1, 1]], np.float32) * 0.5
    haar_edge = np.zeros((128, 512), np.float32)
    for j in range(4):
        for k in range(8):
            for b in range(3):
                for n in range(4):
                    at = 32 * j + 16 * (n // 2) + 2 * k + n % 2
                    haar_edge[at, 128 * j + 8 * b + k] = sign[n, b]
    split = np.zeros((256, 256), np.float32)
    for j in range(128):
        split[2 * j, j] = 0.5
        split[2 * j + 1, 128 + j] = 0.5
    out = np.arange(256)
    box = np.zeros((4, 256, 256), np.float32)
    box_edge = np.zeros((4, 3, 128, 256), np.float32)
    for r in range(1, 5):
        inner = (np.abs(out[:, None] - out[None, :]) <= r).astype(np.float32)
        box[r - 1] = inner
        for b in range(3):
            side = np.zeros((128, 256), np.float32)
            for k in range(8):
                cell = k - 4 if k < 4 else 252 + k
                side[8 * b + k] = np.abs(cell - out) <= r
            box_edge[r - 1, b] = side
    join = np.concatenate([split.T] * 3)
    fold = np.zeros((256, 128), np.float32)
    fold[np.arange(256), np.arange(256) // HR] = 1.0
    fold = np.concatenate([fold] * 3)
    every = (perm, edge, haar_edge, split, join, fold, box, box_edge)
    return [jnp.asarray(c, BF16) for c in every]


def dot(a, b):
    return jnp.dot(a, b, preferred_element_type=F32)


def hi_lo(x):
    hi = x.astype(BF16)
    lo = (x - hi.astype(F32)).astype(BF16)
    return hi, lo


def bands_of(px_ref, n):
    a, b, c, d = (px_ref[j, n] for j in range(4))
    plus, minus, low_plus, low_minus = a + b, a - b, c + d, c - d
    return plus - low_plus, minus + low_minus, minus - low_minus


def chunk(s, x_ref, e_ref, consts, scratch):
    haar_edge_ref, split_ref, _, _, box_ref, box_edge_ref = consts[2:]
    sq_ref, eq_ref, lhs_ref, edge_ref, sum_ref, side_ref, px_ref, data_ref, acc_ref = scratch

    rows = 2 * HR
    for ct in range(2):
        for tb in range(2):
            lane = 512 * ct + 256 * tb
            x = x_ref[s, :, :, lane : lane + 256].reshape(rows * OWN, 256)
            got = dot(x, split_ref[...])
            for odd in range(2):
                px_ref[2 * tb + odd, :, :, 128 * ct : 128 * ct + 128] = got[
                    :, 128 * odd : 128 * odd + 128
                ].reshape(rows, OWN, 128)

    def squares(n, _):
        for b, band in enumerate(bands_of(px_ref, n)):
            sq_ref[b, n] = band * band
        return 0

    lax.fori_loop(0, rows, squares, 0, unroll=2)
    x = jnp.concatenate([e_ref[s, n] for n in (0, 1, 2, 4)])
    one = dot(x, haar_edge_ref[...])
    for n in range(rows):
        g, j = divmod(n, 4)
        part = one[OWN * g : OWN * g + OWN, 128 * j : 128 * j + 128]
        eq_ref[n] = part * part

    def sums(i, _):
        row = eq_ref[i + 4]
        for r in range(1, 5):
            row = row + eq_ref[i + 4 - r] + eq_ref[i + 4 + r]
            hi, lo = hi_lo(row)
            edge_ref[r - 1, i, :, 0:128] = hi
            edge_ref[r - 1, i, :, 128:256] = lo
        for b in range(3):
            row = sq_ref[b, i + 4]
            for r in range(1, 5):
                row = row + sq_ref[b, i + 4 - r] + sq_ref[b, i + 4 + r]
                hi, lo = hi_lo(row)
                lhs_ref[r - 1, b, i, :, 0:256] = hi
                lhs_ref[r - 1, b, i, :, 256:512] = lo
        return 0

    lax.fori_loop(0, HR, sums, 0)

    for r in range(4):
        got = dot(lhs_ref[r].reshape(3 * HR * OWN, 512), box_ref[r])
        sum_ref[r] = got.reshape(3, HR, OWN, 256)
        for b in range(3):
            got = dot(edge_ref[r].reshape(HR * OWN, 256), box_edge_ref[r, b])
            side_ref[r, b] = got.reshape(HR, OWN, 256)

    def residual(i, _):
        res = []
        for b, band in enumerate(bands_of(px_ref, i + 4)):
            var = None
            for r in range(4):
                mean = (sum_ref[r, b, i] + side_ref[r, b, i]) * (1.0 / (2 * r + 3) ** 2)
                var = mean if var is None else jnp.minimum(var, mean)
            gain = NOISE_POWER / jnp.maximum(var, NOISE_POWER)
            res.append(band * gain * 0.5)
        hz, vt, dg = res
        plus, minus = hz + vt, hz - vt
        noise = (plus + dg, minus - dg, -minus - dg, dg - plus)
        at = pl.multiple_of(i * OWN, OWN)
        for j in range(4):
            x = px_ref[j, i + 4]
            for part, value in enumerate((noise[j].astype(BF16).astype(F32) * x, x * x)):
                hi, lo = hi_lo(value)
                data_ref[2 * j + part, pl.ds(at, OWN), :] = hi
                data_ref[2 * j + part, pl.ds(HR * OWN + at, OWN), :] = lo
        return 0

    lax.fori_loop(0, HR, residual, 0)

    ids = e_ref[s, 3].astype(F32)[0:1, :]
    row = lax.broadcasted_iota(jnp.int32, (256, 128), 0)
    col = lax.broadcasted_iota(jnp.int32, (256, 128), 1)
    same = ((row // HR).astype(F32) == ids) & (lax.rem(row, HR) == col // OWN)
    pick = jnp.where(same, 1.0, 0.0).astype(BF16)
    pick = jnp.concatenate([pick, pick], axis=1)
    for j in range(8):
        acc_ref[j] += dot(pick, data_ref[j])


def three(x):
    hi = x.astype(BF16)
    rest = x - hi.astype(F32)
    mid = rest.astype(BF16)
    low = (rest - mid.astype(F32)).astype(BF16)
    return jnp.concatenate([hi, mid, low], axis=1)


def total_gram(acc_ref, fold_ref):
    planes = [acc_ref[2 * j] / acc_ref[2 * j + 1] for j in range(4)]
    gram = jnp.zeros((256, 256), F32)
    for plane in planes:
        hi, lo = hi_lo(plane)
        left = jnp.concatenate([hi, hi, lo], axis=1)
        right = jnp.concatenate([hi, lo, hi], axis=1)
        gram += lax.dot_general(left, right, (((1,), (1,)), ((), ())), preferred_element_type=F32)
    row = lax.broadcasted_iota(jnp.int32, (256, 256), 0)
    col = lax.broadcasted_iota(jnp.int32, (256, 256), 1)
    gram = jnp.where(lax.rem(row, HR) == lax.rem(col, HR), gram, 0.0)
    gram = gram.reshape(CAMS, HR, 256).sum(axis=1)
    gram = dot(three(gram), fold_ref[...]) * 0.25
    total = planes[0] + planes[1] + planes[2] + planes[3]
    total = total.reshape(CAMS, HR, 256).sum(axis=1).sum(axis=1, keepdims=True) * 0.5
    row = lax.broadcasted_iota(jnp.int32, (CAMS, 128), 0)
    lane = lax.broadcasted_iota(jnp.int32, (CAMS, 128), 1)
    gram = jnp.where(lane == lax.rem(row + CAMS - 1, CAMS), total, gram)
    lane = lax.broadcasted_iota(jnp.int32, (8, 128), 1)
    sums = gram[0:8]
    for q in range(1, 4):
        part = pltpu.roll(gram[8 * q : 8 * q + 8], 32 * q, 1)
        sums = jnp.where(lane // 32 == q, part, sums)
    return planes, sums


def correlated(sums):
    gram = jnp.concatenate([sums] + [pltpu.roll(sums, 128 - 32 * q, 1) for q in range(1, 4)])
    row = lax.broadcasted_iota(jnp.int32, gram.shape, 0)
    lane = lax.broadcasted_iota(jnp.int32, gram.shape, 1)
    before = lane == lax.rem(row + CAMS - 1, CAMS)
    total = jnp.sum(jnp.where(before, gram, 0.0), axis=1, keepdims=True)
    after = (row == lax.rem(lane + CAMS - 1, CAMS)) & (lane < CAMS)
    along = jnp.sum(jnp.where(after, gram, 0.0), axis=0, keepdims=True)
    down = jnp.sum(jnp.where(row == lane, along, 0.0), axis=1, keepdims=True)
    gram = jnp.where(before, down, gram)
    pixels = float(256 * 4096)
    average = total / pixels
    across = jnp.sum(jnp.where(row == lane, average, 0.0), axis=0, keepdims=True)
    covar = gram / pixels - average * across
    own = jnp.where(row == lane, covar, 0.0)
    down = jnp.sum(own, axis=1, keepdims=True) + VAR_EPS
    along = jnp.sum(own, axis=0, keepdims=True) + VAR_EPS
    return (covar / jnp.sqrt(down * along))[:, :CAMS]


def join(planes, join_ref, rows_ref):
    for tb in range(2):
        for ct in range(2):
            pair = [planes[2 * tb + odd][:, 128 * ct : 128 * ct + 128] for odd in range(2)]
            got = dot(three(jnp.concatenate(pair, axis=1)), join_ref[...])
            for part in range(2):
                one = got[:, 128 * part : 128 * part + 128].reshape(CAMS, HR, 128)
                rows_ref[2 * ct + part, :, pl.ds(tb, HR, stride=2), :] = one


def pack(fetch, photo_ref, cid_ref, perm_ref, edge_ref, block_ref, side_ref, beside_ref):
    beside_ref[:, 1, :, :, 0:128] = jnp.zeros((8, 2, OWN, 128), BF16)
    beside_ref[:, PH, :, :, 128:256] = jnp.zeros((8, 2, OWN, 128), BF16)

    def block(d, _):
        fetch(d).wait()
        for ct in range(2):
            lane = pl.multiple_of(512 * d + 256 * ct, 256)
            x = photo_ref[:, :, pl.ds(lane, 256)].reshape(256, 256)
            y = dot(perm_ref[...], x).astype(BF16).reshape(2, HR, OWN, 256)
            for tb in range(2):
                lane = ct * 512 + tb * 256
                block_ref[d, :, :, lane : lane + 256] = y[tb]
                for i in range(HR):
                    g, j = divmod(i, 4)
                    if ct == 0:
                        beside_ref[2 * j + tb, d, g, :, 128:256] = y[tb, i, :, 0:128]
                    else:
                        beside_ref[2 * j + tb, d + 2, g, :, 0:128] = y[tb, i, :, 128:256]
        return 0

    lax.fori_loop(0, PH, block, 0)
    side = jnp.zeros((256, 128), F32)
    for jt in range(8):
        side += dot(beside_ref[jt, pl.ds(1, PH)].reshape(256, 256), edge_ref[jt])
    side_ref[:, pl.ds(0, 2)] = side.astype(BF16).reshape(PH, 2, OWN, 128)
    lane = lax.broadcasted_iota(jnp.int32, (OWN, 128), 1)
    ids = jnp.zeros((OWN, 128), jnp.int32)
    for n in range(OWN):
        ids = jnp.where(lax.rem(lane, OWN) == n, cid_ref[n], ids)
    ids = ids.astype(F32).astype(BF16)
    for d in range(PH):
        side_ref[d, 2] = ids


N_CONST = 8


def moved(me, k, sign):
    if isinstance(k, int):
        dy, dx = MOVES[k]
    else:
        dy, dx = 0, 0
        for n in range(1, PH):
            dy = jnp.where(k == n, MOVES[n][0], dy)
            dx = jnp.where(k == n, MOVES[n][1], dx)
    y, x = me // 2, lax.rem(me, 2)
    return lax.rem(y + 4 + sign * dy, 4) * 2 + lax.rem(x + dx, 2)


def fused_kernel(photo_hbm, cid_ref, *rest):
    const_hbm, rest = rest[:N_CONST], rest[N_CONST:]
    fp_ref, sums_ref, block_ref, side_ref, beside_ref, x_ref, e_ref, rows_ref, a_ref, b_ref, by_ref, by_side_ref, photo_ref = rest[:13]
    consts, rest = rest[13 : 13 + N_CONST], rest[13 + N_CONST :]
    scratch, rest = rest[:9], rest[9:]
    acc_ref = scratch[-1]
    (photo_sem, const_sem, own_sem, send_sem, recv_sem, up_send, up_recv, dn_send, dn_recv,
     by_send, by_recv, as_sem, ar_sem, bs_sem, br_sem) = rest
    me = lax.axis_index("photo")
    t = lax.axis_index("tile")

    def load(n):
        if n < N_CONST - 2:
            return [pltpu.make_async_copy(const_hbm[n], consts[n], const_sem.at[n, 0])]
        depth = consts[n].shape[-2] // 2
        lead = (slice(None),) * (len(consts[n].shape) - 2)
        return [
            pltpu.make_async_copy(
                const_hbm[n], consts[n].at[(*lead, pl.ds(depth * part, depth))], const_sem.at[n, part]
            )
            for part in range(2)
        ]

    def fetch(d):
        lanes = pl.ds(pl.multiple_of(512 * d, 512), 512)
        return pltpu.make_async_copy(
            photo_hbm.at[:, :, lanes], photo_ref.at[:, :, lanes], photo_sem.at[d]
        )

    def each(copies, act):
        for copy in copies:
            getattr(copy, act)()

    for d in range(PH):
        fetch(d).start()
    for n in range(N_CONST):
        each(load(n), "start")

    barrier = pltpu.get_barrier_semaphore()
    middle = t * (TI - 1 - t) // 56
    half = t // (TI // 2)
    inward = t + half * (TI - 1 - 2 * t)
    relay = (1 - lax.rem(inward, 2)) * (1 - inward // 6)
    for k in range(1, PH):
        peer = lax.rem(me + k, PH)
        pl.semaphore_signal(barrier, inc=1, device_id={"photo": peer}, device_id_type=MESH)
    for k in range(1, TI):
        pl.semaphore_signal(
            barrier, inc=1, device_id={"tile": lax.rem(t + k, TI)}, device_id_type=MESH
        )

    for k in range(1, PH):
        where = {"photo": lax.rem(me + k, PH), "tile": lax.rem(t + TI // 2, TI)}
        pl.semaphore_signal(barrier, inc=1, device_id=where, device_id_type=MESH)

    @pl.when(middle == 1)
    def _():
        for k in range(1, PH):
            where = {"photo": lax.rem(me + k, PH), "tile": TI - 1 - t}
            pl.semaphore_signal(barrier, inc=1, device_id=where, device_id_type=MESH)
            for q in range(1, 4):
                where = {"photo": lax.rem(me + k, PH), "tile": (1 - half) * (9 + 2 * q) + half * (6 - 2 * q)}
                pl.semaphore_signal(barrier, inc=1, device_id=where, device_id_type=MESH)

    @pl.when(relay == 1)
    def _():
        for k in range(1, PH):
            where = {"photo": lax.rem(me + k, PH), "tile": TI // 2 - half}
            pl.semaphore_signal(barrier, inc=1, device_id=where, device_id_type=MESH)

    each(load(0), "wait")
    each(load(1), "wait")
    pack(fetch, photo_ref, cid_ref, consts[0], consts[1], block_ref, side_ref, beside_ref)
    pl.semaphore_wait(barrier, 2 * PH + TI - 3 + (PH - 1) * (4 * middle + relay))

    def remote(srcs, dsts, send, k, recv, j, where):
        return [
            pltpu.make_async_remote_copy(
                src_ref=a, dst_ref=b, send_sem=send.at[n, k], recv_sem=recv.at[n, j],
                device_id=where, device_id_type=MESH,
            )
            for n, (a, b) in enumerate(zip(srcs, dsts))
        ]

    def a2a(k):
        peer = moved(me, k, 1)
        return remote(
            (block_ref.at[peer], side_ref.at[peer]),
            (x_ref.at[me, pl.ds(4, HR)], e_ref.at[me, pl.ds(1, 3)]),
            send_sem, k, recv_sem, k, {"photo": peer},
        )

    def up(k, srcs, s, where):
        dsts = (x_ref.at[s, pl.ds(12, 4)], e_ref.at[s, 4])
        return remote(srcs, dsts, up_send, k, up_recv, k, where)

    def down(k, srcs, s, where):
        dsts = (x_ref.at[s, pl.ds(0, 4)], e_ref.at[s, 0])
        return remote(srcs, dsts, dn_send, k, dn_recv, k, where)

    def held(s, first):
        return (x_ref.at[s, pl.ds(4 if first else 8, 4)], e_ref.at[s, 1 if first else 2])

    def mine(d, first):
        return (block_ref.at[d, pl.ds(0 if first else 4, 4)], side_ref.at[d, 0 if first else 1])

    def over_middle(first):
        act = up if first else down
        for q in range(4):
            for j, k in enumerate(ROUTES[q]):
                peer = moved(me, k, 1)
                if q == 0:
                    where = {"photo": peer, "tile": TI // 2 - 1 if first else TI // 2}
                    copies = act(k, mine(peer, first), me, where)
                else:
                    copies = remote(
                        mine(peer, first), (by_ref.at[j], by_side_ref.at[j]),
                        up_send if first else dn_send, k, by_recv, j,
                        {"tile": 9 + 2 * q if first else 6 - 2 * q},
                    )
                each(copies, "start")

    def relayed(q, j, first):
        k = ROUTES[q][j]
        if first:
            dsts, recv = (x_ref.at[me, pl.ds(12, 4)], e_ref.at[me, 4]), up_recv
        else:
            dsts, recv = (x_ref.at[me, pl.ds(0, 4)], e_ref.at[me, 0]), dn_recv
        where = {"photo": moved(me, k, 1), "tile": TI // 2 - 1 if first else TI // 2}
        return remote((by_ref.at[j], by_side_ref.at[j]), dsts, by_send, j, recv, k, where)

    def relays(act):
        for q in range(1, 4):
            for first in (False, True):

                @pl.when(t == (9 + 2 * q if first else 6 - 2 * q))
                def _():
                    for j in range(2):
                        act(q, j, first)

    def forward(q, j, first):
        landed = remote(
            mine(me, first), (by_ref.at[j], by_side_ref.at[j]), by_send, j, by_recv, j,
            {"tile": TI // 2 if first else TI // 2 - 1},
        )
        each(landed, "wait_recv")
        each(relayed(q, j, first), "start")

    @pl.when(t == TI // 2 - 1)
    def _():
        over_middle(False)

    @pl.when(t == TI // 2)
    def _():
        over_middle(True)

    for k in WAVES[0]:
        each(a2a(k), "start")

    def pass_on(k, source, s):
        @pl.when((t > 0) & (t != TI // 2))
        def _():
            each(up(k, source(s, True), s, {"tile": t - 1}), "start")

        @pl.when((t < TI - 1) & (t != TI // 2 - 1))
        def _():
            each(down(k, source(s, False), s, {"tile": t + 1}), "start")

    pass_on(0, mine, me)
    own = [
        pltpu.make_async_copy(block_ref.at[me], x_ref.at[me, pl.ds(4, HR)], own_sem.at[0]),
        pltpu.make_async_copy(side_ref.at[me], e_ref.at[me, pl.ds(1, 3)], own_sem.at[1]),
    ]
    each(own, "start")

    @pl.when(t == 0)
    def _():
        x_ref[:, pl.ds(0, 4)] = jnp.zeros((PH, 4, OWN, LANES), BF16)
        e_ref[:, 0] = jnp.zeros((PH, OWN, 128), BF16)

    @pl.when(t == TI - 1)
    def _():
        x_ref[:, pl.ds(12, 4)] = jnp.zeros((PH, 4, OWN, LANES), BF16)
        e_ref[:, 4] = jnp.zeros((PH, OWN, 128), BF16)

    acc_ref[...] = jnp.zeros(acc_ref.shape, F32)
    each(own, "wait")
    for n in range(2, N_CONST):
        each(load(n), "wait")

    def step(k, _):
        s = moved(me, k, -1)

        def ahead():
            each(a2a(k + 1), "wait_recv")
            pass_on(k + 1, held, moved(me, k + 1, -1))

        @pl.when((k > 0) & (k < PH - 1))
        def _():
            ahead()

        @pl.when(t > 0)
        def _():
            each(down(k, held(s, False), s, {"tile": t - 1}), "wait_recv")

        @pl.when(t < TI - 1)
        def _():
            each(up(k, held(s, True), s, {"tile": t + 1}), "wait_recv")

        chunk(s, x_ref, e_ref, consts, scratch)

        @pl.when(k == 0)
        def _():
            relays(forward)

        for n in range(1, 4):

            @pl.when(k == n - 1)
            def _():
                for j in WAVES[n]:
                    each(a2a(j), "start")

        @pl.when(k == 0)
        def _():
            ahead()

        return 0

    lax.fori_loop(0, PH, step, 0)

    place = lax.rem(t, 8)
    plane = me * 2 + t // 8

    def first(k):
        to = lax.rem(plane + k, 16)
        return pltpu.make_async_remote_copy(
            src_ref=a_ref.at[plane], dst_ref=a_ref.at[plane], send_sem=as_sem.at[k],
            recv_sem=ar_sem.at[k],
            device_id={"photo": to // 2, "tile": lax.rem(to, 2) * 8 + place},
            device_id_type=MESH,
        )

    def second(k):
        to = lax.rem(place + k, 8)
        return pltpu.make_async_remote_copy(
            src_ref=b_ref.at[place], dst_ref=b_ref.at[place], send_sem=bs_sem.at[k],
            recv_sem=br_sem.at[k],
            device_id={"tile": t // 8 * 8 + to}, device_id_type=MESH,
        )

    planes, sums = total_gram(acc_ref, consts[5])
    a_ref[plane] = sums
    for k in range(1, 16):
        first(k).start()
    join(planes, consts[4], rows_ref)
    out = [
        pltpu.make_async_copy(
            rows_ref.at[n], fp_ref.at[:, :, pl.ds(128 * n, 128)], own_sem.at[2 + n]
        )
        for n in range(4)
    ]
    each(out, "start")
    for k in range(1, 16):
        first(k).wait_recv()
    sums = a_ref[0]
    for n in range(1, 16):
        sums += a_ref[n]
    b_ref[place] = sums
    for k in range(1, 8):
        second(k).start()
    for k in range(1, 8):
        second(k).wait_recv()
    sums = b_ref[0]
    for n in range(1, 8):
        sums += b_ref[n]
    sums_ref[...] = sums

    each(out, "wait")
    relays(lambda q, j, first: each(relayed(q, j, first), "wait_send"))
    for k in range(1, PH):
        each(a2a(k), "wait_send")
        second(k).wait_send()
    for k in range(1, 16):
        first(k).wait_send()
    for k in range(PH):
        s = moved(me, k, -1)

        @pl.when(t > 0)
        def _():
            each(up(k, held(s, True), s, {"tile": t - 1}), "wait_send")

        @pl.when(t < TI - 1)
        def _():
            each(down(k, held(s, False), s, {"tile": t + 1}), "wait_send")


SCRATCH = [
    ((3, 2 * HR, OWN, 256), F32),
    ((2 * HR, OWN, 128), F32),
    ((4, 3, HR, OWN, 512), BF16),
    ((4, HR, OWN, 256), BF16),
    ((4, 3, HR, OWN, 256), F32),
    ((4, 3, HR, OWN, 256), F32),
    ((4, 2 * HR, OWN, 256), F32),
    ((8, 256, 256), BF16),
    ((8, 256, 256), F32),
]


def fused(photos, camera_id, consts):
    vm = pl.BlockSpec(memory_space=pltpu.VMEM)
    anywhere = pl.BlockSpec(memory_space=pl.ANY)
    dma = pltpu.SemaphoreType.DMA
    return pl.pallas_call(
        fused_kernel,
        out_shape=(
            jax.ShapeDtypeStruct((CAMS, 16, 512), F32),
            jax.ShapeDtypeStruct((8, 128), F32),
        ),
        in_specs=[anywhere, pl.BlockSpec(memory_space=pltpu.SMEM)] + [anywhere] * N_CONST,
        out_specs=(anywhere, vm),
        scratch_shapes=[
            pltpu.VMEM((PH, HR, OWN, LANES), BF16),
            pltpu.VMEM((PH, 3, OWN, 128), BF16),
            pltpu.VMEM((8, PH + 2, 2, OWN, 256), BF16),
            pltpu.VMEM((PH, 2 * HR, OWN, LANES), BF16),
            pltpu.VMEM((PH, 5, OWN, 128), BF16),
            pltpu.VMEM((4, CAMS, 16, 128), F32),
            pltpu.VMEM((16, 8, 128), F32),
            pltpu.VMEM((8, 8, 128), F32),
            pltpu.VMEM((2, 4, OWN, LANES), BF16),
            pltpu.VMEM((2, OWN, 128), BF16),
            pltpu.VMEM((OWN, 16, 4096), BF16),
        ]
        + [pltpu.VMEM(c.shape, c.dtype) for c in consts[:-2]]
        + [pltpu.VMEM((*c.shape[:-2], 2 * c.shape[-2], 256), c.dtype) for c in consts[-2:]]
        + [pltpu.VMEM(s, d) for s, d in SCRATCH]
        + [dma((PH,)), dma((N_CONST, 2)), dma((6,))]
        + [dma((2, PH))] * 6
        + [dma((2, 2))] * 2
        + [dma((16,))] * 2
        + [dma((8,))] * 2,
        compiler_params=pltpu.CompilerParams(
            collective_id=0, has_side_effects=True, vmem_limit_bytes=VMEM_LIMIT
        ),
        name="fused",
    )(photos, camera_id, *consts)


def last_kernel(raw_ref, sums_hbm, fp_ref, corr_hbm, held_ref, sums_ref, corr_ref, in_sem, out_sem):
    parts = 4
    rows = CAMS // parts
    into = [pltpu.make_async_copy(sums_hbm, sums_ref, in_sem.at[parts])] + [
        pltpu.make_async_copy(raw_ref.at[pl.ds(rows * n, rows)], held_ref.at[n], in_sem.at[n])
        for n in range(parts)
    ]
    back = [pltpu.make_async_copy(corr_ref, corr_hbm, out_sem.at[parts])] + [
        pltpu.make_async_copy(held_ref.at[n], fp_ref.at[pl.ds(rows * n, rows)], out_sem.at[n])
        for n in range(parts)
    ]
    for copy in into:
        copy.start()
    for n in range(1, parts + 1):
        into[n].wait()
        back[n].start()
    into[0].wait()
    corr_ref[...] = correlated(sums_ref[...])
    back[0].start()
    for copy in back:
        copy.wait()


def last(raw, sums):
    anywhere = pl.BlockSpec(memory_space=pl.ANY)
    return pl.pallas_call(
        last_kernel,
        out_shape=(
            jax.ShapeDtypeStruct((CAMS, 16, 512), F32),
            jax.ShapeDtypeStruct((CAMS, CAMS), F32),
        ),
        in_specs=[anywhere, anywhere],
        out_specs=(anywhere, anywhere),
        scratch_shapes=[
            pltpu.VMEM((4, CAMS // 4, 16, 512), F32),
            pltpu.VMEM((8, 128), F32),
            pltpu.VMEM((CAMS, CAMS), F32),
            pltpu.SemaphoreType.DMA((5,)),
            pltpu.SemaphoreType.DMA((5,)),
        ],
        name="last",
    )(raw, sums)


def on_device(photos, camera_id):
    return last(*fused(photos, camera_id, constants()))


def solution(mesh):
    return jax.shard_map(
        on_device,
        mesh=mesh,
        in_specs=(P("photo", "tile", None), P("photo")),
        out_specs=(P(None, "tile", "photo"), P()),
        check_vma=False,
    )
```

```python
import functools

import jax
import jax.numpy as jnp
import numpy as np
from jax import lax
from jax.experimental import pallas as pl
from jax.experimental.pallas import tpu as pltpu
from jax.sharding import PartitionSpec as P

MESH = pl.DeviceIdType.MESH
F32 = jnp.float32
BF16 = jnp.bfloat16

CAMS = 32
NOISE_POWER = 1.0
VAR_EPS = 1e-06

PH = 8
TI = 16
OWN = 16
HR = 8
LANES = 1024
VMEM_LIMIT = 60 * 1024 * 1024

MOVES = ((0, 0), (0, 1), (3, 0), (1, 0), (1, 1), (3, 1), (2, 0), (2, 1))
WAVES = ((1, 3, 2), (4, 6, 5), (7,), ())
ROUTES = ((0, 1), (2, 4), (3, 5), (6, 7))


def constants():
    perm = np.zeros((256, 256), np.float32)
    for tb in range(2):
        for i in range(HR):
            for p in range(OWN):
                perm[(tb * HR + i) * OWN + p, p * 16 + 2 * i + tb] = 1.0
    edge = np.zeros((8, 256, 128), np.float32)
    for jt in range(8):
        for k in range(8):
            edge[jt, 120 + k, 16 * jt + k] = 1.0
            edge[jt, 128 + k, 16 * jt + 8 + k] = 1.0
    sign = np.array([[1, 1, 1], [1, -1, -1], [-1, 1, -1], [-1, -1, 1]], np.float32) * 0.5
    haar_edge = np.zeros((128, 512), np.float32)
    for j in range(4):
        for k in range(8):
            for b in range(3):
                for n in range(4):
                    at = 32 * j + 16 * (n // 2) + 2 * k + n % 2
                    haar_edge[at, 128 * j + 8 * b + k] = sign[n, b]
    split = np.zeros((256, 256), np.float32)
    for j in range(128):
        split[2 * j, j] = 0.5
        split[2 * j + 1, 128 + j] = 0.5
    out = np.arange(256)
    box = np.zeros((4, 256, 256), np.float32)
    box_edge = np.zeros((4, 3, 128, 256), np.float32)
    for r in range(1, 5):
        inner = (np.abs(out[:, None] - out[None, :]) <= r).astype(np.float32)
        box[r - 1] = inner
        for b in range(3):
            side = np.zeros((128, 256), np.float32)
            for k in range(8):
                cell = k - 4 if k < 4 else 252 + k
                side[8 * b + k] = np.abs(cell - out) <= r
            box_edge[r - 1, b] = side
    join = np.concatenate([split.T] * 3)
    fold = np.zeros((256, 128), np.float32)
    fold[np.arange(256), np.arange(256) // HR] = 1.0
    fold = np.concatenate([fold] * 3)
    every = (perm, edge, haar_edge, split, join, fold, box, box_edge)
    return [jnp.asarray(c, BF16) for c in every]


def dot(a, b):
    return jnp.dot(a, b, preferred_element_type=F32)


def hi_lo(x):
    hi = x.astype(BF16)
    lo = (x - hi.astype(F32)).astype(BF16)
    return hi, lo


def bands_of(px_ref, n):
    a, b, c, d = (px_ref[j, n] for j in range(4))
    plus, minus, low_plus, low_minus = a + b, a - b, c + d, c - d
    return plus - low_plus, minus + low_minus, minus - low_minus


def chunk(s, x_ref, e_ref, consts, scratch):
    haar_edge_ref, split_ref, _, _, box_ref, box_edge_ref = consts[2:]
    sq_ref, eq_ref, lhs_ref, edge_ref, sum_ref, side_ref, px_ref, data_ref, acc_ref = scratch

    rows = 2 * HR
    for ct in range(2):
        for tb in range(2):
            lane = 512 * ct + 256 * tb
            x = x_ref[s, :, :, lane : lane + 256].reshape(rows * OWN, 256)
            got = dot(x, split_ref[...])
            for odd in range(2):
                px_ref[2 * tb + odd, :, :, 128 * ct : 128 * ct + 128] = got[
                    :, 128 * odd : 128 * odd + 128
                ].reshape(rows, OWN, 128)

    def squares(n, _):
        for b, band in enumerate(bands_of(px_ref, n)):
            sq_ref[b, n] = band * band
        return 0

    lax.fori_loop(0, rows, squares, 0, unroll=True)
    x = jnp.concatenate([e_ref[s, n] for n in (0, 1, 2, 4)])
    one = dot(x, haar_edge_ref[...])
    for n in range(rows):
        g, j = divmod(n, 4)
        part = one[OWN * g : OWN * g + OWN, 128 * j : 128 * j + 128]
        eq_ref[n] = part * part

    def sums(i, _):
        row = eq_ref[i + 4]
        for r in range(1, 5):
            row = row + eq_ref[i + 4 - r] + eq_ref[i + 4 + r]
            hi, lo = hi_lo(row)
            edge_ref[r - 1, i, :, 0:128] = hi
            edge_ref[r - 1, i, :, 128:256] = lo
        for b in range(3):
            row = sq_ref[b, i + 4]
            for r in range(1, 5):
                row = row + sq_ref[b, i + 4 - r] + sq_ref[b, i + 4 + r]
                hi, lo = hi_lo(row)
                lhs_ref[r - 1, b, i, :, 0:256] = hi
                lhs_ref[r - 1, b, i, :, 256:512] = lo
        return 0

    lax.fori_loop(0, HR, sums, 0, unroll=True)

    for r in range(4):
        got = dot(lhs_ref[r].reshape(3 * HR * OWN, 512), box_ref[r])
        sum_ref[r] = got.reshape(3, HR, OWN, 256)
        for b in range(3):
            got = dot(edge_ref[r].reshape(HR * OWN, 256), box_edge_ref[r, b])
            side_ref[r, b] = got.reshape(HR, OWN, 256)

    def residual(i, _):
        res = []
        for b, band in enumerate(bands_of(px_ref, i + 4)):
            var = None
            for r in range(4):
                mean = (sum_ref[r, b, i] + side_ref[r, b, i]) * (1.0 / (2 * r + 3) ** 2)
                var = mean if var is None else jnp.minimum(var, mean)
            gain = NOISE_POWER / jnp.maximum(var, NOISE_POWER)
            res.append(band * gain * 0.5)
        hz, vt, dg = res
        plus, minus = hz + vt, hz - vt
        noise = (plus + dg, minus - dg, -minus - dg, dg - plus)
        at = pl.multiple_of(i * OWN, OWN)
        for j in range(4):
            x = px_ref[j, i + 4]
            for part, value in enumerate((noise[j].astype(BF16).astype(F32) * x, x * x)):
                hi, lo = hi_lo(value)
                data_ref[2 * j + part, pl.ds(at, OWN), :] = hi
                data_ref[2 * j + part, pl.ds(HR * OWN + at, OWN), :] = lo
        return 0

    lax.fori_loop(0, HR, residual, 0, unroll=True)

    ids = e_ref[s, 3].astype(F32)[0:1, :]
    row = lax.broadcasted_iota(jnp.int32, (256, 128), 0)
    col = lax.broadcasted_iota(jnp.int32, (256, 128), 1)
    same = ((row // HR).astype(F32) == ids) & (lax.rem(row, HR) == col // OWN)
    pick = jnp.where(same, 1.0, 0.0).astype(BF16)
    pick = jnp.concatenate([pick, pick], axis=1)
    for j in range(8):
        acc_ref[j] += dot(pick, data_ref[j])


def three(x):
    hi = x.astype(BF16)
    rest = x - hi.astype(F32)
    mid = rest.astype(BF16)
    low = (rest - mid.astype(F32)).astype(BF16)
    return jnp.concatenate([hi, mid, low], axis=1)


def total_gram(acc_ref, fold_ref):
    planes = [acc_ref[2 * j] / acc_ref[2 * j + 1] for j in range(4)]
    gram = jnp.zeros((256, 256), F32)
    for plane in planes:
        hi, lo = hi_lo(plane)
        left = jnp.concatenate([hi, hi, lo], axis=1)
        right = jnp.concatenate([hi, lo, hi], axis=1)
        gram += lax.dot_general(left, right, (((1,), (1,)), ((), ())), preferred_element_type=F32)
    row = lax.broadcasted_iota(jnp.int32, (256, 256), 0)
    col = lax.broadcasted_iota(jnp.int32, (256, 256), 1)
    gram = jnp.where(lax.rem(row, HR) == lax.rem(col, HR), gram, 0.0)
    gram = gram.reshape(CAMS, HR, 256).sum(axis=1)
    gram = dot(three(gram), fold_ref[...]) * 0.25
    total = planes[0] + planes[1] + planes[2] + planes[3]
    total = total.reshape(CAMS, HR, 256).sum(axis=1).sum(axis=1, keepdims=True) * 0.5
    row = lax.broadcasted_iota(jnp.int32, (CAMS, 128), 0)
    lane = lax.broadcasted_iota(jnp.int32, (CAMS, 128), 1)
    gram = jnp.where(lane == lax.rem(row + CAMS - 1, CAMS), total, gram)
    lane = lax.broadcasted_iota(jnp.int32, (8, 128), 1)
    sums = gram[0:8]
    for q in range(1, 4):
        part = pltpu.roll(gram[8 * q : 8 * q + 8], 32 * q, 1)
        sums = jnp.where(lane // 32 == q, part, sums)
    return planes, sums


def correlated(sums):
    gram = jnp.concatenate([sums] + [pltpu.roll(sums, 128 - 32 * q, 1) for q in range(1, 4)])
    row = lax.broadcasted_iota(jnp.int32, gram.shape, 0)
    lane = lax.broadcasted_iota(jnp.int32, gram.shape, 1)
    before = lane == lax.rem(row + CAMS - 1, CAMS)
    total = jnp.sum(jnp.where(before, gram, 0.0), axis=1, keepdims=True)
    after = (row == lax.rem(lane + CAMS - 1, CAMS)) & (lane < CAMS)
    along = jnp.sum(jnp.where(after, gram, 0.0), axis=0, keepdims=True)
    down = jnp.sum(jnp.where(row == lane, along, 0.0), axis=1, keepdims=True)
    gram = jnp.where(before, down, gram)
    pixels = float(256 * 4096)
    average = total / pixels
    across = jnp.sum(jnp.where(row == lane, average, 0.0), axis=0, keepdims=True)
    covar = gram / pixels - average * across
    own = jnp.where(row == lane, covar, 0.0)
    down = jnp.sum(own, axis=1, keepdims=True) + VAR_EPS
    along = jnp.sum(own, axis=0, keepdims=True) + VAR_EPS
    return (covar / jnp.sqrt(down * along))[:, :CAMS]


def join(planes, join_ref, rows_ref):
    for tb in range(2):
        for ct in range(2):
            pair = [planes[2 * tb + odd][:, 128 * ct : 128 * ct + 128] for odd in range(2)]
            got = dot(three(jnp.concatenate(pair, axis=1)), join_ref[...])
            for part in range(2):
                one = got[:, 128 * part : 128 * part + 128].reshape(CAMS, HR, 128)
                rows_ref[2 * ct + part, :, pl.ds(tb, HR, stride=2), :] = one


def pack(fetch, photo_ref, cid_ref, perm_ref, edge_ref, block_ref, side_ref, beside_ref):
    beside_ref[:, 1, :, :, 0:128] = jnp.zeros((8, 2, OWN, 128), BF16)
    beside_ref[:, PH, :, :, 128:256] = jnp.zeros((8, 2, OWN, 128), BF16)

    def block(d, _):
        fetch(d).wait()
        for ct in range(2):
            lane = pl.multiple_of(512 * d + 256 * ct, 256)
            x = photo_ref[:, :, pl.ds(lane, 256)].reshape(256, 256)
            y = dot(perm_ref[...], x).astype(BF16).reshape(2, HR, OWN, 256)
            for tb in range(2):
                lane = ct * 512 + tb * 256
                block_ref[d, :, :, lane : lane + 256] = y[tb]
                for i in range(HR):
                    g, j = divmod(i, 4)
                    if ct == 0:
                        beside_ref[2 * j + tb, d, g, :, 128:256] = y[tb, i, :, 0:128]
                    else:
                        beside_ref[2 * j + tb, d + 2, g, :, 0:128] = y[tb, i, :, 128:256]
        return 0

    lax.fori_loop(0, PH, block, 0)
    side = jnp.zeros((256, 128), F32)
    for jt in range(8):
        side += dot(beside_ref[jt, pl.ds(1, PH)].reshape(256, 256), edge_ref[jt])
    side_ref[:, pl.ds(0, 2)] = side.astype(BF16).reshape(PH, 2, OWN, 128)
    lane = lax.broadcasted_iota(jnp.int32, (OWN, 128), 1)
    ids = jnp.zeros((OWN, 128), jnp.int32)
    for n in range(OWN):
        ids = jnp.where(lax.rem(lane, OWN) == n, cid_ref[n], ids)
    ids = ids.astype(F32).astype(BF16)
    for d in range(PH):
        side_ref[d, 2] = ids


N_CONST = 8


def moved(me, k, sign):
    if isinstance(k, int):
        dy, dx = MOVES[k]
    else:
        dy, dx = 0, 0
        for n in range(1, PH):
            dy = jnp.where(k == n, MOVES[n][0], dy)
            dx = jnp.where(k == n, MOVES[n][1], dx)
    y, x = me // 2, lax.rem(me, 2)
    return lax.rem(y + 4 + sign * dy, 4) * 2 + lax.rem(x + dx, 2)


def fused_kernel(photo_hbm, cid_ref, *rest):
    const_hbm, rest = rest[:N_CONST], rest[N_CONST:]
    fp_ref, sums_ref, block_ref, side_ref, beside_ref, x_ref, e_ref, rows_ref, a_ref, b_ref, by_ref, by_side_ref, photo_ref = rest[:13]
    consts, rest = rest[13 : 13 + N_CONST], rest[13 + N_CONST :]
    scratch, rest = rest[:9], rest[9:]
    acc_ref = scratch[-1]
    (photo_sem, const_sem, own_sem, send_sem, recv_sem, up_send, up_recv, dn_send, dn_recv,
     by_send, by_recv, as_sem, ar_sem, bs_sem, br_sem) = rest
    me = lax.axis_index("photo")
    t = lax.axis_index("tile")

    def load(n):
        if n < N_CONST - 2:
            return [pltpu.make_async_copy(const_hbm[n], consts[n], const_sem.at[n, 0])]
        depth = consts[n].shape[-2] // 2
        lead = (slice(None),) * (len(consts[n].shape) - 2)
        return [
            pltpu.make_async_copy(
                const_hbm[n], consts[n].at[(*lead, pl.ds(depth * part, depth))], const_sem.at[n, part]
            )
            for part in range(2)
        ]

    def fetch(d):
        lanes = pl.ds(pl.multiple_of(512 * d, 512), 512)
        return pltpu.make_async_copy(
            photo_hbm.at[:, :, lanes], photo_ref.at[:, :, lanes], photo_sem.at[d]
        )

    def each(copies, act):
        for copy in copies:
            getattr(copy, act)()

    for d in range(PH):
        fetch(d).start()
    for n in range(N_CONST):
        each(load(n), "start")

    barrier = pltpu.get_barrier_semaphore()
    middle = t * (TI - 1 - t) // 56
    half = t // (TI // 2)
    inward = t + half * (TI - 1 - 2 * t)
    relay = (1 - lax.rem(inward, 2)) * (1 - inward // 6)
    for k in range(1, PH):
        peer = lax.rem(me + k, PH)
        pl.semaphore_signal(barrier, inc=1, device_id={"photo": peer}, device_id_type=MESH)
    for k in range(1, TI):
        pl.semaphore_signal(
            barrier, inc=1, device_id={"tile": lax.rem(t + k, TI)}, device_id_type=MESH
        )

    for k in range(1, PH):
        where = {"photo": lax.rem(me + k, PH), "tile": lax.rem(t + TI // 2, TI)}
        pl.semaphore_signal(barrier, inc=1, device_id=where, device_id_type=MESH)

    @pl.when(middle == 1)
    def _():
        for k in range(1, PH):
            where = {"photo": lax.rem(me + k, PH), "tile": TI - 1 - t}
            pl.semaphore_signal(barrier, inc=1, device_id=where, device_id_type=MESH)
            for q in range(1, 4):
                where = {"photo": lax.rem(me + k, PH), "tile": (1 - half) * (9 + 2 * q) + half * (6 - 2 * q)}
                pl.semaphore_signal(barrier, inc=1, device_id=where, device_id_type=MESH)

    @pl.when(relay == 1)
    def _():
        for k in range(1, PH):
            where = {"photo": lax.rem(me + k, PH), "tile": TI // 2 - half}
            pl.semaphore_signal(barrier, inc=1, device_id=where, device_id_type=MESH)

    each(load(0), "wait")
    each(load(1), "wait")
    pack(fetch, photo_ref, cid_ref, consts[0], consts[1], block_ref, side_ref, beside_ref)
    pl.semaphore_wait(barrier, 2 * PH + TI - 3 + (PH - 1) * (4 * middle + relay))

    def remote(srcs, dsts, send, k, recv, j, where):
        return [
            pltpu.make_async_remote_copy(
                src_ref=a, dst_ref=b, send_sem=send.at[n, k], recv_sem=recv.at[n, j],
                device_id=where, device_id_type=MESH,
            )
            for n, (a, b) in enumerate(zip(srcs, dsts))
        ]

    def a2a(k):
        peer = moved(me, k, 1)
        return remote(
            (block_ref.at[peer], side_ref.at[peer]),
            (x_ref.at[me, pl.ds(4, HR)], e_ref.at[me, pl.ds(1, 3)]),
            send_sem, k, recv_sem, k, {"photo": peer},
        )

    def up(k, srcs, s, where):
        dsts = (x_ref.at[s, pl.ds(12, 4)], e_ref.at[s, 4])
        return remote(srcs, dsts, up_send, k, up_recv, k, where)

    def down(k, srcs, s, where):
        dsts = (x_ref.at[s, pl.ds(0, 4)], e_ref.at[s, 0])
        return remote(srcs, dsts, dn_send, k, dn_recv, k, where)

    def held(s, first):
        return (x_ref.at[s, pl.ds(4 if first else 8, 4)], e_ref.at[s, 1 if first else 2])

    def mine(d, first):
        return (block_ref.at[d, pl.ds(0 if first else 4, 4)], side_ref.at[d, 0 if first else 1])

    def over_middle(first):
        act = up if first else down
        for q in range(4):
            for j, k in enumerate(ROUTES[q]):
                peer = moved(me, k, 1)
                if q == 0:
                    where = {"photo": peer, "tile": TI // 2 - 1 if first else TI // 2}
                    copies = act(k, mine(peer, first), me, where)
                else:
                    copies = remote(
                        mine(peer, first), (by_ref.at[j], by_side_ref.at[j]),
                        up_send if first else dn_send, k, by_recv, j,
                        {"tile": 9 + 2 * q if first else 6 - 2 * q},
                    )
                each(copies, "start")

    def relayed(q, j, first):
        k = ROUTES[q][j]
        if first:
            dsts, recv = (x_ref.at[me, pl.ds(12, 4)], e_ref.at[me, 4]), up_recv
        else:
            dsts, recv = (x_ref.at[me, pl.ds(0, 4)], e_ref.at[me, 0]), dn_recv
        where = {"photo": moved(me, k, 1), "tile": TI // 2 - 1 if first else TI // 2}
        return remote((by_ref.at[j], by_side_ref.at[j]), dsts, by_send, j, recv, k, where)

    def relays(act):
        for q in range(1, 4):
            for first in (False, True):

                @pl.when(t == (9 + 2 * q if first else 6 - 2 * q))
                def _():
                    for j in range(2):
                        act(q, j, first)

    def forward(q, j, first):
        landed = remote(
            mine(me, first), (by_ref.at[j], by_side_ref.at[j]), by_send, j, by_recv, j,
            {"tile": TI // 2 if first else TI // 2 - 1},
        )
        each(landed, "wait_recv")
        each(relayed(q, j, first), "start")

    @pl.when(t == TI // 2 - 1)
    def _():
        over_middle(False)

    @pl.when(t == TI // 2)
    def _():
        over_middle(True)

    for k in WAVES[0]:
        each(a2a(k), "start")

    def pass_on(k, source, s):
        @pl.when((t > 0) & (t != TI // 2))
        def _():
            each(up(k, source(s, True), s, {"tile": t - 1}), "start")

        @pl.when((t < TI - 1) & (t != TI // 2 - 1))
        def _():
            each(down(k, source(s, False), s, {"tile": t + 1}), "start")

    pass_on(0, mine, me)
    own = [
        pltpu.make_async_copy(block_ref.at[me], x_ref.at[me, pl.ds(4, HR)], own_sem.at[0]),
        pltpu.make_async_copy(side_ref.at[me], e_ref.at[me, pl.ds(1, 3)], own_sem.at[1]),
    ]
    each(own, "start")

    @pl.when(t == 0)
    def _():
        x_ref[:, pl.ds(0, 4)] = jnp.zeros((PH, 4, OWN, LANES), BF16)
        e_ref[:, 0] = jnp.zeros((PH, OWN, 128), BF16)

    @pl.when(t == TI - 1)
    def _():
        x_ref[:, pl.ds(12, 4)] = jnp.zeros((PH, 4, OWN, LANES), BF16)
        e_ref[:, 4] = jnp.zeros((PH, OWN, 128), BF16)

    acc_ref[...] = jnp.zeros(acc_ref.shape, F32)
    each(own, "wait")
    for n in range(2, N_CONST):
        each(load(n), "wait")

    def step(k, _):
        s = moved(me, k, -1)

        def ahead():
            each(a2a(k + 1), "wait_recv")
            pass_on(k + 1, held, moved(me, k + 1, -1))

        @pl.when((k > 0) & (k < PH - 1))
        def _():
            ahead()

        @pl.when(t > 0)
        def _():
            each(down(k, held(s, False), s, {"tile": t - 1}), "wait_recv")

        @pl.when(t < TI - 1)
        def _():
            each(up(k, held(s, True), s, {"tile": t + 1}), "wait_recv")

        chunk(s, x_ref, e_ref, consts, scratch)

        @pl.when(k == 0)
        def _():
            relays(forward)

        for n in range(1, 4):

            @pl.when(k == n - 1)
            def _():
                for j in WAVES[n]:
                    each(a2a(j), "start")

        @pl.when(k == 0)
        def _():
            ahead()

        return 0

    lax.fori_loop(0, PH, step, 0)

    place = lax.rem(t, 8)
    plane = me * 2 + t // 8

    def first(k):
        to = lax.rem(plane + k, 16)
        return pltpu.make_async_remote_copy(
            src_ref=a_ref.at[plane], dst_ref=a_ref.at[plane], send_sem=as_sem.at[k],
            recv_sem=ar_sem.at[k],
            device_id={"photo": to // 2, "tile": lax.rem(to, 2) * 8 + place},
            device_id_type=MESH,
        )

    def second(k):
        to = lax.rem(place + k, 8)
        return pltpu.make_async_remote_copy(
            src_ref=b_ref.at[place], dst_ref=b_ref.at[place], send_sem=bs_sem.at[k],
            recv_sem=br_sem.at[k],
            device_id={"tile": t // 8 * 8 + to}, device_id_type=MESH,
        )

    planes, sums = total_gram(acc_ref, consts[5])
    a_ref[plane] = sums
    for k in range(1, 16):
        first(k).start()
    join(planes, consts[4], rows_ref)
    out = [
        pltpu.make_async_copy(
            rows_ref.at[n], fp_ref.at[:, :, pl.ds(128 * n, 128)], own_sem.at[2 + n]
        )
        for n in range(4)
    ]
    each(out, "start")
    for k in range(1, 16):
        first(k).wait_recv()
    sums = a_ref[0]
    for n in range(1, 16):
        sums += a_ref[n]
    b_ref[place] = sums
    for k in range(1, 8):
        second(k).start()
    for k in range(1, 8):
        second(k).wait_recv()
    sums = b_ref[0]
    for n in range(1, 8):
        sums += b_ref[n]
    sums_ref[...] = sums

    each(out, "wait")
    relays(lambda q, j, first: each(relayed(q, j, first), "wait_send"))
    for k in range(1, PH):
        each(a2a(k), "wait_send")
        second(k).wait_send()
    for k in range(1, 16):
        first(k).wait_send()
    for k in range(PH):
        s = moved(me, k, -1)

        @pl.when(t > 0)
        def _():
            each(up(k, held(s, True), s, {"tile": t - 1}), "wait_send")

        @pl.when(t < TI - 1)
        def _():
            each(down(k, held(s, False), s, {"tile": t + 1}), "wait_send")


SCRATCH = [
    ((3, 2 * HR, OWN, 256), F32),
    ((2 * HR, OWN, 128), F32),
    ((4, 3, HR, OWN, 512), BF16),
    ((4, HR, OWN, 256), BF16),
    ((4, 3, HR, OWN, 256), F32),
    ((4, 3, HR, OWN, 256), F32),
    ((4, 2 * HR, OWN, 256), F32),
    ((8, 256, 256), BF16),
    ((8, 256, 256), F32),
]


def fused(photos, camera_id, consts):
    vm = pl.BlockSpec(memory_space=pltpu.VMEM)
    anywhere = pl.BlockSpec(memory_space=pl.ANY)
    dma = pltpu.SemaphoreType.DMA
    return pl.pallas_call(
        fused_kernel,
        out_shape=(
            jax.ShapeDtypeStruct((CAMS, 16, 512), F32),
            jax.ShapeDtypeStruct((8, 128), F32),
        ),
        in_specs=[anywhere, pl.BlockSpec(memory_space=pltpu.SMEM)] + [anywhere] * N_CONST,
        out_specs=(anywhere, vm),
        scratch_shapes=[
            pltpu.VMEM((PH, HR, OWN, LANES), BF16),
            pltpu.VMEM((PH, 3, OWN, 128), BF16),
            pltpu.VMEM((8, PH + 2, 2, OWN, 256), BF16),
            pltpu.VMEM((PH, 2 * HR, OWN, LANES), BF16),
            pltpu.VMEM((PH, 5, OWN, 128), BF16),
            pltpu.VMEM((4, CAMS, 16, 128), F32),
            pltpu.VMEM((16, 8, 128), F32),
            pltpu.VMEM((8, 8, 128), F32),
            pltpu.VMEM((2, 4, OWN, LANES), BF16),
            pltpu.VMEM((2, OWN, 128), BF16),
            pltpu.VMEM((OWN, 16, 4096), BF16),
        ]
        + [pltpu.VMEM(c.shape, c.dtype) for c in consts[:-2]]
        + [pltpu.VMEM((*c.shape[:-2], 2 * c.shape[-2], 256), c.dtype) for c in consts[-2:]]
        + [pltpu.VMEM(s, d) for s, d in SCRATCH]
        + [dma((PH,)), dma((N_CONST, 2)), dma((6,))]
        + [dma((2, PH))] * 6
        + [dma((2, 2))] * 2
        + [dma((16,))] * 2
        + [dma((8,))] * 2,
        compiler_params=pltpu.CompilerParams(
            collective_id=0, has_side_effects=True, vmem_limit_bytes=VMEM_LIMIT
        ),
        name="fused",
    )(photos, camera_id, *consts)


def last_kernel(raw_ref, sums_hbm, fp_ref, corr_hbm, held_ref, sums_ref, corr_ref, in_sem, out_sem):
    parts = 4
    rows = CAMS // parts
    into = [pltpu.make_async_copy(sums_hbm, sums_ref, in_sem.at[parts])] + [
        pltpu.make_async_copy(raw_ref.at[pl.ds(rows * n, rows)], held_ref.at[n], in_sem.at[n])
        for n in range(parts)
    ]
    back = [pltpu.make_async_copy(corr_ref, corr_hbm, out_sem.at[parts])] + [
        pltpu.make_async_copy(held_ref.at[n], fp_ref.at[pl.ds(rows * n, rows)], out_sem.at[n])
        for n in range(parts)
    ]
    for copy in into:
        copy.start()
    for n in range(1, parts + 1):
        into[n].wait()
        back[n].start()
    into[0].wait()
    corr_ref[...] = correlated(sums_ref[...])
    back[0].start()
    for copy in back:
        copy.wait()


def last(raw, sums):
    anywhere = pl.BlockSpec(memory_space=pl.ANY)
    return pl.pallas_call(
        last_kernel,
        out_shape=(
            jax.ShapeDtypeStruct((CAMS, 16, 512), F32),
            jax.ShapeDtypeStruct((CAMS, CAMS), F32),
        ),
        in_specs=[anywhere, anywhere],
        out_specs=(anywhere, anywhere),
        scratch_shapes=[
            pltpu.VMEM((4, CAMS // 4, 16, 512), F32),
            pltpu.VMEM((8, 128), F32),
            pltpu.VMEM((CAMS, CAMS), F32),
            pltpu.SemaphoreType.DMA((5,)),
            pltpu.SemaphoreType.DMA((5,)),
        ],
        name="last",
    )(raw, sums)


def on_device(photos, camera_id):
    return last(*fused(photos, camera_id, constants()))


def solution(mesh):
    return jax.shard_map(
        on_device,
        mesh=mesh,
        in_specs=(P("photo", "tile", None), P("photo")),
        out_specs=(P(None, "tile", "photo"), P()),
        check_vma=False,
    )
```
